32 devices in a mesh: gz: 4 (over y, x), gy: 2 (over core), gx: 4 (over z).
Axes of the slice: x: 2, y: 2, z: 4, core: 2. Of those that a mesh axis runs over, the one named last changes fastest.
Arguments:
- populations: float32 [19, 32, 16, 512], P(None, 'gz', 'gy', 'gx'), may hold values from 0.1 to 20, as said below
- solid: int32 [32, 16, 512], P('gz', 'gy', 'gx'), may hold values 0 or 1
- ports: int32 [2, 16, 512], P(None, 'gy', 'gx'), may hold values 0 or 1
- concentration: float32 [2, 4, 2, 64], P(None, 'gz'), may hold values from 0 to 1
- loaded: float32 [2, 4, 2, 64], P(None, 'gz'), may hold values from 0 to 2
Outputs:
- final_populations: float32 [19, 32, 16, 512], P(None, 'gz', 'gy', 'gx')
- new_concentration: float32 [2, 4, 2, 64], P(None, 'gz')
- new_loaded: float32 [2, 4, 2, 64], P(None, 'gz')
The draws below stay inside these ranges and needn't reach their ends.
Inputs may be any that keep to these rules, and one draw needn't show every extreme that they name: `populations`: every population is positive and of the size of its lattice weight times 36.
All inputs are finite; a program needn't handle non-finite values. No bound on the sum of `solid` or of `ports` on one device may be relied on, other than what follows from the above.
Results may differ from the reference program's by a relative error of at most 0.00002.
Values sent between devices are 32-bit elements; how exact they have to be, the bound alone decides.
A program may use at most 64 MiB of HBM per device.

```python
import jax
import jax.numpy as jnp

ITERS = 2
NZ = 32
NY = 16
NX = 512
NCZ = 4
NCY = 2
NCX = 64


lattice = [(0, 0, 0), (1, 0, 0), (-1, 0, 0), (0, 1, 0), (0, -1, 0), (0, 0, 1), (0, 0, -1), (1, 1, 0), (-1, -1, 0), (1, -1, 0), (-1, 1, 0), (1, 0, 1), (-1, 0, -1), (1, 0, -1), (-1, 0, 1), (0, 1, 1), (0, -1, -1), (0, 1, -1), (0, -1, 1)]


weights = [1.0 / 3.0] + [1.0 / 18.0] * 6 + [1.0 / 36.0] * 12


def draw_populations(key, part):
    keys = jax.random.split(key, 5)
    grid = (NZ, NY, NX)
    density = 36.0 * jax.random.uniform(keys[0], grid, jnp.float32, 0.9, 1.1)
    speed_z = jax.random.uniform(keys[1], grid, jnp.float32, 0.02, 0.1)
    noise = jax.random.uniform(keys[4], (19,) + grid, jnp.float32, -0.3, 0.3)
    speed_y = jax.random.uniform(keys[2], grid, jnp.float32, -0.02, 0.02)
    speed_x = jax.random.uniform(keys[3], grid, jnp.float32, -0.02, 0.02)
    square = speed_z * speed_z + speed_y * speed_y + speed_x * speed_x
    result = []
    for member in range(19):
        step_z, step_y, step_x = lattice[member]
        along = step_z * speed_z + step_y * speed_y + step_x * speed_x
        result.append(weights[member] * density * (1.0 + 3.0 * along + 4.5 * along * along - 1.5 * square))
    return jnp.stack(result) * (1.0 + noise)


def set_ends(values, rng, least, largest):
    longest = values.shape.index(max(values.shape))
    spots = []
    for shift in (0, 1):
        where = [jax.random.randint(jax.random.fold_in(rng, axis), (), 0, length) for axis, length in enumerate(values.shape)]
        where[longest] = (where[longest] + shift) % values.shape[longest]
        spots.append(tuple(where))
    return values.at[spots[0]].set(least).at[spots[1]].set(largest)


def levels(stream_key, shape, cuts, smallest, largest):
    gain, own = 1.0, jax.random.fold_in(stream_key, 6)
    for axis_at, blocks in cuts:
        draws = jnp.exp(jax.random.uniform(jax.random.fold_in(own, axis_at), (blocks,), jnp.float32, smallest / len(cuts), largest / len(cuts)))
        gain = gain * jnp.repeat(draws, shape[axis_at] // blocks).reshape([-1 if axis == axis_at else 1 for axis in range(len(shape))])
    return gain


def setup_inputs(seed: int = 0) -> dict:
    key_list = jax.random.split(jax.random.key(seed), 6)
    return {
        "populations": draw_populations(jax.random.fold_in(key_list[5], 71), 0),
        "solid": set_ends((jax.random.randint(key_list[1], (NZ, NY, NX), 0, 5) < 2).astype(jnp.int32), jax.random.fold_in(key_list[1], 1), 0, 1),
        "ports": set_ends((jax.random.randint(key_list[2], (2, NY, NX), 0, 4) < 3).astype(jnp.int32), jax.random.fold_in(key_list[2], 1), 0, 1),
        "concentration": jnp.clip(1.0 * jax.random.uniform(key_list[3], (2, NCZ, NCY, NCX), jnp.float32) ** levels(key_list[3], (2, NCZ, NCY, NCX), ((1, 4),), -0.2, 0.2), 0.0, 1.0),
        "loaded": jnp.clip(2.0 * jax.random.uniform(key_list[4], (2, NCZ, NCY, NCX), jnp.float32) ** levels(key_list[4], (2, NCZ, NCY, NCX), ((1, 4),), -0.2, 0.2), 0.0, 2.0),
    }


lattice = [(0, 0, 0), (1, 0, 0), (-1, 0, 0), (0, 1, 0), (0, -1, 0), (0, 0, 1), (0, 0, -1),
           (1, 1, 0), (-1, -1, 0), (1, -1, 0), (-1, 1, 0), (1, 0, 1), (-1, 0, -1), (1, 0, -1), (-1, 0, 1),
           (0, 1, 1), (0, -1, -1), (0, 1, -1), (0, -1, 1)]
opposite = [0, 2, 1, 4, 3, 6, 5, 8, 7, 10, 9, 12, 11, 14, 13, 16, 15, 18, 17]
weights = [1.0 / 3.0] + [1.0 / 18.0] * 6 + [1.0 / 36.0] * 12
relax_rate = 1.25
base_density = 36.0
inlet_speed = 0.05
spread_base = (0.03, 0.06)
spread_length = 0.1
uptake_rate = (0.3, 0.6)
affinity = (2.0, 0.5)
phase_ratio = 0.5
feed_level = (1.0, 0.5)


def equilibrium(density, velocity):
    speed_z, speed_y, speed_x = velocity
    square = speed_z * speed_z + speed_y * speed_y + speed_x * speed_x
    result = []
    for member in range(19):
        step_z, step_y, step_x = lattice[member]
        along = step_z * speed_z + step_y * speed_y + step_x * speed_x
        result.append(weights[member] * density * (1.0 + 3.0 * along + 4.5 * along * along - 1.5 * square))
    return result


def moments(pops):
    density = pops[0]
    for member in range(1, 19):
        density = density + pops[member]
    flows = []
    for position in range(3):
        total = jnp.zeros_like(pops[0])
        for member in range(19):
            heading = lattice[member][position]
            if heading == 1:
                total = total + pops[member]
            elif heading == -1:
                total = total - pops[member]
        flows.append(total)
    return density, flows


def collide(pops, solid_flag):
    density, flows = moments(pops)
    velocity = [flow / density for flow in flows]
    balance = equilibrium(density, velocity)
    post = [jnp.where(solid_flag, pops[opposite[member]],
                      pops[member] - relax_rate * (pops[member] - balance[member])) for member in range(19)]
    return post, velocity


def close_ends(moved, post, velocity, ports, first_dev, last_dev):
    inflow = equilibrium(base_density, (inlet_speed, 0.0, 0.0))
    outflow = equilibrium(base_density, (velocity[0][-1], velocity[1][-1], velocity[2][-1]))
    inlet_open = ports[0] == 1
    outlet_open = ports[1] == 1
    result = list(moved)
    for member in range(19):
        step_z = lattice[member][0]
        back = post[opposite[member]]
        if step_z == 1:
            entering = jnp.where(inlet_open, inflow[member], back[0])
            result[member] = result[member].at[0].set(jnp.where(first_dev, entering, result[member][0]))
        elif step_z == -1:
            entering = jnp.where(outlet_open, outflow[member], back[-1])
            result[member] = result[member].at[-1].set(jnp.where(last_dev, entering, result[member][-1]))
    return result


def block_sum(field):
    depth, height, width = field.shape
    return field.reshape(depth // 8, 8, height // 8, 8, width // 8, 8).sum(axis=(1, 3, 5))


def cell_velocity(pops, solid):
    density, flows = moments(pops)
    fluid = (solid == 0).astype(pops[0].dtype)
    return jnp.stack([block_sum(flow * fluid) for flow in flows]) / (512.0 * base_density)


def transport(padded, loaded, coarse_vel):
    centre = padded[:, 1:-1]
    neighbours = [(padded[:, :-2], padded[:, 2:]),
                  (jnp.roll(centre, 1, axis=2), jnp.roll(centre, -1, axis=2)),
                  (jnp.roll(centre, 1, axis=3), jnp.roll(centre, -1, axis=3))]
    change = jnp.zeros_like(centre)
    curvature = jnp.zeros_like(centre)
    reach = jnp.zeros_like(coarse_vel[0])
    for direction in range(3):
        courant = 8.0 * coarse_vel[direction]
        before, after = neighbours[direction]
        change = change - jnp.maximum(courant, 0.0) * (centre - before) - jnp.minimum(courant, 0.0) * (after - centre)
        curvature = curvature + after - 2.0 * centre + before
        reach = reach + jnp.abs(courant)
    base = jnp.array(spread_base, dtype=centre.dtype)[:, None, None, None]
    speed = jnp.array(uptake_rate, dtype=centre.dtype)[:, None, None, None]
    holding = jnp.array(affinity, dtype=centre.dtype)[:, None, None, None]
    rate = speed * (holding * centre - loaded)
    new_conc = centre + change + (base + spread_length * reach) * curvature - phase_ratio * rate
    return new_conc, loaded + rate


def reference(populations, solid, ports, concentration, loaded):
    pops = [populations[member] for member in range(19)]
    solid_flag = solid == 1
    for iteration in range(ITERS):
        post, velocity = collide(pops, solid_flag)
        moved = []
        for member in range(19):
            step_z, step_y, step_x = lattice[member]
            moved.append(jnp.roll(post[member], (step_z, step_y, step_x), axis=(0, 1, 2)))
        pops = close_ends(moved, post, velocity, ports, True, True)
    final = jnp.stack(pops)
    coarse_vel = cell_velocity(pops, solid)
    feed = jnp.broadcast_to(jnp.array(feed_level, dtype=concentration.dtype)[:, None, None],
                            (2, concentration.shape[2], concentration.shape[3]))
    padded = jnp.concatenate([feed[:, None], concentration, concentration[:, -1:]], axis=1)
    new_conc, new_load = transport(padded, loaded, coarse_vel)
    return (final, new_conc, new_load)
```

```python
import functools

import jax
import jax.numpy as jnp
from jax import lax
from jax.experimental import pallas as pl
from jax.experimental.pallas import tpu as pltpu
from jax.sharding import PartitionSpec as P

ITERS = 2
CELL = 8
MESH = pl.DeviceIdType.MESH

lattice = [
    (0, 0, 0),
    (1, 0, 0),
    (-1, 0, 0),
    (0, 1, 0),
    (0, -1, 0),
    (0, 0, 1),
    (0, 0, -1),
    (1, 1, 0),
    (-1, -1, 0),
    (1, -1, 0),
    (-1, 1, 0),
    (1, 0, 1),
    (-1, 0, -1),
    (1, 0, -1),
    (-1, 0, 1),
    (0, 1, 1),
    (0, -1, -1),
    (0, 1, -1),
    (0, -1, 1),
]
opposite = [0, 2, 1, 4, 3, 6, 5, 8, 7, 10, 9, 12, 11, 14, 13, 16, 15, 18, 17]
weights = [1.0 / 3.0] + [1.0 / 18.0] * 6 + [1.0 / 36.0] * 12
relax_rate = 1.25
base_density = 36.0
inlet_speed = 0.05
spread_base = (0.03, 0.06)
spread_length = 0.1
uptake_rate = (0.3, 0.6)
affinity = (2.0, 0.5)
phase_ratio = 0.5
feed_level = (1.0, 0.5)

GROUPS = [[[m for m in range(19) if lattice[m][d] == s] for s in (1, -1)] for d in range(3)]
FLAT = [m for m in range(19) if lattice[m][2] == 0]
SOLID = 14
ORDER = GROUPS[0][0] + [m for m in range(19) if lattice[m][0] == 0] + [None] + GROUPS[0][1]
SLOT = {m: i for i, m in enumerate(ORDER) if m is not None}
TYPES = [(cy, cx) for cy in (1, 0, -1) for cx in (1, 0, -1)]


def moments(f):
    density = f[0]
    for member in range(1, 19):
        density = density + f[member]
    return density, momentum(f)


def momentum(f):
    flows = []
    for d in range(3):
        total = None
        for a, b in zip(GROUPS[d][0], [opposite[m] for m in GROUPS[d][0]]):
            part = f[a] - f[b]
            total = part if total is None else total + part
        flows.append(total)
    return flows


def balance(scale, velocity, members):
    square = velocity[0] * velocity[0] + velocity[1] * velocity[1] + velocity[2] * velocity[2]
    base = 1.0 - 1.5 * square
    cache, result = {}, {}
    for w in set(weights[m] for m in members):
        cache[w] = scale * w
    for m in members:
        if m == 0:
            result[m] = cache[weights[0]] * base
            continue
        key = min(m, opposite[m])
        if ("pair", key) not in cache:
            along = None
            for d in range(3):
                step = lattice[key][d]
                if step:
                    term = velocity[d]
                    if along is None:
                        along = term if step == 1 else -term
                    else:
                        along = along + term if step == 1 else along - term
            cache[("pair", key)] = (base + 4.5 * along * along, 3.0 * along)
        even, odd = cache[("pair", key)]
        result[m] = cache[weights[m]] * (even + odd if m == key else even - odd)
    return result


def collide(f, solid):
    density, flows = moments(f)
    inverse = 1.0 / density
    velocity = [flow * inverse for flow in flows]
    feq = balance(relax_rate * density, velocity, range(19))
    post = [
        jnp.where(solid, f[opposite[m]], (1.0 - relax_rate) * f[m] + feq[m]) for m in range(19)
    ]
    return post, velocity


def edge_rows(side, ends):
    far, near = ends
    across = [m for m in GROUPS[0][side[0]] if lattice[m][1] == 1 - 2 * side[1]]
    along = [m for m in GROUPS[1][side[1]] if lattice[m][0] == 0]
    return [(across[0], far, 0), (across[0], near, 1)] + [(m, near, 0) for m in along]


def kernel(sizes, *refs):
    nz, ny, nx = sizes
    (pop_hbm, solid_hbm, ports_hbm, conc_hbm, load_hbm, out, new_conc, new_load,
     pops, solid, ports, conc, load, post0, post1, bound, speed, xpack, xrecv, xside, xline, ypack, yrecv,
     ypack1, yrecv1, cpack, crecv, cpack1, crecv1, epack, erecv, erecv_far, xpack1, xrecv1, yline, yline1, sline,
     frame, pore, near, wrapped, sent_v, all_v, vel, load_sem, send_sem, recv_sem, near_sem, vsend, vrecv) = refs
    D, H, W = solid.shape
    T = D + 2
    ncy, ncx = conc.shape[2:]
    f32 = jnp.float32
    gz, gy, gx = lax.axis_index("gz"), lax.axis_index("gy"), lax.axis_index("gx")
    is_first, is_last = gz == 0, gz == nz - 1
    has_up, has_down = gz < nz - 1, gz > 0
    bound_at = len(FLAT) * T
    port_at = bound_at + 5
    solid_at = port_at + 2 + (port_at % 2)
    bound_at1 = len(FLAT) * D

    small = [
        pltpu.make_async_copy(a, b, load_sem.at[D + i])
        for i, (a, b) in enumerate(
            ((solid_hbm, solid), (ports_hbm, ports), (conc_hbm, conc), (load_hbm, load)))
    ]

    def plane_in(z):
        return pltpu.make_async_copy(pop_hbm.at[:, z], pops.at[:, z], load_sem.at[z])

    ends_z = [D - 1, D - 2, 0, 1]
    plane_in(ends_z[0]).start()
    small[0].start()
    small[1].start()
    for z in ends_z[1:]:
        plane_in(z).start()
    for z in range(2, D - 2):
        plane_in(z).start()
    for copy in small[2:]:
        copy.start()

    def at(offset):
        dz, dy, dx = offset
        return {"gz": gz + dz, "gy": lax.rem(gy + dy + ny, ny), "gx": lax.rem(gx + dx + nx, nx)}

    flat = [(0, dy, dx) for dy in range(ny) for dx in range(nx) if dy or dx]
    targets = sorted({(dy % ny, dx) for dy in (0, 1, -1) for dx in (0, 1)})
    barrier = pltpu.get_barrier_semaphore()

    def greet(offsets):
        for offset in offsets:
            pl.semaphore_signal(barrier, inc=1, device_id=at(offset), device_id_type=MESH)

    @pl.when(has_up)
    def _():
        greet([(1, -dy, -dx) for dy, dx in targets])

    @pl.when(has_down)
    def _():
        greet([(-1, -dy, -dx) for dy, dx in targets])

    greet(flat)

    lane = lax.broadcasted_iota(jnp.int32, (H, W), 1)
    row = lax.broadcasted_iota(jnp.int32, (H, W), 0)
    pair = lax.div(lane, 2)
    first_mask = jnp.full((H, W), gz, jnp.int32) == 0
    last_mask = jnp.full((H, W), gz, jnp.int32) == nz - 1
    zero = jnp.zeros((H, W), f32)

    def rolled(x, step, axis):
        size = x.shape[axis]
        if isinstance(step, int):
            step = step % size
            return pltpu.roll(x, step, axis) if step else x
        return pltpu.roll(x, step, axis)

    def put(acc, value, spot, shift):
        return jnp.where(lane == spot, rolled(value, shift, 1), acc)

    def put_pair(acc, value, half, shift):
        return jnp.where(pair == half, rolled(value, shift, 1), acc)

    def wrapped_up(spot):
        return spot % W if isinstance(spot, int) else jnp.where(spot >= W, spot - W, spot)

    side_sets = [(pl.ds(0, 2), 1)] if ny == 2 else [(pl.ds(0, 1), 1), (pl.ds(1, 1), -1)]
    counter = [0]

    def remote(src, dst, offset):
        i = counter[0]
        counter[0] += 1
        return pltpu.make_async_remote_copy(
            src_ref=src, dst_ref=dst, send_sem=send_sem.at[i], recv_sem=recv_sem.at[i],
            device_id=at(offset), device_id_type=MESH)

    def run(copies, method, incoming=False):
        conds = {1: has_down, -1: has_up} if incoming else {1: has_up, -1: has_down}
        for copy in copies.get(0, ()):
            getattr(copy, method)()
        for dz in (1, -1):
            if copies.get(dz):
                @pl.when(conds[dz])
                def _():
                    for copy in copies[dz]:
                        getattr(copy, method)()

    layers, edges, flanks = {1: [], -1: []}, {1: [], -1: []}, {1: [], -1: []}
    layers[1].append(remote(post0.at[D + 1, pl.ds(0, 15)], post0.at[1, pl.ds(0, 15)], (1, 0, 0)))
    layers[1].append(remote(post0.at[D, pl.ds(0, 5)], post0.at[0, pl.ds(0, 5)], (1, 0, 0)))
    layers[-1].append(remote(post0.at[2, pl.ds(5, 15)], post0.at[D + 2, pl.ds(5, 15)], (-1, 0, 0)))
    layers[-1].append(remote(post0.at[3, pl.ds(15, 5)], post0.at[D + 3, pl.ds(15, 5)], (-1, 0, 0)))
    for dz in (1, -1):
        zs = 0 if dz == 1 else 1
        for where, dy in side_sets:
            edges[dz].append(remote(epack.at[zs, where], erecv_far.at[zs, where], (dz, dy, 1)))
            edges[dz].append(remote(epack.at[zs, where], erecv.at[zs, where], (dz, dy, 0)))
        flanks[dz].append(remote(xpack, xside.at[zs], (dz, 0, 1)))
    slab_x = [remote(xpack, xrecv, (0, 0, 1))]
    slab_c = [remote(cpack.at[where], crecv.at[where], (0, dy, 1)) for where, dy in side_sets]
    slab_y = [remote(ypack.at[where], yrecv.at[where], (0, dy, 0)) for where, dy in side_sets]
    back_x = [remote(xpack1, xrecv1, (0, 0, -1))]
    back_c = [remote(cpack1.at[where], crecv1.at[where], (0, dy, -1)) for where, dy in side_sets]
    back_y = [remote(ypack1.at[where], yrecv1.at[where], (0, dy, 0)) for where, dy in side_sets]
    ends = {1: [], -1: []}
    for s in range(2):
        dz = 1 - 2 * s
        ends[dz].append(
            pltpu.make_async_remote_copy(
                src_ref=conc, dst_ref=near.at[s], send_sem=near_sem.at[0, s],
                recv_sem=near_sem.at[1, s], device_id=at((dz, 0, 0)), device_id_type=MESH))

    edge_table = [
        [edge_rows((zs, s), ((D - 2, D - 1), (1, 0))[zs]) for s in range(2)] for zs in range(2)]

    def first_plane(z, packs):
        plane_in(z).wait()
        f = [pops[m, z] for m in range(19)]
        flag = solid[z]
        post, velocity = collide(f, flag == 1)
        wall = flag.astype(f32)
        for m in range(19):
            post0[z + 2, SLOT[m]] = post[m]
        post0[z + 2, SOLID] = wall
        for s in range(2):
            for i, m in enumerate(GROUPS[1][s]):
                ypack[s, i, pl.ds(z, 1), :] = post[m][H - 1 :, :] if s == 0 else post[m][:1, :]
            ypack[s, 5, pl.ds(z, 1), :] = wall[H - 1 :, :] if s == 0 else wall[:1, :]
        if isinstance(z, int):
            for zs in range(2):
                for s in range(2):
                    for r, (m, source, _) in enumerate(edge_table[zs][s]):
                        if source == z:
                            epack[zs, s, r : r + 1, :] = post[m][H - 1 :, :] if s == 0 else post[m][:1, :]
            if z == D - 1:
                outflow = balance(base_density, velocity, GROUPS[0][1])
                for j, m in enumerate(GROUPS[0][1]):
                    bound[0, j] = jnp.where(ports[1] == 1, outflow[m], post[opposite[m]])
            if z == 0:
                inflow = equilibrium_at_inlet()
                for j, m in enumerate(GROUPS[0][0]):
                    entering = jnp.where(ports[0] == 1, inflow[m], post[opposite[m]])
                    bound[0, j] = jnp.where(first_mask, entering, bound[0, j])
        twos, ones = packs
        for i, m in enumerate(GROUPS[2][0]):
            q = i * T + z + lattice[m][0] + 1
            twos = put_pair(twos, post[m], q, wrapped_up(2 * q + 2))
        for i, m in enumerate(FLAT):
            q = i * T + z + lattice[m][0] + 1
            ones = put(ones, post[m], q, q + 1)
        q = solid_at // 2 + z + 1
        ones = put_pair(ones, wall, q, wrapped_up(2 * q + 2))
        return twos, ones

    small[0].wait()
    small[1].wait()
    packs = (zero, zero)
    for z in ends_z:
        packs = first_plane(z, packs)

    count = lambda flag: jnp.where(flag, len(targets), 0)
    pl.semaphore_wait(barrier, len(flat) + count(has_up) + count(has_down))
    run(edges, "start")
    run(layers, "start")

    packs = lax.fori_loop(2, D - 2, first_plane, packs)
    twos, ones = packs
    for j in range(5):
        ones = put(ones, bound[0, j], bound_at + j, bound_at + j + 1)
    for j in range(2):
        ones = put(ones, ports[j].astype(f32), port_at + j, port_at + j + 1)
    xpack[0], xpack[1] = twos, ones
    run(flanks, "start")
    run({0: slab_x}, "start")
    for s in range(2):
        acc = zero
        for i in range(6):
            acc = put_pair(acc, ypack[s, i], i, 2 * i + 2)
        cpack[s] = acc
    run({0: slab_c + slab_y}, "start")
    small[2].wait()
    small[3].wait()
    run(ends, "start")

    g_low, g_high = lane < 0, lane < 0
    h_low, h_high = lane < 0, lane < 0
    for members, is_pair in ((GROUPS[2][0], True), (FLAT, False)):
        spot = pair if is_pair else lane
        low, high = lane < 0, lane < 0
        for i, m in enumerate(members):
            cz = lattice[m][0]
            if cz >= 0:
                low = low | ((spot >= i * T) & (spot < i * T + 1 + cz))
            if cz <= 0:
                high = high | ((spot >= i * T + D + 1 + cz) & (spot < i * T + T))
        if is_pair:
            g_low, g_high = low, high
        else:
            h_low, h_high = low, high
    s_low, s_high = pair == solid_at // 2, pair == solid_at // 2 + D + 1

    diffs = []
    wide = sent_v.shape[-1]
    parts = []
    for c in (1, 0, -1):
        voxel = lax.broadcasted_iota(jnp.int32, (W, wide), 0) + gx * W - 1 + c
        voxel = jnp.where(voxel < 0, voxel + nx * W, voxel)
        cell = lax.broadcasted_iota(jnp.int32, (W, wide), 1) * CELL
        parts.append(((voxel >= cell) & (voxel < cell + CELL)).astype(f32))
    pick = jnp.concatenate(parts, axis=0).astype(jnp.bfloat16)

    run({0: slab_y + slab_c}, "wait_recv")

    def filled(tile, columns, lanes, spot):
        if lanes == 0:
            return tile
        if lanes == 1:
            return jnp.where(lane < 1, rolled(columns, -(spot + 1), 1), rolled(tile, 1, 1))
        return jnp.where(lane < 2, rolled(columns, -spot, 1), rolled(tile, 2, 1))

    for s in range(2):
        corner = crecv[s]
        for i, m in enumerate(GROUPS[1][s]):
            cz, _, cx = lattice[m]
            yline[s, i, 1 + cz : 1 + cz + D, :] = filled(yrecv[s, i], corner, 1 + cx, 2 * i)
        for n in range(3):
            sline[s, n] = filled(yrecv[s, 5], corner, n, 10)

    run({0: slab_x}, "wait_recv")
    xline[0], xline[1] = xrecv[0], xrecv[1]

    def set_frame(k):
        columns = xline[1]
        walls = post0[k + 1, SOLID]
        spot = solid_at + 2 * k
        one = jnp.where(lane < 1, rolled(columns, W - 1 - spot, 1), rolled(walls, 1, 1))
        frame[k] = one
        return walls, one, jnp.where(lane < 2, rolled(columns, W - spot, 1), rolled(walls, 2, 1))

    def set_pore(k, carry):
        views = set_frame(k)
        for n, view in enumerate(views):
            cx = 1 - n
            pore[k, TYPES.index((0, cx))] = 1.0 - view
            for cy in (1, -1):
                s = 1 if cy == 1 else 0
                line = sline[s, n, pl.ds(k - 1, 1), :]
                moved = jnp.where(row == (H - 1 if cy == 1 else 0),
                                  jnp.broadcast_to(line, (H, W)), rolled(view, -cy, 0))
                pore[k, TYPES.index((cy, cx))] = 1.0 - moved
        return carry

    for n in range(9):
        pore[0, n] = zero
        pore[D + 1, n] = zero
    lax.fori_loop(1, D + 1, set_pore, 0)

    def stream(k, place):
        pairs_in, singles_in = xline[0], xline[1]
        f = []
        for m in range(19):
            cz, cy, cx = lattice[m]
            v = post0[k + 1 - cz, SLOT[m]]
            if cx == 1:
                spot = 2 * (GROUPS[2][0].index(m) * T + k)
                column = rolled(pairs_in, W - spot, 1)
                v = jnp.where(lane < 2, column, rolled(v, 2, 1))
            elif cx == 0:
                spot = FLAT.index(m) * T + k
                column = rolled(singles_in, W - spot, 1)
                v = jnp.where(lane < 1, column, rolled(v, 1, 1))
            if cy:
                s = 0 if cy == 1 else 1
                line = yline[s, GROUPS[1][s].index(m), pl.ds(k, 1), :]
                v = jnp.where(row == (0 if s == 0 else H - 1),
                              jnp.broadcast_to(line, (H, W)), rolled(v, cy, 0))
            f.append(v)
        return f

    def port_view(j):
        column = rolled(xline[1], W - port_at - j, 1)
        return jnp.where(lane < 1, column, rolled(ports[j].astype(f32), 1, 1)) > 0.5

    def bound_view(j):
        column = rolled(xline[1], W - bound_at - j, 1)
        return jnp.where(lane < 1, column, rolled(bound[0, j], 1, 1))

    def contribute(k, place, post, sums):
        sums = dict(zip(names, sums))
        for m in range(1, 19):
            cz, cy, cx = lattice[m]
            if (place == "low" and cz != 1) or (place == "high" and cz != -1):
                continue
            part = post[m] * pore[k + cz, TYPES.index((cy, cx))]
            if cy or cx:
                sums["n", cy, cx] = sums["n", cy, cx] + part
            if cz == 1:
                sums["z", cy, cx] = sums["z", cy, cx] + part
            if cz == -1:
                sums["z", cy, cx] = sums["z", cy, cx] - part
        return tuple(sums[name] for name in names)

    names = [("n", cy, cx) for cy, cx in TYPES if cy or cx]
    names += [("z", cy, cx) for cy, cx in TYPES if not (cy and cx)]

    def second_plane(k, place, carry):
        f = stream(k, place)
        if place == "first":
            for j, m in enumerate(GROUPS[0][0]):
                f[m] = jnp.where(first_mask, bound_view(j), f[m])
        if place == "last":
            for j, m in enumerate(GROUPS[0][1]):
                f[m] = jnp.where(last_mask, bound_view(j), f[m])
        post, velocity = collide(f, frame[k] > 0.5)
        if place == "low":
            post = [jnp.where(first_mask, 0.0, p) if lattice[m][0] == 1 else p for m, p in enumerate(post)]
        if place == "high":
            post = [jnp.where(last_mask, 0.0, p) if lattice[m][0] == -1 else p for m, p in enumerate(post)]
        twos, ones, sums = carry[0], carry[1], carry[2:]
        for m in range(19):
            cz, cy, cx = lattice[m]
            if (place == "low" and cz != 1) or (place == "high" and cz != -1):
                continue
            post1[k, m] = post[m]
            if (place == "first" and cz == -1) or (place == "last" and cz == 1):
                continue
            t = k - 1 + cz
            if cy:
                s = 0 if cy == 1 else 1
                ypack1[s, GROUPS[1][s].index(m), pl.ds(t, 1), :] = post[m][H - 1 :, :] if s == 0 else post[m][:1, :]
            if cx == -1:
                q = GROUPS[2][1].index(m) * D + t
                twos = put_pair(twos, post[m], q, 2 * q)
            elif cx == 0:
                q = FLAT.index(m) * D + t
                ones = put(ones, post[m], q, q)
        sums = contribute(k, place, post, sums)
        if place in ("first", "last"):
            if place == "first":
                members = GROUPS[0][0]
                values = equilibrium_at_inlet()
                opened, mask = port_view(0), first_mask
            else:
                members = GROUPS[0][1]
                values = balance(base_density, velocity, members)
                opened, mask = port_view(1), last_mask
            sums = list(sums)
            still = pore[k, TYPES.index((0, 0))]
            extra = [zero, zero, zero]
            for j, m in enumerate(members):
                value = jnp.where(opened, values[m], post[opposite[m]])
                bound[1, j] = value if place == "first" else jnp.where(last_mask, value, bound[1, j])
                for d in range(3):
                    if lattice[m][d]:
                        extra[d] = extra[d] + value if lattice[m][d] == 1 else extra[d] - value
            for d in range(3):
                add = jnp.where(mask, extra[d] * still, 0.0)
                speed[d] = add if place == "first" else speed[d] + add
        return (twos, ones) + tuple(sums)

    carry = (zero,) * (2 + len(names))
    carry = lax.fori_loop(2, D, lambda k, c: second_plane(k, "mid", c), carry)

    run(edges, "wait_recv", incoming=True)
    run(flanks, "wait_recv", incoming=True)
    below, above = xside[0], xside[1]
    xline[0] = jnp.where(g_low, rolled(below[0], -2 * D, 1),
                         jnp.where(g_high, rolled(above[0], 2 * D, 1), xline[0]))
    low = jnp.where(s_low, rolled(below[1], -2 * D, 1), rolled(below[1], -D, 1))
    high = jnp.where(s_high, rolled(above[1], 2 * D, 1), rolled(above[1], D, 1))
    xline[1] = jnp.where(h_low | s_low, low, jnp.where(h_high | s_high, high, xline[1]))
    for zs in range(2):
        for s in range(2):
            tile, far = erecv[zs, s], erecv_far[zs, s]
            views = [tile] + [
                jnp.where(lane < n, rolled(far, n, 1), rolled(tile, n, 1)) for n in (1, 2)]
            for r, (m, _, target) in enumerate(edge_table[zs][s]):
                k = target if zs == 0 else D + 1 - target
                yline[s, GROUPS[1][s].index(m), k : k + 1, :] = views[1 + lattice[m][2]][r : r + 1, :]
    run(layers, "wait_recv", incoming=True)
    set_frame(0)
    set_frame(D + 1)
    carry = second_plane(0, "low", carry)
    carry = second_plane(1, "first", carry)
    carry = second_plane(D, "last", carry)
    carry = second_plane(D + 1, "high", carry)

    twos, ones, sums = carry[0], carry[1], dict(zip(names, carry[2:]))
    for j in range(5):
        ones = put(ones, bound[1, j], bound_at1 + j, bound_at1 + j)
    xpack1[0], xpack1[1] = twos, ones
    run({0: back_x + back_y}, "start")

    top, bottom = row == H - 1, row == 0
    blocks = []
    for cx in (1, 0, -1):
        own = [zero, zero, zero]
        up, down = [zero] * 3, [zero] * 3
        if ("n", 0, cx) in sums and cx:
            own[2] = sums["n", 0, cx] if cx == 1 else -sums["n", 0, cx]
        own[0] = sums["z", 0, cx]
        for cy, beyond, edge in ((1, up, top), (-1, down, bottom)):
            n = sums["n", cy, cx]
            values = [sums.get(("z", cy, cx)), n if cy == 1 else -n, {1: n, 0: None, -1: -n}[cx]]
            for d in range(3):
                if values[d] is not None:
                    own[d] = own[d] + jnp.where(edge, 0.0, values[d])
                    beyond[d] = values[d]
        if cx == 0:
            own = [own[d] + speed[d] for d in range(3)]
        totals = [jnp.sum(v, axis=0, keepdims=True) for v in own]
        ups = [v[H - 1 :, :] for v in up]
        downs = [v[:1, :] for v in down]
        if ny == 2:
            lines = totals + [a + b for a, b in zip(ups, downs)]
        else:
            lines = totals + ups + downs
        blocks.append(lines)
    tiles = []
    for base in range(0, sent_v.shape[0], H):
        here = []
        for lines in blocks:
            tile = zero
            for r, line in enumerate(lines[base : base + H]):
                tile = jnp.where(row == r, jnp.broadcast_to(line, (H, W)), tile)
            here.append(tile)
        tiles.append(jnp.concatenate(here, axis=1))

    def exact_pick(x):
        high = x.astype(jnp.bfloat16).astype(f32)
        mid = (x - high).astype(jnp.bfloat16).astype(f32)
        low = x - high - mid
        stacked = jnp.concatenate([high, mid, low], axis=0).astype(jnp.bfloat16)
        made = jnp.dot(stacked, pick, preferred_element_type=f32)
        return made[:H] + made[H : 2 * H] + made[2 * H :]

    for i, tile in enumerate(tiles):
        sent_v[i * H : (i + 1) * H, :] = exact_pick(tile) * (1.0 / (CELL * CELL * CELL * base_density))
    tell = [
        pltpu.make_async_remote_copy(
            src_ref=sent_v, dst_ref=all_v.at[gy, gx], send_sem=vsend.at[i],
            recv_sem=vrecv.at[i], device_id=at(offset), device_id_type=MESH)
        for i, offset in enumerate(flat)
    ]
    for copy in tell:
        copy.start()
    all_v[gy, gx] = sent_v[...]
    for s in range(2):
        acc = zero
        for i, m in enumerate(GROUPS[1][s]):
            if lattice[m][2] <= 0:
                acc = put_pair(acc, ypack1[s, i], i, 2 * i)
        cpack1[s] = acc
    run({0: back_c}, "start")

    @pl.when(is_first)
    def _():
        for s in range(2):
            near[0, s] = jnp.full(near.shape[2:], feed_level[s], f32)

    @pl.when(is_last)
    def _():
        near[1] = conc[...]

    run(ends, "wait_recv", incoming=True)
    source = lax.broadcasted_iota(jnp.int32, (ncx, ncx), 0)
    target = lax.broadcasted_iota(jnp.int32, (ncx, ncx), 1)
    ahead = jnp.where(target == ncx - 1, 0, target + 1)
    behind = jnp.where(target == 0, ncx - 1, target - 1)
    take_after = (source == ahead).astype(f32)
    take_before = (source == behind).astype(f32)

    def exact_dot(a, b):
        return jnp.dot(a, b, precision=lax.Precision.HIGHEST, preferred_element_type=f32)

    for s in range(2):
        c = conc[s, 0]
        wrapped[s, 1 : ncy + 1, :] = c
        wrapped[s, 0:1, :] = conc[s, 0, ncy - 1 : ncy, :]
        wrapped[s, ncy + 1 : ncy + 2, :] = conc[s, 0, 0:1, :]
        pairs = [
            (near[0, s, 0], near[1, s, 0]),
            (wrapped[s, 0:ncy, :], wrapped[s, 2 : ncy + 2, :]),
            (exact_dot(c, take_before), exact_dot(c, take_after)),
        ]
        curvature = sum(b + a - 2.0 * c for b, a in pairs)
        rate = uptake_rate[s] * (affinity[s] * c - load[s, 0])
        new_load[s, 0] = load[s, 0] + rate
        diffs.append((c - phase_ratio * rate + spread_base[s] * curvature, curvature,
                      [(c - b, a - c) for b, a in pairs]))

    run({0: back_y + back_x + back_c}, "wait_recv")

    def emptied(tile, columns, lanes, spot):
        if lanes == 0:
            return tile
        if lanes == 1:
            return jnp.where(lane >= W - 1, rolled(columns, W - 1 - spot, 1), rolled(tile, -1, 1))
        return jnp.where(lane >= W - 2, rolled(columns, W - 2 - spot, 1), rolled(tile, -2, 1))

    for s in range(2):
        corner = crecv1[s]
        for i, m in enumerate(GROUPS[1][s]):
            yline1[s, i] = emptied(yrecv1[s, i], corner, 1 - lattice[m][2], 2 * i)

    def last_plane(t, place):
        pairs_in, singles_in = xrecv1[0], xrecv1[1]
        for m in range(19):
            cz, cy, cx = lattice[m]
            side = {"first": 1, "last": -1}.get(place)
            v = post1[t + 1 - cz, m]
            if cx == -1:
                spot = 2 * (GROUPS[2][1].index(m) * D + t)
                column = rolled(pairs_in, wrapped_up(2 * W - 2 - spot), 1)
                v = jnp.where(lane >= W - 2, column, rolled(v, -2, 1))
            elif cx == 0:
                spot = FLAT.index(m) * D + t
                column = rolled(singles_in, W - 1 - spot, 1)
                v = jnp.where(lane >= W - 1, column, rolled(v, -1, 1))
            if cy:
                s = 0 if cy == 1 else 1
                line = yline1[s, GROUPS[1][s].index(m), pl.ds(t, 1), :]
                v = jnp.where(row == (0 if s == 0 else H - 1),
                              jnp.broadcast_to(line, (H, W)), rolled(v, cy, 0))
            if cz == side:
                j = GROUPS[0][0 if cz == 1 else 1].index(m)
                column = rolled(singles_in, W - 1 - bound_at1 - j, 1)
                kept = jnp.where(lane >= W - 1, column, rolled(bound[1, j], -1, 1))
                v = jnp.where(first_mask if cz == 1 else last_mask, kept, v)
            out[m, t] = v

    def mid_plane(t, c):
        last_plane(t, "mid")
        return c

    last_plane(0, "first")
    lax.fori_loop(1, D - 1, mid_plane, 0)
    last_plane(D - 1, "last")

    run(edges, "wait_send")
    run(layers, "wait_send")
    run(flanks, "wait_send")
    run({0: slab_x + slab_c + slab_y + back_x + back_c + back_y}, "wait_send")
    run(ends, "wait_send")
    for copy in tell:
        copy.wait_recv()

    totals = []
    for y in range(ny):
        total = all_v[y, 0]
        for x in range(1, nx):
            total = total + all_v[y, x]
        totals.append(total)
    for y in range(ny):
        for d in range(3):
            own = totals[y][d : d + 1]
            if ny == 2:
                own = own + totals[1 - y][3 + d : 4 + d]
            else:
                own = own + totals[(y - 1) % ny][3 + d : 4 + d] + totals[(y + 1) % ny][6 + d : 7 + d]
            vel[d, y : y + 1, :] = own
    courant = [CELL * vel[d][:, :ncx] for d in range(3)]
    reach = jnp.abs(courant[0]) + jnp.abs(courant[1]) + jnp.abs(courant[2])
    for s in range(2):
        value, curvature, steps = diffs[s]
        for d in range(3):
            low, high = steps[d]
            value = value - jnp.maximum(courant[d], 0.0) * low - jnp.minimum(courant[d], 0.0) * high
        new_conc[s, 0] = value + spread_length * reach * curvature
    for copy in tell:
        copy.wait_send()


def hand_out(*refs):
    copies = [pltpu.make_async_copy(refs[i], refs[3 + i], refs[6].at[i]) for i in range(3)]
    for copy in copies:
        copy.start()
    for copy in copies:
        copy.wait()


def equilibrium_at_inlet():
    result = {}
    for m in GROUPS[0][0]:
        along = inlet_speed
        result[m] = weights[m] * base_density * (
            1.0 + 3.0 * along + 4.5 * along * along - 1.5 * inlet_speed * inlet_speed)
    return result


def solution(mesh):
    sizes = tuple(mesh.shape[a] for a in ("gz", "gy", "gx"))
    nz, ny, nx = sizes

    def body(populations, solid, ports, concentration, loaded):
        D, H, W = solid.shape
        ncy, ncx = concentration.shape[2:]
        assert D == CELL and H == CELL and W % 128 == 0 and 12 * (D + 2) <= W
        assert nz > 1 and ny > 1 and nx > 1
        wide = -(-ncx // 128) * 128
        f32 = jnp.float32
        tile = (H, W)
        rows = H if ny == 2 else 2 * H
        sides = 1 if ny == 2 else 2
        moves = 4 + 2 * (2 * sides + 1) + 2 * (1 + 2 * sides)
        anywhere = pl.BlockSpec(memory_space=pl.ANY)
        inside = pl.BlockSpec(memory_space=pltpu.VMEM)
        results = (populations, concentration, loaded)
        made = pl.pallas_call(
            functools.partial(kernel, sizes),
            out_shape=tuple(pltpu.VMEM(a.shape, f32) for a in results),
            in_specs=[anywhere] * 5,
            out_specs=(inside,) * 3,
            scratch_shapes=[
                pltpu.VMEM(populations.shape, f32),
                pltpu.VMEM(solid.shape, jnp.int32),
                pltpu.VMEM(ports.shape, jnp.int32),
                pltpu.VMEM(concentration.shape, f32),
                pltpu.VMEM(loaded.shape, f32),
                pltpu.VMEM((D + 4, 20) + tile, f32),
                pltpu.VMEM((D + 2, 19) + tile, f32),
                pltpu.VMEM((2, 5) + tile, f32),
                pltpu.VMEM((3,) + tile, f32),
                pltpu.VMEM((2,) + tile, f32),
                pltpu.VMEM((2,) + tile, f32),
                pltpu.VMEM((2, 2) + tile, f32),
                pltpu.VMEM((2,) + tile, f32),
                pltpu.VMEM((2, 6, D, W), f32),
                pltpu.VMEM((2, 6, D, W), f32),
                pltpu.VMEM((2, 5, D, W), f32),
                pltpu.VMEM((2, 5, D, W), f32),
                pltpu.VMEM((2, D, W), f32),
                pltpu.VMEM((2, D, W), f32),
                pltpu.VMEM((2, D, W), f32),
                pltpu.VMEM((2, D, W), f32),
                pltpu.VMEM((2, 2) + tile, f32),
                pltpu.VMEM((2, 2) + tile, f32),
                pltpu.VMEM((2, 2) + tile, f32),
                pltpu.VMEM((2,) + tile, f32),
                pltpu.VMEM((2,) + tile, f32),
                pltpu.VMEM((2, 5, 2 * H, W), f32),
                pltpu.VMEM((2, 5, D, W), f32),
                pltpu.VMEM((2, 3, D, W), f32),
                pltpu.VMEM((D + 2,) + tile, f32),
                pltpu.VMEM((D + 2, 9) + tile, f32),
                pltpu.VMEM((2,) + concentration.shape, f32),
                pltpu.VMEM((2, ncy + 2, ncx), f32),
                pltpu.VMEM((rows, wide), f32),
                pltpu.VMEM((ny, nx, rows, wide), f32),
                pltpu.VMEM((3, ncy, wide), f32),
                pltpu.SemaphoreType.DMA((D + 4,)),
                pltpu.SemaphoreType.DMA((moves,)),
                pltpu.SemaphoreType.DMA((moves,)),
                pltpu.SemaphoreType.DMA((2, 2)),
                pltpu.SemaphoreType.DMA((ny * nx - 1,)),
                pltpu.SemaphoreType.DMA((ny * nx - 1,)),
            ],
            compiler_params=pltpu.CompilerParams(collective_id=0, has_side_effects=True),
        )(populations, solid, ports, concentration, loaded)
        return pl.pallas_call(
            hand_out,
            out_shape=tuple(jax.ShapeDtypeStruct(a.shape, f32) for a in results),
            in_specs=[inside] * 3,
            out_specs=(anywhere,) * 3,
            scratch_shapes=[pltpu.SemaphoreType.DMA((3,))],
        )(*[pltpu.with_memory_space_constraint(a, pltpu.VMEM) for a in made])

    placed = (
        P(None, "gz", "gy", "gx"),
        P("gz", "gy", "gx"),
        P(None, "gy", "gx"),
        P(None, "gz", None, None),
        P(None, "gz", None, None),
    )
    return jax.shard_map(
        body,
        mesh=mesh,
        in_specs=placed,
        out_specs=(P(None, "gz", "gy", "gx"), P(None, "gz", None, None), P(None, "gz", None, None)),
        check_vma=False,
    )
```

```python
import functools

import jax
import jax.numpy as jnp
from jax import lax
from jax.experimental import pallas as pl
from jax.experimental.pallas import tpu as pltpu
from jax.sharding import PartitionSpec as P

ITERS = 2
CELL = 8
MESH = pl.DeviceIdType.MESH

lattice = [
    (0, 0, 0),
    (1, 0, 0),
    (-1, 0, 0),
    (0, 1, 0),
    (0, -1, 0),
    (0, 0, 1),
    (0, 0, -1),
    (1, 1, 0),
    (-1, -1, 0),
    (1, -1, 0),
    (-1, 1, 0),
    (1, 0, 1),
    (-1, 0, -1),
    (1, 0, -1),
    (-1, 0, 1),
    (0, 1, 1),
    (0, -1, -1),
    (0, 1, -1),
    (0, -1, 1),
]
opposite = [0, 2, 1, 4, 3, 6, 5, 8, 7, 10, 9, 12, 11, 14, 13, 16, 15, 18, 17]
weights = [1.0 / 3.0] + [1.0 / 18.0] * 6 + [1.0 / 36.0] * 12
relax_rate = 1.25
base_density = 36.0
inlet_speed = 0.05
spread_base = (0.03, 0.06)
spread_length = 0.1
uptake_rate = (0.3, 0.6)
affinity = (2.0, 0.5)
phase_ratio = 0.5
feed_level = (1.0, 0.5)

GROUPS = [[[m for m in range(19) if lattice[m][d] == s] for s in (1, -1)] for d in range(3)]
FLAT = [m for m in range(19) if lattice[m][2] == 0]
SOLID = 14
ORDER = GROUPS[0][0] + [m for m in range(19) if lattice[m][0] == 0] + [None] + GROUPS[0][1]
SLOT = {m: i for i, m in enumerate(ORDER) if m is not None}
TYPES = [(cy, cx) for cy in (1, 0, -1) for cx in (1, 0, -1)]


def moments(f):
    density = f[0]
    for member in range(1, 19):
        density = density + f[member]
    return density, momentum(f)


def momentum(f):
    flows = []
    for d in range(3):
        total = None
        for a, b in zip(GROUPS[d][0], [opposite[m] for m in GROUPS[d][0]]):
            part = f[a] - f[b]
            total = part if total is None else total + part
        flows.append(total)
    return flows


def balance(scale, velocity, members):
    square = velocity[0] * velocity[0] + velocity[1] * velocity[1] + velocity[2] * velocity[2]
    base = 1.0 - 1.5 * square
    cache, result = {}, {}
    for w in set(weights[m] for m in members):
        cache[w] = scale * w
    for m in members:
        if m == 0:
            result[m] = cache[weights[0]] * base
            continue
        key = min(m, opposite[m])
        if ("pair", key) not in cache:
            along = None
            for d in range(3):
                step = lattice[key][d]
                if step:
                    term = velocity[d]
                    if along is None:
                        along = term if step == 1 else -term
                    else:
                        along = along + term if step == 1 else along - term
            cache[("pair", key)] = (base + 4.5 * along * along, 3.0 * along)
        even, odd = cache[("pair", key)]
        result[m] = cache[weights[m]] * (even + odd if m == key else even - odd)
    return result


def collide(f, solid):
    density, flows = moments(f)
    inverse = 1.0 / density
    velocity = [flow * inverse for flow in flows]
    feq = balance(relax_rate * density, velocity, range(19))
    post = [
        jnp.where(solid, f[opposite[m]], (1.0 - relax_rate) * f[m] + feq[m]) for m in range(19)
    ]
    return post, velocity


def edge_rows(side, ends):
    far, near = ends
    across = [m for m in GROUPS[0][side[0]] if lattice[m][1] == 1 - 2 * side[1]]
    along = [m for m in GROUPS[1][side[1]] if lattice[m][0] == 0]
    return [(across[0], far, 0), (across[0], near, 1)] + [(m, near, 0) for m in along]


def level_sums(view, line, row, last, rolled):
    parts = {}
    for cy in (0, 1, -1):
        members = [m for m in range(19) if lattice[m][0] == 0 and lattice[m][1] == cy]
        for weigh in (lambda m: 1, lambda m: lattice[m][2]):
            moved, edge = None, None
            for m in members:
                for which, value in ((0, view(m)), (1, line(m) if cy else None)):
                    if value is None or not weigh(m):
                        continue
                    if which == 0:
                        value = value if weigh(m) == 1 else -value
                        moved = value if moved is None else moved + value
                    else:
                        value = value if weigh(m) == 1 else -value
                        edge = value if edge is None else edge + value
            if cy:
                edge = 0.0 if edge is None else jnp.broadcast_to(edge, moved.shape)
                moved = jnp.where(row == (0 if cy == 1 else last), edge, rolled(moved, cy, 0))
            parts.setdefault(cy, []).append(moved)
    return (parts[0][0] + parts[1][0] + parts[-1][0], parts[1][0] - parts[-1][0],
            parts[0][1] + parts[1][1] + parts[-1][1])


def kernel(sizes, *refs):
    nz, ny, nx = sizes
    (pop_hbm, solid_hbm, ports_hbm, conc_hbm, load_hbm, out, new_conc, new_load,
     pops, solid, ports, conc, load, post0, post1, bound, speed, zpack, zrecv, xpack, xrecv, xside, xline,
     ypack, yrecv, ypack1, yrecv1, cpack, crecv, cpack1, crecv1, epack, erecv, erecv_far, xpack1, xrecv1,
     yline, yline1, sline, frame, pore, sxpack, sxrecv, sypack, syrecv, screcv, cend, near, wrapped,
     sent_v, all_v, vel, count_ref, load_sem, send_sem, recv_sem) = refs
    D, H, W = solid.shape
    T = D + 2
    ncy, ncx = conc.shape[2:]
    f32 = jnp.float32
    gz, gy, gx = lax.axis_index("gz"), lax.axis_index("gy"), lax.axis_index("gx")
    is_first, is_last = gz == 0, gz == nz - 1
    has_up, has_down = gz < nz - 1, gz > 0
    early = jnp.where(gz == 0, gx, 1) == 0
    late = jnp.where(gz == 0, gx, 1) > 0
    bound_at = len(FLAT) * T
    port_at = bound_at + 5
    solid_at = port_at + 2 + (port_at % 2)
    bound_at1 = len(FLAT) * D

    spans = [(0, 2), (D - 2, 2), (2, D - 4)]
    planes_in = [
        pltpu.make_async_copy(pop_hbm.at[:, pl.ds(a, n)], pops.at[:, pl.ds(a, n)], load_sem.at[i])
        for i, (a, n) in enumerate(spans)
    ]
    small = [
        pltpu.make_async_copy(a, b, load_sem.at[3 + i])
        for i, (a, b) in enumerate(
            ((solid_hbm, solid), (ports_hbm, ports), (conc_hbm, conc), (load_hbm, load)))
    ]
    planes_in[0].start()
    small[0].start()
    small[1].start()
    planes_in[1].start()
    planes_in[2].start()
    small[2].start()
    small[3].start()

    def at(offset):
        dz, dy, dx = offset
        return {"gz": gz + dz, "gy": lax.rem(gy + dy + ny, ny), "gx": lax.rem(gx + dx + nx, nx)}

    flat = [(0, dy, dx) for dx in [nx - 1] + list(range(nx - 1)) for dy in range(ny) if dy or dx]
    told = {(0, dy % ny, nx - 1) for dy in (0, 1, -1)} if nx > 2 else set()
    targets = sorted({(dy % ny, dx) for dy in (0, 1, -1) for dx in (0, 1)})
    barrier = pltpu.get_barrier_semaphore()

    def greet(offsets):
        for offset in offsets:
            pl.semaphore_signal(barrier, inc=1, device_id=at(offset), device_id_type=MESH)

    greet([(0, -dy, -dx) for _, dy, dx in flat if (0, dy, dx) not in told])

    @pl.when(has_up)
    def _():
        greet([(1, -dy, -dx) for dy, dx in targets])

    @pl.when(has_down)
    def _():
        greet([(-1, -dy, -dx) for dy, dx in targets])

    lane = lax.broadcasted_iota(jnp.int32, (H, W), 1)
    row = lax.broadcasted_iota(jnp.int32, (H, W), 0)
    pair = lax.div(lane, 2)
    first_mask = jnp.full((H, W), gz, jnp.int32) == 0
    last_mask = jnp.full((H, W), gz, jnp.int32) == nz - 1
    zero = jnp.zeros((H, W), f32)

    def rolled(x, step, axis):
        step = step % x.shape[axis]
        return pltpu.roll(x, step, axis) if step else x

    def put(acc, value, spot, shift):
        return jnp.where(lane == spot, rolled(value, shift, 1), acc)

    def put_pair(acc, value, half, shift):
        return jnp.where(pair == half, rolled(value, shift, 1), acc)

    def edge_row(value, s):
        return value[H - 1 :, :] if s == 0 else value[:1, :]

    FLAGS, Y, X, BELOW, ABOVE, BACK, VEL = range(7)
    SLAB, UP, DOWN, VEL_OUT = range(4)
    side_sets = [(pl.ds(0, 2), 1)] if ny == 2 else [(pl.ds(0, 1), 1), (pl.ds(1, 1), -1)]

    def remote(src, dst, offset, group):
        sent = {0: SLAB, 1: UP, -1: DOWN}[offset[0]]
        return pltpu.make_async_remote_copy(
            src_ref=src, dst_ref=dst, send_sem=send_sem.at[sent], recv_sem=recv_sem.at[group],
            device_id=at(offset), device_id_type=MESH)

    def arrived(sem, tiles):
        whole = count_ref.at[pl.ds(0, tiles)]
        pltpu.make_async_copy(whole, whole, sem).wait()

    def start(copies):
        for copy in copies:
            copy.start()

    along_z = {}
    for dz, zs, group in ((1, 0, BELOW), (-1, 1, ABOVE)):
        along_z[dz] = [remote(zpack.at[zs], zrecv.at[zs], (dz, 0, 0), group)]
        for where, dy in side_sets:
            along_z[dz].append(remote(epack.at[zs, where], erecv_far.at[zs, where], (dz, dy, 1), group))
            along_z[dz].append(remote(epack.at[zs, where], erecv.at[zs, where], (dz, dy, 0), group))
    flank = {dz: remote(xpack, xside.at[zs], (dz, 0, 1), group)
             for dz, zs, group in ((1, 0, BELOW), (-1, 1, ABOVE))}
    ends = {dz: remote(cend, near.at[zs], (dz, 0, 0), group)
            for dz, zs, group in ((1, 0, BELOW), (-1, 1, ABOVE))}
    z_tiles = zpack.shape[1] + 4 + 2 + cend.shape[0] // H
    flags = [remote(sxpack, sxrecv, (0, 0, 1), FLAGS)]
    for where, dy in side_sets:
        flags.append(remote(sypack.at[where], screcv.at[where], (0, dy, 1), FLAGS))
        flags.append(remote(sypack.at[where], syrecv.at[where], (0, dy, 0), FLAGS))
    slab = [remote(xpack, xrecv, (0, 0, 1), X)]
    back_c = []
    back = [remote(xpack1, xrecv1, (0, 0, -1), BACK)]
    for where, dy in side_sets:
        slab.append(remote(cpack.at[where], crecv.at[where], (0, dy, 1), Y))
        slab.append(remote(ypack.at[where], yrecv.at[where], (0, dy, 0), Y))
        back.append(remote(ypack1.at[where], yrecv1.at[where], (0, dy, 0), BACK))
        back_c.append(remote(cpack1.at[where], crecv1.at[where], (0, dy, -1), BACK))
    slab_tiles = 5 + 2 + 12 + 14

    edge_table = [
        [edge_rows((zs, s), ((D - 2, D - 1), (1, 0))[zs]) for s in range(2)] for zs in range(2)]

    small[0].wait()
    small[1].wait()
    walls_out = zero
    for z in range(D):
        wall = solid[z].astype(f32)
        walls_out = put_pair(walls_out, wall, z, 2 * z + 2)
        for s in range(2):
            sypack[s, z : z + 1, :] = edge_row(wall, s)
    sxpack[...] = walls_out

    def shifted(value, lanes, fill=0.0):
        return jnp.where(lane < lanes, fill, rolled(value, lanes, 1)) if lanes else value

    def first_plane(z, packs):
        f = [pops[m, z] for m in range(19)]
        flag = solid[z]
        post, velocity = collide(f, flag == 1)
        for m in range(19):
            post0[z, m] = post[m]
        for zs, ends_at in ((0, (D - 1, D - 2)), (1, (0, 1))):
            if z in ends_at:
                base = 5 * ends_at.index(z)
                for j, m in enumerate(GROUPS[0][zs]):
                    zpack[zs, base + j] = post[m]
            if z == ends_at[0]:
                sums = level_sums(lambda m: shifted(post[m], 1 + lattice[m][2]), lambda m: None,
                                  row, H - 1, rolled)
                for d in range(3):
                    zpack[zs, 10 + d] = sums[d]
                zpack[zs, 13] = flag.astype(f32)
        for s in range(2):
            for i, m in enumerate(GROUPS[1][s]):
                ypack[s, i, z : z + 1, :] = edge_row(post[m], s)
        for zs in range(2):
            for s in range(2):
                for r, (m, source, _) in enumerate(edge_table[zs][s]):
                    if source == z:
                        epack[zs, s, r : r + 1, :] = edge_row(post[m], s)
        if z == 0:
            inflow = equilibrium_at_inlet()
            for j, m in enumerate(GROUPS[0][0]):
                bound[0, j] = jnp.where(ports[0] == 1, inflow[m], post[opposite[m]])
        if z == D - 1:
            outflow = balance(base_density, velocity, GROUPS[0][1])
            for j, m in enumerate(GROUPS[0][1]):
                leaving = jnp.where(ports[1] == 1, outflow[m], post[opposite[m]])
                bound[0, j] = jnp.where(last_mask, leaving, bound[0, j])
        twos, ones = packs
        for i, m in enumerate(GROUPS[2][0]):
            q = i * T + z + lattice[m][0] + 1
            twos = put_pair(twos, post[m], q, 2 * q + 2)
        for i, m in enumerate(FLAT):
            q = i * T + z + lattice[m][0] + 1
            ones = put(ones, post[m], q, q + 1)
        if z in (0, D - 1):
            q = solid_at // 2 + (0 if z == 0 else 1)
            ones = put_pair(ones, flag.astype(f32), q, 2 * q + 2)
        return twos, ones

    def enter():
        count = lambda flag: jnp.where(flag, len(targets), 0)
        pl.semaphore_wait(barrier, len(flat) - len(told) + count(has_up) + count(has_down))
        start(flags)

    packs = (zero, zero)
    planes_in[0].wait()
    for z in (0, 1):
        packs = first_plane(z, packs)

    @pl.when(late)
    def _():
        enter()

        @pl.when(has_down)
        def _():
            start(along_z[-1])

    planes_in[1].wait()
    for z in (D - 1, D - 2):
        packs = first_plane(z, packs)

    @pl.when(late)
    def _():
        @pl.when(has_up)
        def _():
            start(along_z[1])

    planes_in[2].wait()
    for z in range(2, D - 2):
        packs = first_plane(z, packs)
    twos, ones = packs
    for j in range(5):
        ones = put(ones, bound[0, j], bound_at + j, bound_at + j + 1)
    for j in range(2):
        ones = put(ones, ports[j].astype(f32), port_at + j, port_at + j + 1)
    xpack[0], xpack[1] = twos, ones
    for s in range(2):
        acc = zero
        for i in range(5):
            acc = put_pair(acc, ypack[s, i], i, 2 * i + 2)
        cpack[s] = acc
    small[2].wait()
    small[3].wait()
    cend[...] = jnp.zeros(cend.shape, f32)
    for s in range(2):
        cend[s * ncy : (s + 1) * ncy, 0:ncx] = conc[s, 0]

    @pl.when(early)
    def _():
        enter()

        @pl.when(has_up)
        def _():
            start(along_z[1])

    start(slab[:1])
    for dz, there in ((-1, has_down), (1, has_up)):
        @pl.when(there)
        def _():
            flank[dz].start()
    start(slab[1:])
    for dz, there in ((-1, has_down), (1, has_up)):
        @pl.when(there)
        def _():
            ends[dz].start()

    x_low, x_high = [], []
    for members, spot in ((GROUPS[2][0], pair), (FLAT, lane)):
        low, high = lane < 0, lane < 0
        for i, m in enumerate(members):
            cz = lattice[m][0]
            if cz >= 0:
                low = low | ((spot >= i * T) & (spot < i * T + 1 + cz))
            if cz <= 0:
                high = high | ((spot >= i * T + D + 1 + cz) & (spot < i * T + T))
        x_low.append(low)
        x_high.append(high)

    diffs = []
    wide = sent_v.shape[-1]
    parts = []
    for c in (1, 0, -1):
        voxel = lax.broadcasted_iota(jnp.int32, (W, wide), 0) + gx * W - 1 + c
        voxel = jnp.where(voxel < 0, voxel + nx * W, voxel)
        cell = lax.broadcasted_iota(jnp.int32, (W, wide), 1) * CELL
        parts.append(((voxel >= cell) & (voxel < cell + CELL)).astype(f32))
    pick = jnp.concatenate(parts, axis=0).astype(jnp.bfloat16)

    arrived(recv_sem.at[FLAGS], 5)
    for s in range(2):
        for n in range(3):
            tile, far = syrecv[s], screcv[s]
            sline[s, n] = shifted(tile, n, rolled(far, n, 1)) if n else tile
    for n in range(9):
        pore[0, n] = zero
        pore[D + 1, n] = zero
    for k in range(1, D + 1):
        walls = solid[k - 1].astype(f32)
        columns = sxrecv[...]
        one = shifted(walls, 1, rolled(columns, 1 - 2 * k, 1))
        two = shifted(walls, 2, rolled(columns, 2 - 2 * k, 1))
        frame[k] = one
        for n, view in enumerate((walls, one, two)):
            cx = 1 - n
            pore[k, TYPES.index((0, cx))] = 1.0 - view
            for cy in (1, -1):
                s = 1 if cy == 1 else 0
                line = sline[s, n, k - 1 : k, :]
                moved = jnp.where(row == (H - 1 if cy == 1 else 0),
                                  jnp.broadcast_to(line, (H, W)), rolled(view, -cy, 0))
                pore[k, TYPES.index((cy, cx))] = 1.0 - moved

    arrived(recv_sem.at[Y], 12)

    def filled(tile, columns, lanes, spot):
        return shifted(tile, lanes, rolled(columns, -(spot + 2 - lanes), 1)) if lanes else tile

    for s in range(2):
        corner = crecv[s]
        for i, m in enumerate(GROUPS[1][s]):
            cz, _, cx = lattice[m]
            yline[s, i, 1 + cz : 1 + cz + D, :] = filled(yrecv[s, i], corner, 1 + cx, 2 * i)

    def column_of(m, k):
        if lattice[m][2] == 1:
            return rolled(xline[0], -2 * (GROUPS[2][0].index(m) * T + k), 1)
        return rolled(xline[1], -(FLAT.index(m) * T + k), 1)

    def line_of(m, k):
        s = 0 if lattice[m][1] == 1 else 1
        return yline[s, GROUPS[1][s].index(m), k : k + 1, :]

    def stream(k, members):
        f = {}
        for m in members:
            cz, cy, cx = lattice[m]
            z = k - 1 - cz
            if 0 <= z < D:
                v = post0[z, m]
            else:
                zs = 0 if cz == 1 else 1
                v = zrecv[zs, GROUPS[0][zs].index(m) + (5 if z in (-2, D + 1) else 0)]
            if cx >= 0:
                v = shifted(v, 1 + cx, column_of(m, k))
            if cy:
                v = jnp.where(row == (0 if cy == 1 else H - 1),
                              jnp.broadcast_to(line_of(m, k), (H, W)), rolled(v, cy, 0))
            f[m] = v
        return f

    def port_view(j):
        return shifted(ports[j].astype(f32), 1, rolled(xline[1], -(port_at + j), 1)) > 0.5

    def bound_view(j):
        return shifted(bound[0, j], 1, rolled(xline[1], -(bound_at + j), 1))

    names = [("n", cy, cx) for cy, cx in TYPES if cy or cx]
    names += [("z", cy, cx) for cy, cx in TYPES if not (cy and cx)]

    def keep(k, post, carry):
        twos, ones, sums = carry
        for m, value in post.items():
            cz, cy, cx = lattice[m]
            post1[k, m] = value
            t = k - 1 + cz
            if not 0 <= t < D:
                continue
            if cy:
                s = 0 if cy == 1 else 1
                ypack1[s, GROUPS[1][s].index(m), t : t + 1, :] = edge_row(value, s)
            if cx == -1:
                q = GROUPS[2][1].index(m) * D + t
                twos = put_pair(twos, value, q, 2 * q)
            elif cx == 0:
                q = FLAT.index(m) * D + t
                ones = put(ones, value, q, q)
            if m:
                part = value * pore[k + cz, TYPES.index((cy, cx))]
                if cy or cx:
                    sums["n", cy, cx] = sums["n", cy, cx] + part
                if cz == 1:
                    sums["z", cy, cx] = sums["z", cy, cx] + part
                if cz == -1:
                    sums["z", cy, cx] = sums["z", cy, cx] - part
        return twos, ones, sums

    def inner_plane(k, carry):
        f = stream(k, range(19))
        if k == 1:
            for j, m in enumerate(GROUPS[0][0]):
                f[m] = jnp.where(first_mask, bound_view(j), f[m])
        if k == D:
            for j, m in enumerate(GROUPS[0][1]):
                f[m] = jnp.where(last_mask, bound_view(j), f[m])
        post, velocity = collide([f[m] for m in range(19)], frame[k] > 0.5)
        carry = keep(k, dict(enumerate(post)), carry)
        if k in (1, D):
            if k == 1:
                members, opened, mask = GROUPS[0][0], port_view(0), first_mask
                values = equilibrium_at_inlet()
            else:
                members, opened, mask = GROUPS[0][1], port_view(1), last_mask
                values = balance(base_density, velocity, members)
            extra = [zero, zero, zero]
            for j, m in enumerate(members):
                value = jnp.where(opened, values[m], post[opposite[m]])
                bound[1, j] = value if k == 1 else jnp.where(last_mask, value, bound[1, j])
                for d in range(3):
                    if lattice[m][d]:
                        extra[d] = extra[d] + value if lattice[m][d] == 1 else extra[d] - value
            for d in range(3):
                add = jnp.where(mask, extra[d] * pore[k, TYPES.index((0, 0))], 0.0)
                speed[d] = add if k == 1 else speed[d] + add
        return carry

    def outer_plane(k, carry):
        zs, mask = (0, first_mask) if k == 0 else (1, last_mask)
        members = GROUPS[0][zs]
        f = stream(k, GROUPS[0][0] + GROUPS[0][1])
        sums = level_sums(
            lambda m: jnp.where(lane < 1 + lattice[m][2], column_of(m, k), 0.0) if lattice[m][2] >= 0 else None,
            lambda m: line_of(m, k), row, H - 1, rolled)
        density, flow_y, flow_x = [zrecv[zs, 10 + d] + sums[d] for d in range(3)]
        flows = [None, flow_y, flow_x]
        for m, value in f.items():
            density = density + value
            for d in range(3):
                if lattice[m][d]:
                    signed = value if lattice[m][d] == 1 else -value
                    flows[d] = signed if flows[d] is None else flows[d] + signed
        inverse = 1.0 / density
        feq = balance(relax_rate * density, [flow * inverse for flow in flows], members)
        wall = frame[k] > 0.5
        post = {}
        for m in members:
            made = jnp.where(wall, f[opposite[m]], (1.0 - relax_rate) * f[m] + feq[m])
            post[m] = jnp.where(mask, 0.0, made)
        return keep(k, post, carry)

    arrived(recv_sem.at[X], 2)
    xline[0], xline[1] = xrecv[0], xrecv[1]
    carry = (zero, zero, {name: zero for name in names})
    for k in range(2, D):
        carry = inner_plane(k, carry)

    for zs, there, group in ((0, has_down, BELOW), (1, has_up, ABOVE)):
        @pl.when(there)
        def _():
            arrived(recv_sem.at[group], z_tiles)

        beside = xside[zs, 0], xside[zs, 1]
        move = -D if zs == 0 else D
        masks = x_low if zs == 0 else x_high
        for n in range(2):
            xline[n] = jnp.where(masks[n], rolled(beside[n], move * (2 - n), 1), xline[n])
        for s in range(2):
            tile, far = erecv[zs, s], erecv_far[zs, s]
            views = [tile] + [shifted(tile, n, rolled(far, n, 1)) for n in (1, 2)]
            for r, (m, _, target) in enumerate(edge_table[zs][s]):
                k = target if zs == 0 else D + 1 - target
                yline[s, GROUPS[1][s].index(m), k : k + 1, :] = views[1 + lattice[m][2]][r : r + 1, :]
        k = 0 if zs == 0 else D + 1
        spot = solid_at + (3 if zs == 0 else 1)
        frame[k] = shifted(zrecv[zs, 13], 1, rolled(beside[1], -spot, 1))
        carry = inner_plane(1 if zs == 0 else D, carry)
        carry = outer_plane(k, carry)

    twos, ones, sums = carry
    for j in range(5):
        ones = put(ones, bound[1, j], bound_at1 + j, bound_at1 + j)
    xpack1[0], xpack1[1] = twos, ones
    start(back)

    top, bottom = row == H - 1, row == 0
    blocks = []
    for cx in (1, 0, -1):
        own = [zero, zero, zero]
        up, down = [zero] * 3, [zero] * 3
        if ("n", 0, cx) in sums and cx:
            own[2] = sums["n", 0, cx] if cx == 1 else -sums["n", 0, cx]
        own[0] = sums["z", 0, cx]
        for cy, beyond, edge in ((1, up, top), (-1, down, bottom)):
            n = sums["n", cy, cx]
            values = [sums.get(("z", cy, cx)), n if cy == 1 else -n, {1: n, 0: None, -1: -n}[cx]]
            for d in range(3):
                if values[d] is not None:
                    own[d] = own[d] + jnp.where(edge, 0.0, values[d])
                    beyond[d] = values[d]
        if cx == 0:
            own = [own[d] + speed[d] for d in range(3)]
        totals = [jnp.sum(v, axis=0, keepdims=True) for v in own]
        ups = [v[H - 1 :, :] for v in up]
        downs = [v[:1, :] for v in down]
        if ny == 2:
            lines = totals + [a + b for a, b in zip(ups, downs)]
        else:
            lines = totals + ups + downs
        blocks.append(lines)
    tiles = []
    for base in range(0, sent_v.shape[0], H):
        here = []
        for lines in blocks:
            tile = zero
            for r, line in enumerate(lines[base : base + H]):
                tile = jnp.where(row == r, jnp.broadcast_to(line, (H, W)), tile)
            here.append(tile)
        tiles.append(jnp.concatenate(here, axis=1))

    def exact_pick(x):
        high = x.astype(jnp.bfloat16).astype(f32)
        mid = (x - high).astype(jnp.bfloat16).astype(f32)
        low = x - high - mid
        stacked = jnp.concatenate([high, mid, low], axis=0).astype(jnp.bfloat16)
        made = jnp.dot(stacked, pick, preferred_element_type=f32)
        return made[:H] + made[H : 2 * H] + made[2 * H :]

    for i, tile in enumerate(tiles):
        sent_v[i * H : (i + 1) * H, :] = exact_pick(tile) * (1.0 / (CELL * CELL * CELL * base_density))
    tell = [
        pltpu.make_async_remote_copy(
            src_ref=sent_v, dst_ref=all_v.at[gy, gx], send_sem=send_sem.at[VEL_OUT],
            recv_sem=recv_sem.at[VEL], device_id=at(offset), device_id_type=MESH)
        for offset in flat
    ]
    start(tell)
    all_v[gy, gx] = sent_v[...]
    for s in range(2):
        acc = zero
        for i, m in enumerate(GROUPS[1][s]):
            if lattice[m][2] <= 0:
                acc = put_pair(acc, ypack1[s, i], i, 2 * i)
        cpack1[s] = acc
    start(back_c)

    @pl.when(is_first)
    def _():
        for s in range(2):
            near[0, s * ncy : (s + 1) * ncy, :] = jnp.full((ncy, wide), feed_level[s], f32)

    @pl.when(is_last)
    def _():
        near[1] = cend[...]

    source = lax.broadcasted_iota(jnp.int32, (ncx, ncx), 0)
    target = lax.broadcasted_iota(jnp.int32, (ncx, ncx), 1)
    ahead = jnp.where(target == ncx - 1, 0, target + 1)
    behind = jnp.where(target == 0, ncx - 1, target - 1)
    take_after = (source == ahead).astype(f32)
    take_before = (source == behind).astype(f32)

    def exact_dot(a, b):
        return jnp.dot(a, b, precision=lax.Precision.HIGHEST, preferred_element_type=f32)

    for s in range(2):
        c = conc[s, 0]
        wrapped[s, 1 : ncy + 1, :] = c
        wrapped[s, 0:1, :] = conc[s, 0, ncy - 1 : ncy, :]
        wrapped[s, ncy + 1 : ncy + 2, :] = conc[s, 0, 0:1, :]
        pairs = [
            tuple(near[e, s * ncy : (s + 1) * ncy, 0:ncx] for e in range(2)),
            (wrapped[s, 0:ncy, :], wrapped[s, 2 : ncy + 2, :]),
            (exact_dot(c, take_before), exact_dot(c, take_after)),
        ]
        curvature = sum(b + a - 2.0 * c for b, a in pairs)
        rate = uptake_rate[s] * (affinity[s] * c - load[s, 0])
        new_load[s, 0] = load[s, 0] + rate
        diffs.append((c - phase_ratio * rate + spread_base[s] * curvature, curvature,
                      [(c - b, a - c) for b, a in pairs]))

    arrived(recv_sem.at[BACK], 14)

    def emptied(tile, lanes, columns):
        return jnp.where(lane >= W - lanes, columns, rolled(tile, -lanes, 1)) if lanes else tile

    for s in range(2):
        corner = crecv1[s]
        for i, m in enumerate(GROUPS[1][s]):
            lanes = 1 - lattice[m][2]
            yline1[s, i] = emptied(yrecv1[s, i], lanes, rolled(corner, -lanes - 2 * i, 1))

    for t in range(D):
        for m in range(19):
            cz, cy, cx = lattice[m]
            v = post1[t + 1 - cz, m]
            if cx == -1:
                spot = 2 * (GROUPS[2][1].index(m) * D + t)
                v = emptied(v, 2, rolled(xrecv1[0], -2 - spot, 1))
            elif cx == 0:
                v = emptied(v, 1, rolled(xrecv1[1], -1 - (FLAT.index(m) * D + t), 1))
            if cy:
                s = 0 if cy == 1 else 1
                line = yline1[s, GROUPS[1][s].index(m), t : t + 1, :]
                v = jnp.where(row == (0 if s == 0 else H - 1),
                              jnp.broadcast_to(line, (H, W)), rolled(v, cy, 0))
            if (t == 0 and cz == 1) or (t == D - 1 and cz == -1):
                j = GROUPS[0][0 if cz == 1 else 1].index(m)
                kept = emptied(bound[1, j], 1, rolled(xrecv1[1], -1 - (bound_at1 + j), 1))
                v = jnp.where(first_mask if cz == 1 else last_mask, kept, v)
            out[m, t] = v

    arrived(send_sem.at[SLAB], slab_tiles)
    for sem, there in ((UP, has_up), (DOWN, has_down)):
        @pl.when(there)
        def _():
            arrived(send_sem.at[sem], z_tiles)
    vel_tiles = len(flat) * (sent_v.shape[0] // H)
    arrived(recv_sem.at[VEL], vel_tiles)
    totals = []
    for y in range(ny):
        total = all_v[y, 0]
        for x in range(1, nx):
            total = total + all_v[y, x]
        totals.append(total)
    for y in range(ny):
        for d in range(3):
            own = totals[y][d : d + 1]
            if ny == 2:
                own = own + totals[1 - y][3 + d : 4 + d]
            else:
                own = own + totals[(y - 1) % ny][3 + d : 4 + d] + totals[(y + 1) % ny][6 + d : 7 + d]
            vel[d, y : y + 1, :] = own
    courant = [CELL * vel[d][:, :ncx] for d in range(3)]
    reach = jnp.abs(courant[0]) + jnp.abs(courant[1]) + jnp.abs(courant[2])
    for s in range(2):
        value, curvature, steps = diffs[s]
        for d in range(3):
            low, high = steps[d]
            value = value - jnp.maximum(courant[d], 0.0) * low - jnp.minimum(courant[d], 0.0) * high
        new_conc[s, 0] = value + spread_length * reach * curvature
    arrived(send_sem.at[VEL_OUT], vel_tiles)


def hand_out(*refs):
    copies = [pltpu.make_async_copy(refs[i], refs[3 + i], refs[6].at[i]) for i in range(3)]
    for copy in copies:
        copy.start()
    for copy in copies:
        copy.wait()


def equilibrium_at_inlet():
    result = {}
    for m in GROUPS[0][0]:
        along = inlet_speed
        result[m] = weights[m] * base_density * (
            1.0 + 3.0 * along + 4.5 * along * along - 1.5 * inlet_speed * inlet_speed)
    return result


def solution(mesh):
    sizes = tuple(mesh.shape[a] for a in ("gz", "gy", "gx"))
    nz, ny, nx = sizes

    def body(populations, solid, ports, concentration, loaded):
        D, H, W = solid.shape
        ncy, ncx = concentration.shape[2:]
        assert D == CELL and H == CELL and W % 128 == 0 and 12 * (D + 2) <= W
        wide = -(-ncx // 128) * 128
        assert nz > 1 and ny > 1 and nx > 1 and W == wide
        f32 = jnp.float32
        tile = (H, W)
        rows = H if ny == 2 else 2 * H
        ends = -(-2 * ncy // H) * H
        anywhere = pl.BlockSpec(memory_space=pl.ANY)
        inside = pl.BlockSpec(memory_space=pltpu.VMEM)
        results = (populations, concentration, loaded)
        made = pl.pallas_call(
            functools.partial(kernel, sizes),
            out_shape=tuple(pltpu.VMEM(a.shape, f32) for a in results),
            in_specs=[anywhere] * 5,
            out_specs=(inside,) * 3,
            scratch_shapes=[
                pltpu.VMEM(populations.shape, f32),
                pltpu.VMEM(solid.shape, jnp.int32),
                pltpu.VMEM(ports.shape, jnp.int32),
                pltpu.VMEM(concentration.shape, f32),
                pltpu.VMEM(loaded.shape, f32),
                pltpu.VMEM((D, 19) + tile, f32),
                pltpu.VMEM((D + 2, 19) + tile, f32),
                pltpu.VMEM((2, 5) + tile, f32),
                pltpu.VMEM((3,) + tile, f32),
                pltpu.VMEM((2, 14) + tile, f32),
                pltpu.VMEM((2, 14) + tile, f32),
                pltpu.VMEM((2,) + tile, f32),
                pltpu.VMEM((2,) + tile, f32),
                pltpu.VMEM((2, 2) + tile, f32),
                pltpu.VMEM((2,) + tile, f32),
                pltpu.VMEM((2, 5, D, W), f32),
                pltpu.VMEM((2, 5, D, W), f32),
                pltpu.VMEM((2, 5, D, W), f32),
                pltpu.VMEM((2, 5, D, W), f32),
                pltpu.VMEM((2, D, W), f32),
                pltpu.VMEM((2, D, W), f32),
                pltpu.VMEM((2, D, W), f32),
                pltpu.VMEM((2, D, W), f32),
                pltpu.VMEM((2, 2) + tile, f32),
                pltpu.VMEM((2, 2) + tile, f32),
                pltpu.VMEM((2, 2) + tile, f32),
                pltpu.VMEM((2,) + tile, f32),
                pltpu.VMEM((2,) + tile, f32),
                pltpu.VMEM((2, 5, 2 * H, W), f32),
                pltpu.VMEM((2, 5, D, W), f32),
                pltpu.VMEM((2, 3, D, W), f32),
                pltpu.VMEM((D + 2,) + tile, f32),
                pltpu.VMEM((D + 2, 9) + tile, f32),
                pltpu.VMEM(tile, f32),
                pltpu.VMEM(tile, f32),
                pltpu.VMEM((2, D, W), f32),
                pltpu.VMEM((2, D, W), f32),
                pltpu.VMEM((2, D, W), f32),
                pltpu.VMEM((ends, wide), f32),
                pltpu.VMEM((2, ends, wide), f32),
                pltpu.VMEM((2, ncy + 2, ncx), f32),
                pltpu.VMEM((rows, wide), f32),
                pltpu.VMEM((ny, nx, rows, wide), f32),
                pltpu.VMEM((3, ncy, wide), f32),
                pltpu.VMEM((max(40, 2 * ny * nx),) + tile, f32),
                pltpu.SemaphoreType.DMA((7,)),
                pltpu.SemaphoreType.DMA((4,)),
                pltpu.SemaphoreType.DMA((7,)),
            ],
            compiler_params=pltpu.CompilerParams(collective_id=0, has_side_effects=True),
        )(populations, solid, ports, concentration, loaded)
        return pl.pallas_call(
            hand_out,
            out_shape=tuple(jax.ShapeDtypeStruct(a.shape, f32) for a in results),
            in_specs=[inside] * 3,
            out_specs=(anywhere,) * 3,
            scratch_shapes=[pltpu.SemaphoreType.DMA((3,))],
        )(*[pltpu.with_memory_space_constraint(a, pltpu.VMEM) for a in made])

    placed = (
        P(None, "gz", "gy", "gx"),
        P("gz", "gy", "gx"),
        P(None, "gy", "gx"),
        P(None, "gz", None, None),
        P(None, "gz", None, None),
    )
    return jax.shard_map(
        body,
        mesh=mesh,
        in_specs=placed,
        out_specs=(P(None, "gz", "gy", "gx"), P(None, "gz", None, None), P(None, "gz", None, None)),
        check_vma=False,
    )
```

```python
import functools

import jax
import jax.numpy as jnp
from jax import lax
from jax.experimental import pallas as pl
from jax.experimental.pallas import tpu as pltpu
from jax.sharding import PartitionSpec as P

ITERS = 2
CELL = 8
MESH = pl.DeviceIdType.MESH

lattice = [
    (0, 0, 0),
    (1, 0, 0),
    (-1, 0, 0),
    (0, 1, 0),
    (0, -1, 0),
    (0, 0, 1),
    (0, 0, -1),
    (1, 1, 0),
    (-1, -1, 0),
    (1, -1, 0),
    (-1, 1, 0),
    (1, 0, 1),
    (-1, 0, -1),
    (1, 0, -1),
    (-1, 0, 1),
    (0, 1, 1),
    (0, -1, -1),
    (0, 1, -1),
    (0, -1, 1),
]
opposite = [0, 2, 1, 4, 3, 6, 5, 8, 7, 10, 9, 12, 11, 14, 13, 16, 15, 18, 17]
weights = [1.0 / 3.0] + [1.0 / 18.0] * 6 + [1.0 / 36.0] * 12
relax_rate = 1.25
base_density = 36.0
inlet_speed = 0.05
spread_base = (0.03, 0.06)
spread_length = 0.1
uptake_rate = (0.3, 0.6)
affinity = (2.0, 0.5)
phase_ratio = 0.5
feed_level = (1.0, 0.5)

GROUPS = [[[m for m in range(19) if lattice[m][d] == s] for s in (1, -1)] for d in range(3)]
FLAT = [m for m in range(19) if lattice[m][2] == 0]
SOLID = 14
ORDER = GROUPS[0][0] + [m for m in range(19) if lattice[m][0] == 0] + [None] + GROUPS[0][1]
SLOT = {m: i for i, m in enumerate(ORDER) if m is not None}
TYPES = [(cy, cx) for cy in (1, 0, -1) for cx in (1, 0, -1)]


def moments(f):
    density = f[0]
    for member in range(1, 19):
        density = density + f[member]
    return density, momentum(f)


def momentum(f):
    flows = []
    for d in range(3):
        total = None
        for a, b in zip(GROUPS[d][0], [opposite[m] for m in GROUPS[d][0]]):
            part = f[a] - f[b]
            total = part if total is None else total + part
        flows.append(total)
    return flows


def balance(scale, velocity, members):
    square = velocity[0] * velocity[0] + velocity[1] * velocity[1] + velocity[2] * velocity[2]
    base = 1.0 - 1.5 * square
    cache, result = {}, {}
    for w in set(weights[m] for m in members):
        cache[w] = scale * w
    for m in members:
        if m == 0:
            result[m] = cache[weights[0]] * base
            continue
        key = min(m, opposite[m])
        if ("pair", key) not in cache:
            along = None
            for d in range(3):
                step = lattice[key][d]
                if step:
                    term = velocity[d]
                    if along is None:
                        along = term if step == 1 else -term
                    else:
                        along = along + term if step == 1 else along - term
            cache[("pair", key)] = (base + 4.5 * along * along, 3.0 * along)
        even, odd = cache[("pair", key)]
        result[m] = cache[weights[m]] * (even + odd if m == key else even - odd)
    return result


def collide(f, solid):
    density, flows = moments(f)
    inverse = 1.0 / density
    velocity = [flow * inverse for flow in flows]
    feq = balance(relax_rate * density, velocity, range(19))
    post = [
        jnp.where(solid, f[opposite[m]], (1.0 - relax_rate) * f[m] + feq[m]) for m in range(19)
    ]
    return post, velocity


def edge_rows(side, ends):
    far, near = ends
    across = [m for m in GROUPS[0][side[0]] if lattice[m][1] == 1 - 2 * side[1]]
    along = [m for m in GROUPS[1][side[1]] if lattice[m][0] == 0]
    return [(across[0], far, 0), (across[0], near, 1)] + [(m, near, 0) for m in along]


def level_sums(view, line, row, last, rolled):
    parts = {}
    for cy in (0, 1, -1):
        members = [m for m in range(19) if lattice[m][0] == 0 and lattice[m][1] == cy]
        for weigh in (lambda m: 1, lambda m: lattice[m][2]):
            moved, edge = None, None
            for m in members:
                for which, value in ((0, view(m)), (1, line(m) if cy else None)):
                    if value is None or not weigh(m):
                        continue
                    if which == 0:
                        value = value if weigh(m) == 1 else -value
                        moved = value if moved is None else moved + value
                    else:
                        value = value if weigh(m) == 1 else -value
                        edge = value if edge is None else edge + value
            if cy:
                edge = 0.0 if edge is None else jnp.broadcast_to(edge, moved.shape)
                moved = jnp.where(row == (0 if cy == 1 else last), edge, rolled(moved, cy, 0))
            parts.setdefault(cy, []).append(moved)
    return (parts[0][0] + parts[1][0] + parts[-1][0], parts[1][0] - parts[-1][0],
            parts[0][1] + parts[1][1] + parts[-1][1])


def kernel(sizes, *refs):
    nz, ny, nx = sizes
    (pop_hbm, solid_hbm, ports_hbm, conc_hbm, load_hbm, out, new_conc, new_load,
     pops, solid, ports, conc, load, post0, post1, bound, speed, zpack, zrecv, xpack, xrecv, xside, xline,
     ypack, yrecv, ypack1, yrecv1, cpack, crecv, cpack1, crecv1, epack, erecv, erecv_far, xpack1, xrecv1,
     yline, yline1, sline, frame, pore, sxpack, sxrecv, sypack, syrecv, screcv, szpack, szrecv, fpack, epack_far, cend, near, wrapped,
     sent_v, all_v, vel, count_ref, load_sem, send_sem, recv_sem) = refs
    D, H, W = solid.shape
    T = D + 2
    ncy, ncx = conc.shape[2:]
    f32 = jnp.float32
    gz, gy, gx = lax.axis_index("gz"), lax.axis_index("gy"), lax.axis_index("gx")
    is_first, is_last = gz == 0, gz == nz - 1
    has_up, has_down = gz < nz - 1, gz > 0
    early = jnp.where(gz == 0, gx, 1) == 0
    late = jnp.where(gz == 0, gx, 1) > 0
    bound_at = len(FLAT) * T
    port_at = bound_at + 5
    solid_at = port_at + 2 + (port_at % 2)
    bound_at1 = len(FLAT) * D

    spans = [(0, 2), (D - 2, 2), (2, D - 4)]
    planes_in = [
        pltpu.make_async_copy(pop_hbm.at[:, pl.ds(a, n)], pops.at[:, pl.ds(a, n)], load_sem.at[i])
        for i, (a, n) in enumerate(spans)
    ]
    small = [
        pltpu.make_async_copy(a, b, load_sem.at[3 + i])
        for i, (a, b) in enumerate(
            ((solid_hbm, solid), (ports_hbm, ports), (conc_hbm, conc), (load_hbm, load)))
    ]
    small[0].start()
    planes_in[0].start()
    small[1].start()
    small[2].start()
    small[3].start()
    planes_in[1].start()
    planes_in[2].start()

    def at(offset):
        dz, dy, dx = offset
        return {"gz": gz + dz, "gy": lax.rem(gy + dy + ny, ny), "gx": lax.rem(gx + dx + nx, nx)}

    flat = [(0, dy, dx) for dx in [nx - 1] + list(range(nx - 1)) for dy in range(ny) if dy or dx]
    told = {(0, dy % ny, nx - 1) for dy in (0, 1, -1)} if nx > 2 else set()
    targets = sorted({(dy % ny, dx) for dy in (0, 1, -1) for dx in (0, 1)})
    barrier = pltpu.get_barrier_semaphore()

    def greet(offsets):
        for offset in offsets:
            pl.semaphore_signal(barrier, inc=1, device_id=at(offset), device_id_type=MESH)

    greet([(0, -dy, -dx) for _, dy, dx in flat if (0, dy, dx) not in told])

    @pl.when(has_up)
    def _():
        greet([(1, -dy, -dx) for dy, dx in targets])

    @pl.when(has_down)
    def _():
        greet([(-1, -dy, -dx) for dy, dx in targets])

    lane = lax.broadcasted_iota(jnp.int32, (H, W), 1)
    row = lax.broadcasted_iota(jnp.int32, (H, W), 0)
    pair = lax.div(lane, 2)
    first_mask = jnp.full((H, W), gz, jnp.int32) == 0
    last_mask = jnp.full((H, W), gz, jnp.int32) == nz - 1
    zero = jnp.zeros((H, W), f32)

    def rolled(x, step, axis):
        step = step % x.shape[axis]
        return pltpu.roll(x, step, axis) if step else x

    def put(acc, value, spot, shift):
        return jnp.where(lane == spot, rolled(value, shift, 1), acc)

    def put_pair(acc, value, half, shift):
        return jnp.where(pair == half, rolled(value, shift, 1), acc)

    def edge_row(value, s):
        return value[H - 1 :, :] if s == 0 else value[:1, :]

    FLAGS, Y, X, BELOW, ABOVE, BACK, VEL = range(7)
    SLAB, UP, DOWN, VEL_OUT = range(4)
    side_sets = [(pl.ds(0, 2), 1)] if ny == 2 else [(pl.ds(0, 1), 1), (pl.ds(1, 1), -1)]

    def remote(src, dst, offset, group):
        sent = {0: SLAB, 1: UP, -1: DOWN}[offset[0]]
        return pltpu.make_async_remote_copy(
            src_ref=src, dst_ref=dst, send_sem=send_sem.at[sent], recv_sem=recv_sem.at[group],
            device_id=at(offset), device_id_type=MESH)

    def arrived(sem, tiles):
        whole = count_ref.at[pl.ds(0, tiles)]
        pltpu.make_async_copy(whole, whole, sem).wait()

    def start(copies):
        for copy in copies:
            copy.start()

    along_z, first_z = {}, {}
    for dz, zs, group in ((1, 0, BELOW), (-1, 1, ABOVE)):
        first_z[dz] = [
            remote(szpack.at[zs], szrecv.at[zs], (dz, 0, 0), group),
            remote(cend, near.at[zs], (dz, 0, 0), group),
        ]
        along_z[dz] = [
            remote(zpack.at[zs], zrecv.at[zs], (dz, 0, 0), group),
            remote(fpack.at[zs], xside.at[zs], (dz, 0, 1), group),
        ]
        for i, (where, dy) in enumerate(side_sets):
            along_z[dz].append(remote(epack_far.at[zs], erecv_far.at[zs, i], (dz, dy, 1), group))
            along_z[dz].append(remote(epack.at[zs, where], erecv.at[zs, where], (dz, dy, 0), group))
    z_tiles = 1 + cend.shape[0] // H + zpack.shape[1] + 1 + len(side_sets) + 2
    flags = [remote(sxpack, sxrecv, (0, 0, 1), FLAGS)]
    for where, dy in side_sets:
        flags.append(remote(sypack.at[where], screcv.at[where], (0, dy, 1), FLAGS))
        flags.append(remote(sypack.at[where], syrecv.at[where], (0, dy, 0), FLAGS))
    slab = [remote(xpack, xrecv, (0, 0, 1), X)]
    back_c = []
    back = [remote(xpack1, xrecv1, (0, 0, -1), BACK)]
    for where, dy in side_sets:
        slab.append(remote(cpack.at[where], crecv.at[where], (0, dy, 1), Y))
        slab.append(remote(ypack.at[where], yrecv.at[where], (0, dy, 0), Y))
        back.append(remote(ypack1.at[where], yrecv1.at[where], (0, dy, 0), BACK))
        back_c.append(remote(cpack1.at[where], crecv1.at[where], (0, dy, -1), BACK))
    slab_tiles = 5 + 2 + 12 + 14

    edge_table = [
        [edge_rows((zs, s), ((D - 2, D - 1), (1, 0))[zs]) for s in range(2)] for zs in range(2)]

    for copy in small:
        copy.wait()
    cend[...] = jnp.zeros(cend.shape, f32)
    for s in range(2):
        cend[s * ncy : (s + 1) * ncy, 0:ncx] = conc[s, 0]
    szpack[0] = solid[D - 1].astype(f32)
    szpack[1] = solid[0].astype(f32)
    walls_out = zero
    for z in range(D):
        wall = solid[z].astype(f32)
        walls_out = put_pair(walls_out, wall, z, 2 * z + 2)
        for s in range(2):
            sypack[s, z : z + 1, :] = edge_row(wall, s)
    sxpack[...] = walls_out

    def shifted(value, lanes, fill=0.0):
        return jnp.where(lane < lanes, fill, rolled(value, lanes, 1)) if lanes else value

    def first_plane(z, packs):
        f = [pops[m, z] for m in range(19)]
        flag = solid[z]
        post, velocity = collide(f, flag == 1)
        for m in range(19):
            post0[z, m] = post[m]
        for zs, ends_at in ((0, (D - 1, D - 2)), (1, (0, 1))):
            if z in ends_at:
                base = 5 * ends_at.index(z)
                for j, m in enumerate(GROUPS[0][zs]):
                    zpack[zs, base + j] = post[m]
            if z == ends_at[0]:
                sums = level_sums(lambda m: shifted(post[m], 1 + lattice[m][2]), lambda m: None,
                                  row, H - 1, rolled)
                for d in range(3):
                    zpack[zs, 10 + d] = sums[d]
        for s in range(2):
            for i, m in enumerate(GROUPS[1][s]):
                ypack[s, i, z : z + 1, :] = edge_row(post[m], s)
        for zs in range(2):
            for s in range(2):
                for r, (m, source, _) in enumerate(edge_table[zs][s]):
                    if source == z:
                        epack[zs, s, r : r + 1, :] = edge_row(post[m], s)
        if z == 0:
            inflow = equilibrium_at_inlet()
            for j, m in enumerate(GROUPS[0][0]):
                bound[0, j] = jnp.where(ports[0] == 1, inflow[m], post[opposite[m]])
        if z == D - 1:
            outflow = balance(base_density, velocity, GROUPS[0][1])
            for j, m in enumerate(GROUPS[0][1]):
                leaving = jnp.where(ports[1] == 1, outflow[m], post[opposite[m]])
                bound[0, j] = jnp.where(last_mask, leaving, bound[0, j])
        twos, ones = packs
        for i, m in enumerate(GROUPS[2][0]):
            q = i * T + z + lattice[m][0] + 1
            twos = put_pair(twos, post[m], q, 2 * q + 2)
        for i, m in enumerate(FLAT):
            q = i * T + z + lattice[m][0] + 1
            ones = put(ones, post[m], q, q + 1)
        if z in (0, D - 1):
            q = solid_at // 2 + (0 if z == 0 else 1)
            ones = put_pair(ones, flag.astype(f32), q, 2 * q + 2)
        return twos, ones

    def enter():
        count = lambda flag: jnp.where(flag, len(targets), 0)
        pl.semaphore_wait(barrier, len(flat) - len(told) + count(has_up) + count(has_down))

    def send(copies_of):
        for dz, there in ((-1, has_down), (1, has_up)):
            if dz in copies_of:
                @pl.when(there)
                def _():
                    start(copies_of[dz])

    def pack_z(zs, packs):
        twos, ones = packs
        base = 0 if zs == 1 else D
        mine = lane < 0
        for i in range(5):
            mine = mine | ((pair >= i * T + base) & (pair < i * T + base + 2))
        fpack[zs] = jnp.where(mine, twos, rolled(ones, 4, 1))
        epack_far[zs] = jnp.where(lane >= W - 2, epack[zs, 0], rolled(epack[zs, 1], 2, 1))

    @pl.when(late)
    def _():
        enter()
        start(flags)
        send(first_z)

    packs = (zero, zero)
    planes_in[0].wait()
    for z in (0, 1):
        packs = first_plane(z, packs)
    pack_z(1, packs)

    @pl.when(late)
    def _():
        send({-1: along_z[-1]})

    planes_in[1].wait()
    for z in (D - 1, D - 2):
        packs = first_plane(z, packs)
    pack_z(0, packs)

    @pl.when(late)
    def _():
        send({1: along_z[1]})

    planes_in[2].wait()
    for z in range(2, D - 2):
        packs = first_plane(z, packs)
    twos, ones = packs
    for j in range(5):
        ones = put(ones, bound[0, j], bound_at + j, bound_at + j + 1)
    for j in range(2):
        ones = put(ones, ports[j].astype(f32), port_at + j, port_at + j + 1)
    xpack[0], xpack[1] = twos, ones
    for s in range(2):
        acc = zero
        for i in range(5):
            acc = put_pair(acc, ypack[s, i], i, 2 * i + 2)
        cpack[s] = acc

    @pl.when(early)
    def _():
        enter()
        start(flags)
        send(first_z)
        send({1: along_z[1]})

    start(slab)

    x_low, x_high = [], []
    for members, spot in ((GROUPS[2][0], pair), (FLAT, lane)):
        low, high = lane < 0, lane < 0
        for i, m in enumerate(members):
            cz = lattice[m][0]
            if cz >= 0:
                low = low | ((spot >= i * T) & (spot < i * T + 1 + cz))
            if cz <= 0:
                high = high | ((spot >= i * T + D + 1 + cz) & (spot < i * T + T))
        x_low.append(low)
        x_high.append(high)

    diffs = []
    wide = sent_v.shape[-1]
    parts = []
    for c in (1, 0, -1):
        voxel = lax.broadcasted_iota(jnp.int32, (W, wide), 0) + gx * W - 1 + c
        voxel = jnp.where(voxel < 0, voxel + nx * W, voxel)
        cell = lax.broadcasted_iota(jnp.int32, (W, wide), 1) * CELL
        parts.append(((voxel >= cell) & (voxel < cell + CELL)).astype(f32))
    pick = jnp.concatenate(parts, axis=0).astype(jnp.bfloat16)

    arrived(recv_sem.at[FLAGS], 5)
    for s in range(2):
        for n in range(3):
            tile, far = syrecv[s], screcv[s]
            sline[s, n] = shifted(tile, n, rolled(far, n, 1)) if n else tile
    for n in range(9):
        pore[0, n] = zero
        pore[D + 1, n] = zero
    for k in range(1, D + 1):
        walls = solid[k - 1].astype(f32)
        columns = sxrecv[...]
        one = shifted(walls, 1, rolled(columns, 1 - 2 * k, 1))
        two = shifted(walls, 2, rolled(columns, 2 - 2 * k, 1))
        frame[k] = one
        for n, view in enumerate((walls, one, two)):
            cx = 1 - n
            pore[k, TYPES.index((0, cx))] = 1.0 - view
            for cy in (1, -1):
                s = 1 if cy == 1 else 0
                line = sline[s, n, k - 1 : k, :]
                moved = jnp.where(row == (H - 1 if cy == 1 else 0),
                                  jnp.broadcast_to(line, (H, W)), rolled(view, -cy, 0))
                pore[k, TYPES.index((cy, cx))] = 1.0 - moved

    arrived(recv_sem.at[Y], 12)

    def filled(tile, columns, lanes, spot):
        return shifted(tile, lanes, rolled(columns, -(spot + 2 - lanes), 1)) if lanes else tile

    for s in range(2):
        corner = crecv[s]
        for i, m in enumerate(GROUPS[1][s]):
            cz, _, cx = lattice[m]
            yline[s, i, 1 + cz : 1 + cz + D, :] = filled(yrecv[s, i], corner, 1 + cx, 2 * i)

    def column_of(m, k):
        if lattice[m][2] == 1:
            return rolled(xline[0], -2 * (GROUPS[2][0].index(m) * T + k), 1)
        return rolled(xline[1], -(FLAT.index(m) * T + k), 1)

    def line_of(m, k):
        s = 0 if lattice[m][1] == 1 else 1
        return yline[s, GROUPS[1][s].index(m), k : k + 1, :]

    def stream(k, members):
        f = {}
        for m in members:
            cz, cy, cx = lattice[m]
            z = k - 1 - cz
            if 0 <= z < D:
                v = post0[z, m]
            else:
                zs = 0 if cz == 1 else 1
                v = zrecv[zs, GROUPS[0][zs].index(m) + (5 if z in (-2, D + 1) else 0)]
            if cx >= 0:
                v = shifted(v, 1 + cx, column_of(m, k))
            if cy:
                v = jnp.where(row == (0 if cy == 1 else H - 1),
                              jnp.broadcast_to(line_of(m, k), (H, W)), rolled(v, cy, 0))
            f[m] = v
        return f

    def port_view(j):
        return shifted(ports[j].astype(f32), 1, rolled(xline[1], -(port_at + j), 1)) > 0.5

    def bound_view(j):
        return shifted(bound[0, j], 1, rolled(xline[1], -(bound_at + j), 1))

    names = [("n", cy, cx) for cy, cx in TYPES if cy or cx]
    names += [("z", cy, cx) for cy, cx in TYPES if not (cy and cx)]

    def keep(k, post, carry):
        twos, ones, sums = carry
        for m, value in post.items():
            cz, cy, cx = lattice[m]
            post1[k, m] = value
            t = k - 1 + cz
            if not 0 <= t < D:
                continue
            if cy:
                s = 0 if cy == 1 else 1
                ypack1[s, GROUPS[1][s].index(m), t : t + 1, :] = edge_row(value, s)
            if cx == -1:
                q = GROUPS[2][1].index(m) * D + t
                twos = put_pair(twos, value, q, 2 * q)
            elif cx == 0:
                q = FLAT.index(m) * D + t
                ones = put(ones, value, q, q)
            if m:
                part = value * pore[k + cz, TYPES.index((cy, cx))]
                if cy or cx:
                    sums["n", cy, cx] = sums["n", cy, cx] + part
                if cz == 1:
                    sums["z", cy, cx] = sums["z", cy, cx] + part
                if cz == -1:
                    sums["z", cy, cx] = sums["z", cy, cx] - part
        return twos, ones, sums

    def inner_plane(k, carry):
        f = stream(k, range(19))
        if k == 1:
            for j, m in enumerate(GROUPS[0][0]):
                f[m] = jnp.where(first_mask, bound_view(j), f[m])
        if k == D:
            for j, m in enumerate(GROUPS[0][1]):
                f[m] = jnp.where(last_mask, bound_view(j), f[m])
        post, velocity = collide([f[m] for m in range(19)], frame[k] > 0.5)
        carry = keep(k, dict(enumerate(post)), carry)
        if k in (1, D):
            if k == 1:
                members, opened, mask = GROUPS[0][0], port_view(0), first_mask
                values = equilibrium_at_inlet()
            else:
                members, opened, mask = GROUPS[0][1], port_view(1), last_mask
                values = balance(base_density, velocity, members)
            extra = [zero, zero, zero]
            for j, m in enumerate(members):
                value = jnp.where(opened, values[m], post[opposite[m]])
                bound[1, j] = value if k == 1 else jnp.where(last_mask, value, bound[1, j])
                for d in range(3):
                    if lattice[m][d]:
                        extra[d] = extra[d] + value if lattice[m][d] == 1 else extra[d] - value
            for d in range(3):
                add = jnp.where(mask, extra[d] * pore[k, TYPES.index((0, 0))], 0.0)
                speed[d] = add if k == 1 else speed[d] + add
        return carry

    def outer_plane(k, carry):
        zs, mask = (0, first_mask) if k == 0 else (1, last_mask)
        members = GROUPS[0][zs]
        f = stream(k, GROUPS[0][0] + GROUPS[0][1])
        sums = level_sums(
            lambda m: jnp.where(lane < 1 + lattice[m][2], column_of(m, k), 0.0) if lattice[m][2] >= 0 else None,
            lambda m: line_of(m, k), row, H - 1, rolled)
        density, flow_y, flow_x = [zrecv[zs, 10 + d] + sums[d] for d in range(3)]
        flows = [None, flow_y, flow_x]
        for m, value in f.items():
            density = density + value
            for d in range(3):
                if lattice[m][d]:
                    signed = value if lattice[m][d] == 1 else -value
                    flows[d] = signed if flows[d] is None else flows[d] + signed
        inverse = 1.0 / density
        feq = balance(relax_rate * density, [flow * inverse for flow in flows], members)
        wall = frame[k] > 0.5
        post = {}
        for m in members:
            made = jnp.where(wall, f[opposite[m]], (1.0 - relax_rate) * f[m] + feq[m])
            post[m] = jnp.where(mask, 0.0, made)
        return keep(k, post, carry)

    arrived(recv_sem.at[X], 2)
    xline[0], xline[1] = xrecv[0], xrecv[1]
    carry = (zero, zero, {name: zero for name in names})
    for k in range(2, D):
        carry = inner_plane(k, carry)

    for zs, there, group in ((0, has_down, BELOW), (1, has_up, ABOVE)):
        @pl.when(there)
        def _():
            arrived(recv_sem.at[group], z_tiles)

        beside = xside[zs]
        move = -D if zs == 0 else D
        masks = x_low if zs == 0 else x_high
        xline[0] = jnp.where(masks[0], rolled(beside, 2 * move, 1), xline[0])
        xline[1] = jnp.where(masks[1], rolled(beside, move - 4, 1), xline[1])
        for s in range(2):
            tile = erecv[zs, s]
            far = erecv_far[zs, 0 if ny == 2 else s]
            if s == 1:
                far = rolled(far, -2, 1)
            views = [tile] + [shifted(tile, n, rolled(far, n, 1)) for n in (1, 2)]
            for r, (m, _, target) in enumerate(edge_table[zs][s]):
                k = target if zs == 0 else D + 1 - target
                yline[s, GROUPS[1][s].index(m), k : k + 1, :] = views[1 + lattice[m][2]][r : r + 1, :]
        k = 0 if zs == 0 else D + 1
        spot = solid_at + 4 + (3 if zs == 0 else 1)
        frame[k] = shifted(szrecv[zs], 1, rolled(beside, -spot, 1))
        carry = inner_plane(1 if zs == 0 else D, carry)
        carry = outer_plane(k, carry)

    twos, ones, sums = carry
    for j in range(5):
        ones = put(ones, bound[1, j], bound_at1 + j, bound_at1 + j)
    xpack1[0], xpack1[1] = twos, ones
    start(back)

    top, bottom = row == H - 1, row == 0
    blocks = []
    for cx in (1, 0, -1):
        own = [zero, zero, zero]
        up, down = [zero] * 3, [zero] * 3
        if ("n", 0, cx) in sums and cx:
            own[2] = sums["n", 0, cx] if cx == 1 else -sums["n", 0, cx]
        own[0] = sums["z", 0, cx]
        for cy, beyond, edge in ((1, up, top), (-1, down, bottom)):
            n = sums["n", cy, cx]
            values = [sums.get(("z", cy, cx)), n if cy == 1 else -n, {1: n, 0: None, -1: -n}[cx]]
            for d in range(3):
                if values[d] is not None:
                    own[d] = own[d] + jnp.where(edge, 0.0, values[d])
                    beyond[d] = values[d]
        if cx == 0:
            own = [own[d] + speed[d] for d in range(3)]
        totals = [jnp.sum(v, axis=0, keepdims=True) for v in own]
        ups = [v[H - 1 :, :] for v in up]
        downs = [v[:1, :] for v in down]
        if ny == 2:
            lines = totals + [a + b for a, b in zip(ups, downs)]
        else:
            lines = totals + ups + downs
        blocks.append(lines)
    tiles = []
    for base in range(0, sent_v.shape[0], H):
        here = []
        for lines in blocks:
            tile = zero
            for r, line in enumerate(lines[base : base + H]):
                tile = jnp.where(row == r, jnp.broadcast_to(line, (H, W)), tile)
            here.append(tile)
        tiles.append(jnp.concatenate(here, axis=1))

    def exact_pick(x):
        high = x.astype(jnp.bfloat16).astype(f32)
        mid = (x - high).astype(jnp.bfloat16).astype(f32)
        low = x - high - mid
        stacked = jnp.concatenate([high, mid, low], axis=0).astype(jnp.bfloat16)
        made = jnp.dot(stacked, pick, preferred_element_type=f32)
        return made[:H] + made[H : 2 * H] + made[2 * H :]

    for i, tile in enumerate(tiles):
        sent_v[i * H : (i + 1) * H, :] = exact_pick(tile) * (1.0 / (CELL * CELL * CELL * base_density))
    tell = [
        pltpu.make_async_remote_copy(
            src_ref=sent_v, dst_ref=all_v.at[gy, gx], send_sem=send_sem.at[VEL_OUT],
            recv_sem=recv_sem.at[VEL], device_id=at(offset), device_id_type=MESH)
        for offset in flat
    ]
    start(tell)
    all_v[gy, gx] = sent_v[...]
    for s in range(2):
        acc = zero
        for i, m in enumerate(GROUPS[1][s]):
            if lattice[m][2] <= 0:
                acc = put_pair(acc, ypack1[s, i], i, 2 * i)
        cpack1[s] = acc
    start(back_c)

    @pl.when(is_first)
    def _():
        for s in range(2):
            near[0, s * ncy : (s + 1) * ncy, :] = jnp.full((ncy, wide), feed_level[s], f32)

    @pl.when(is_last)
    def _():
        near[1] = cend[...]

    source = lax.broadcasted_iota(jnp.int32, (ncx, ncx), 0)
    target = lax.broadcasted_iota(jnp.int32, (ncx, ncx), 1)
    ahead = jnp.where(target == ncx - 1, 0, target + 1)
    behind = jnp.where(target == 0, ncx - 1, target - 1)
    take_after = (source == ahead).astype(f32)
    take_before = (source == behind).astype(f32)

    def exact_dot(a, b):
        return jnp.dot(a, b, precision=lax.Precision.HIGHEST, preferred_element_type=f32)

    for s in range(2):
        c = conc[s, 0]
        wrapped[s, 1 : ncy + 1, :] = c
        wrapped[s, 0:1, :] = conc[s, 0, ncy - 1 : ncy, :]
        wrapped[s, ncy + 1 : ncy + 2, :] = conc[s, 0, 0:1, :]
        pairs = [
            tuple(near[e, s * ncy : (s + 1) * ncy, 0:ncx] for e in range(2)),
            (wrapped[s, 0:ncy, :], wrapped[s, 2 : ncy + 2, :]),
            (exact_dot(c, take_before), exact_dot(c, take_after)),
        ]
        curvature = sum(b + a - 2.0 * c for b, a in pairs)
        rate = uptake_rate[s] * (affinity[s] * c - load[s, 0])
        new_load[s, 0] = load[s, 0] + rate
        diffs.append((c - phase_ratio * rate + spread_base[s] * curvature, curvature,
                      [(c - b, a - c) for b, a in pairs]))

    arrived(recv_sem.at[BACK], 14)

    def emptied(tile, lanes, columns):
        return jnp.where(lane >= W - lanes, columns, rolled(tile, -lanes, 1)) if lanes else tile

    for s in range(2):
        corner = crecv1[s]
        for i, m in enumerate(GROUPS[1][s]):
            lanes = 1 - lattice[m][2]
            yline1[s, i] = emptied(yrecv1[s, i], lanes, rolled(corner, -lanes - 2 * i, 1))

    for t in range(D):
        for m in range(19):
            cz, cy, cx = lattice[m]
            v = post1[t + 1 - cz, m]
            if cx == -1:
                spot = 2 * (GROUPS[2][1].index(m) * D + t)
                v = emptied(v, 2, rolled(xrecv1[0], -2 - spot, 1))
            elif cx == 0:
                v = emptied(v, 1, rolled(xrecv1[1], -1 - (FLAT.index(m) * D + t), 1))
            if cy:
                s = 0 if cy == 1 else 1
                line = yline1[s, GROUPS[1][s].index(m), t : t + 1, :]
                v = jnp.where(row == (0 if s == 0 else H - 1),
                              jnp.broadcast_to(line, (H, W)), rolled(v, cy, 0))
            if (t == 0 and cz == 1) or (t == D - 1 and cz == -1):
                j = GROUPS[0][0 if cz == 1 else 1].index(m)
                kept = emptied(bound[1, j], 1, rolled(xrecv1[1], -1 - (bound_at1 + j), 1))
                v = jnp.where(first_mask if cz == 1 else last_mask, kept, v)
            out[m, t] = v

    arrived(send_sem.at[SLAB], slab_tiles)
    for sem, there in ((UP, has_up), (DOWN, has_down)):
        @pl.when(there)
        def _():
            arrived(send_sem.at[sem], z_tiles)
    vel_tiles = len(flat) * (sent_v.shape[0] // H)
    arrived(recv_sem.at[VEL], vel_tiles)
    totals = []
    for y in range(ny):
        total = all_v[y, 0]
        for x in range(1, nx):
            total = total + all_v[y, x]
        totals.append(total)
    for y in range(ny):
        for d in range(3):
            own = totals[y][d : d + 1]
            if ny == 2:
                own = own + totals[1 - y][3 + d : 4 + d]
            else:
                own = own + totals[(y - 1) % ny][3 + d : 4 + d] + totals[(y + 1) % ny][6 + d : 7 + d]
            vel[d, y : y + 1, :] = own
    courant = [CELL * vel[d][:, :ncx] for d in range(3)]
    reach = jnp.abs(courant[0]) + jnp.abs(courant[1]) + jnp.abs(courant[2])
    for s in range(2):
        value, curvature, steps = diffs[s]
        for d in range(3):
            low, high = steps[d]
            value = value - jnp.maximum(courant[d], 0.0) * low - jnp.minimum(courant[d], 0.0) * high
        new_conc[s, 0] = value + spread_length * reach * curvature
    arrived(send_sem.at[VEL_OUT], vel_tiles)


def hand_out(*refs):
    copies = [pltpu.make_async_copy(refs[i], refs[3 + i], refs[6].at[i]) for i in range(3)]
    for copy in copies:
        copy.start()
    for copy in copies:
        copy.wait()


def equilibrium_at_inlet():
    result = {}
    for m in GROUPS[0][0]:
        along = inlet_speed
        result[m] = weights[m] * base_density * (
            1.0 + 3.0 * along + 4.5 * along * along - 1.5 * inlet_speed * inlet_speed)
    return result


def solution(mesh):
    sizes = tuple(mesh.shape[a] for a in ("gz", "gy", "gx"))
    nz, ny, nx = sizes

    def body(populations, solid, ports, concentration, loaded):
        D, H, W = solid.shape
        ncy, ncx = concentration.shape[2:]
        assert D == CELL and H == CELL and W % 128 == 0 and 12 * (D + 2) <= W
        wide = -(-ncx // 128) * 128
        assert nz > 1 and ny > 1 and nx > 1 and W == wide
        f32 = jnp.float32
        tile = (H, W)
        rows = H if ny == 2 else 2 * H
        ends = -(-2 * ncy // H) * H
        anywhere = pl.BlockSpec(memory_space=pl.ANY)
        inside = pl.BlockSpec(memory_space=pltpu.VMEM)
        results = (populations, concentration, loaded)
        made = pl.pallas_call(
            functools.partial(kernel, sizes),
            out_shape=tuple(pltpu.VMEM(a.shape, f32) for a in results),
            in_specs=[anywhere] * 5,
            out_specs=(inside,) * 3,
            scratch_shapes=[
                pltpu.VMEM(populations.shape, f32),
                pltpu.VMEM(solid.shape, jnp.int32),
                pltpu.VMEM(ports.shape, jnp.int32),
                pltpu.VMEM(concentration.shape, f32),
                pltpu.VMEM(loaded.shape, f32),
                pltpu.VMEM((D, 19) + tile, f32),
                pltpu.VMEM((D + 2, 19) + tile, f32),
                pltpu.VMEM((2, 5) + tile, f32),
                pltpu.VMEM((3,) + tile, f32),
                pltpu.VMEM((2, 13) + tile, f32),
                pltpu.VMEM((2, 13) + tile, f32),
                pltpu.VMEM((2,) + tile, f32),
                pltpu.VMEM((2,) + tile, f32),
                pltpu.VMEM((2,) + tile, f32),
                pltpu.VMEM((2,) + tile, f32),
                pltpu.VMEM((2, 5, D, W), f32),
                pltpu.VMEM((2, 5, D, W), f32),
                pltpu.VMEM((2, 5, D, W), f32),
                pltpu.VMEM((2, 5, D, W), f32),
                pltpu.VMEM((2, D, W), f32),
                pltpu.VMEM((2, D, W), f32),
                pltpu.VMEM((2, D, W), f32),
                pltpu.VMEM((2, D, W), f32),
                pltpu.VMEM((2, 2) + tile, f32),
                pltpu.VMEM((2, 2) + tile, f32),
                pltpu.VMEM((2, 2) + tile, f32),
                pltpu.VMEM((2,) + tile, f32),
                pltpu.VMEM((2,) + tile, f32),
                pltpu.VMEM((2, 5, 2 * H, W), f32),
                pltpu.VMEM((2, 5, D, W), f32),
                pltpu.VMEM((2, 3, D, W), f32),
                pltpu.VMEM((D + 2,) + tile, f32),
                pltpu.VMEM((D + 2, 9) + tile, f32),
                pltpu.VMEM(tile, f32),
                pltpu.VMEM(tile, f32),
                pltpu.VMEM((2, D, W), f32),
                pltpu.VMEM((2, D, W), f32),
                pltpu.VMEM((2, D, W), f32),
                pltpu.VMEM((2,) + tile, f32),
                pltpu.VMEM((2,) + tile, f32),
                pltpu.VMEM((2,) + tile, f32),
                pltpu.VMEM((2,) + tile, f32),
                pltpu.VMEM((ends, wide), f32),
                pltpu.VMEM((2, ends, wide), f32),
                pltpu.VMEM((2, ncy + 2, ncx), f32),
                pltpu.VMEM((rows, wide), f32),
                pltpu.VMEM((ny, nx, rows, wide), f32),
                pltpu.VMEM((3, ncy, wide), f32),
                pltpu.VMEM((max(40, 2 * ny * nx),) + tile, f32),
                pltpu.SemaphoreType.DMA((7,)),
                pltpu.SemaphoreType.DMA((4,)),
                pltpu.SemaphoreType.DMA((7,)),
            ],
            compiler_params=pltpu.CompilerParams(collective_id=0, has_side_effects=True),
        )(populations, solid, ports, concentration, loaded)
        return pl.pallas_call(
            hand_out,
            out_shape=tuple(jax.ShapeDtypeStruct(a.shape, f32) for a in results),
            in_specs=[inside] * 3,
            out_specs=(anywhere,) * 3,
            scratch_shapes=[pltpu.SemaphoreType.DMA((3,))],
        )(*[pltpu.with_memory_space_constraint(a, pltpu.VMEM) for a in made])

    placed = (
        P(None, "gz", "gy", "gx"),
        P("gz", "gy", "gx"),
        P(None, "gy", "gx"),
        P(None, "gz", None, None),
        P(None, "gz", None, None),
    )
    return jax.shard_map(
        body,
        mesh=mesh,
        in_specs=placed,
        out_specs=(P(None, "gz", "gy", "gx"), P(None, "gz", None, None), P(None, "gz", None, None)),
        check_vma=False,
    )
```

```python
import functools

import jax
import jax.numpy as jnp
from jax import lax
from jax.experimental import pallas as pl
from jax.experimental.pallas import tpu as pltpu
from jax.sharding import PartitionSpec as P

ITERS = 2
CELL = 8
MESH = pl.DeviceIdType.MESH

lattice = [
    (0, 0, 0),
    (1, 0, 0),
    (-1, 0, 0),
    (0, 1, 0),
    (0, -1, 0),
    (0, 0, 1),
    (0, 0, -1),
    (1, 1, 0),
    (-1, -1, 0),
    (1, -1, 0),
    (-1, 1, 0),
    (1, 0, 1),
    (-1, 0, -1),
    (1, 0, -1),
    (-1, 0, 1),
    (0, 1, 1),
    (0, -1, -1),
    (0, 1, -1),
    (0, -1, 1),
]
opposite = [0, 2, 1, 4, 3, 6, 5, 8, 7, 10, 9, 12, 11, 14, 13, 16, 15, 18, 17]
weights = [1.0 / 3.0] + [1.0 / 18.0] * 6 + [1.0 / 36.0] * 12
relax_rate = 1.25
base_density = 36.0
inlet_speed = 0.05
spread_base = (0.03, 0.06)
spread_length = 0.1
uptake_rate = (0.3, 0.6)
affinity = (2.0, 0.5)
phase_ratio = 0.5
feed_level = (1.0, 0.5)

GROUPS = [[[m for m in range(19) if lattice[m][d] == s] for s in (1, -1)] for d in range(3)]
FLAT = [m for m in range(19) if lattice[m][2] == 0]
SOLID = 14
ORDER = GROUPS[0][0] + [m for m in range(19) if lattice[m][0] == 0] + [None] + GROUPS[0][1]
SLOT = {m: i for i, m in enumerate(ORDER) if m is not None}
TYPES = [(cy, cx) for cy in (1, 0, -1) for cx in (1, 0, -1)]


def moments(f):
    density = f[0]
    for member in range(1, 19):
        density = density + f[member]
    return density, momentum(f)


def momentum(f):
    flows = []
    for d in range(3):
        total = None
        for a, b in zip(GROUPS[d][0], [opposite[m] for m in GROUPS[d][0]]):
            part = f[a] - f[b]
            total = part if total is None else total + part
        flows.append(total)
    return flows


def balance(scale, velocity, members):
    square = velocity[0] * velocity[0] + velocity[1] * velocity[1] + velocity[2] * velocity[2]
    base = 1.0 - 1.5 * square
    cache, result = {}, {}
    for w in set(weights[m] for m in members):
        cache[w] = scale * w
    for m in members:
        if m == 0:
            result[m] = cache[weights[0]] * base
            continue
        key = min(m, opposite[m])
        if ("pair", key) not in cache:
            along = None
            for d in range(3):
                step = lattice[key][d]
                if step:
                    term = velocity[d]
                    if along is None:
                        along = term if step == 1 else -term
                    else:
                        along = along + term if step == 1 else along - term
            cache[("pair", key)] = (base + 4.5 * along * along, 3.0 * along)
        even, odd = cache[("pair", key)]
        result[m] = cache[weights[m]] * (even + odd if m == key else even - odd)
    return result


def collide(f, solid):
    density, flows = moments(f)
    inverse = 1.0 / density
    velocity = [flow * inverse for flow in flows]
    feq = balance(relax_rate * density, velocity, range(19))
    post = [
        jnp.where(solid, f[opposite[m]], (1.0 - relax_rate) * f[m] + feq[m]) for m in range(19)
    ]
    return post, velocity


def edge_rows(side, ends):
    far, near = ends
    across = [m for m in GROUPS[0][side[0]] if lattice[m][1] == 1 - 2 * side[1]]
    along = [m for m in GROUPS[1][side[1]] if lattice[m][0] == 0]
    return [(across[0], far, 0), (across[0], near, 1)] + [(m, near, 0) for m in along]


def level_sums(view, line, row, last, rolled):
    parts = {}
    for cy in (0, 1, -1):
        members = [m for m in range(19) if lattice[m][0] == 0 and lattice[m][1] == cy]
        for weigh in (lambda m: 1, lambda m: lattice[m][2]):
            moved, edge = None, None
            for m in members:
                for which, value in ((0, view(m)), (1, line(m) if cy else None)):
                    if value is None or not weigh(m):
                        continue
                    if which == 0:
                        value = value if weigh(m) == 1 else -value
                        moved = value if moved is None else moved + value
                    else:
                        value = value if weigh(m) == 1 else -value
                        edge = value if edge is None else edge + value
            if cy:
                edge = 0.0 if edge is None else jnp.broadcast_to(edge, moved.shape)
                moved = jnp.where(row == (0 if cy == 1 else last), edge, rolled(moved, cy, 0))
            parts.setdefault(cy, []).append(moved)
    return (parts[0][0] + parts[1][0] + parts[-1][0], parts[1][0] - parts[-1][0],
            parts[0][1] + parts[1][1] + parts[-1][1])


def kernel(sizes, *refs):
    nz, ny, nx = sizes
    (pop_hbm, solid_hbm, ports_hbm, conc_hbm, load_hbm, out, new_conc, new_load,
     pops, solid, ports, conc, load, post0, post1, bound, speed, zpack, zrecv, xpack, xrecv, xside, xline,
     ypack, yrecv, ypack1, yrecv1, cpack, crecv, cpack1, crecv1, epack, erecv, erecv_far, xpack1, xrecv1,
     yline, yline1, sline, frame, pore, sxpack, sxrecv, sypack, syrecv, screcv, szpack, szrecv, fpack, epack_far, cend, near, wrapped,
     sent_v, all_v, vel, count_ref, load_sem, send_sem, recv_sem) = refs
    D, H, W = solid.shape
    T = D + 2
    ncy, ncx = conc.shape[2:]
    f32 = jnp.float32
    gz, gy, gx = lax.axis_index("gz"), lax.axis_index("gy"), lax.axis_index("gx")
    is_first, is_last = gz == 0, gz == nz - 1
    has_up, has_down = gz < nz - 1, gz > 0
    early = jnp.where(gz == 0, gx, 1) == 0
    late = jnp.where(gz == 0, gx, 1) > 0
    bound_at = len(FLAT) * T
    port_at = bound_at + 5
    solid_at = port_at + 2 + (port_at % 2)
    bound_at1 = len(FLAT) * D

    spans = [(0, 2), (D - 2, 2), (2, D - 4)]
    planes_in = [
        pltpu.make_async_copy(pop_hbm.at[:, pl.ds(a, n)], pops.at[:, pl.ds(a, n)], load_sem.at[i])
        for i, (a, n) in enumerate(spans)
    ]
    small = [
        pltpu.make_async_copy(a, b, load_sem.at[3 + i])
        for i, (a, b) in enumerate(
            ((solid_hbm, solid), (ports_hbm, ports), (conc_hbm, conc), (load_hbm, load)))
    ]
    def at(offset):
        dz, dy, dx = offset
        return {"gz": gz + dz, "gy": lax.rem(gy + dy + ny, ny), "gx": lax.rem(gx + dx + nx, nx)}

    flat = [(0, dy, dx) for dx in list(range(1, nx)) + [0] for dy in range(ny) if dy or dx]
    told = {(0, dy % ny, nx - 1) for dy in (0, 1, -1)} if nx > 2 else set()
    targets = sorted({(dy % ny, dx) for dy in (0, 1, -1) for dx in (0, 1)})
    barrier = pltpu.get_barrier_semaphore()

    def greet(offsets):
        for offset in offsets:
            pl.semaphore_signal(barrier, inc=1, device_id=at(offset), device_id_type=MESH)

    @pl.when(has_down)
    def _():
        greet([(-1, -dy, -dx) for dy, dx in targets])

    @pl.when(has_up)
    def _():
        greet([(1, -dy, -dx) for dy, dx in targets])

    greet([(0, -dy, -dx) for _, dy, dx in flat if (0, dy, dx) not in told])

    small[0].start()
    planes_in[0].start()
    small[1].start()
    small[2].start()
    small[3].start()
    planes_in[1].start()
    planes_in[2].start()

    lane = lax.broadcasted_iota(jnp.int32, (H, W), 1)
    row = lax.broadcasted_iota(jnp.int32, (H, W), 0)
    pair = lax.div(lane, 2)
    first_mask = jnp.full((H, W), gz, jnp.int32) == 0
    last_mask = jnp.full((H, W), gz, jnp.int32) == nz - 1
    zero = jnp.zeros((H, W), f32)

    def rolled(x, step, axis):
        step = step % x.shape[axis]
        return pltpu.roll(x, step, axis) if step else x

    def put(acc, value, spot, shift):
        return jnp.where(lane == spot, rolled(value, shift, 1), acc)

    def put_pair(acc, value, half, shift):
        return jnp.where(pair == half, rolled(value, shift, 1), acc)

    def edge_row(value, s):
        return value[H - 1 :, :] if s == 0 else value[:1, :]

    FLAGS, Y, X, BELOW, ABOVE, BACK, VEL = range(7)
    SLAB, UP, DOWN, VEL_OUT = range(4)
    side_sets = [(pl.ds(0, 2), 1)] if ny == 2 else [(pl.ds(0, 1), 1), (pl.ds(1, 1), -1)]

    def remote(src, dst, offset, group):
        sent = {0: SLAB, 1: UP, -1: DOWN}[offset[0]]
        return pltpu.make_async_remote_copy(
            src_ref=src, dst_ref=dst, send_sem=send_sem.at[sent], recv_sem=recv_sem.at[group],
            device_id=at(offset), device_id_type=MESH)

    def arrived(sem, tiles):
        whole = count_ref.at[pl.ds(0, tiles)]
        pltpu.make_async_copy(whole, whole, sem).wait()

    def start(copies):
        for copy in copies:
            copy.start()

    along_z, first_z = {}, {}
    for dz, zs, group in ((1, 0, BELOW), (-1, 1, ABOVE)):
        first_z[dz] = [
            remote(szpack.at[zs], szrecv.at[zs], (dz, 0, 0), group),
            remote(cend, near.at[zs], (dz, 0, 0), group),
        ]
        along_z[dz] = [
            remote(zpack.at[zs], zrecv.at[zs], (dz, 0, 0), group),
            remote(fpack.at[zs], xside.at[zs], (dz, 0, 1), group),
        ]
        for i, (where, dy) in enumerate(side_sets):
            along_z[dz].append(remote(epack_far.at[zs], erecv_far.at[zs, i], (dz, dy, 1), group))
            along_z[dz].append(remote(epack.at[zs, where], erecv.at[zs, where], (dz, dy, 0), group))
    z_tiles = 1 + cend.shape[0] // H + zpack.shape[1] + 1 + len(side_sets) + 2
    flags = [remote(sxpack, sxrecv, (0, 0, 1), FLAGS)]
    for where, dy in side_sets:
        flags.append(remote(sypack.at[where], screcv.at[where], (0, dy, 1), FLAGS))
        flags.append(remote(sypack.at[where], syrecv.at[where], (0, dy, 0), FLAGS))
    slab = [remote(xpack, xrecv, (0, 0, 1), X)]
    back_c = []
    back = [remote(xpack1, xrecv1, (0, 0, -1), BACK)]
    for where, dy in side_sets:
        slab.append(remote(cpack.at[where], crecv.at[where], (0, dy, 1), Y))
        slab.append(remote(ypack.at[where], yrecv.at[where], (0, dy, 0), Y))
        back.append(remote(ypack1.at[where], yrecv1.at[where], (0, dy, 0), BACK))
        back_c.append(remote(cpack1.at[where], crecv1.at[where], (0, dy, -1), BACK))
    slab_tiles = 5 + 2 + 12 + 14

    edge_table = [
        [edge_rows((zs, s), ((D - 2, D - 1), (1, 0))[zs]) for s in range(2)] for zs in range(2)]

    for copy in small:
        copy.wait()
    cend[...] = jnp.zeros(cend.shape, f32)
    for s in range(2):
        cend[s * ncy : (s + 1) * ncy, 0:ncx] = conc[s, 0]
    szpack[0] = solid[D - 1].astype(f32)
    szpack[1] = solid[0].astype(f32)
    walls_out = zero
    for z in range(D):
        wall = solid[z].astype(f32)
        walls_out = put_pair(walls_out, wall, z, 2 * z + 2)
        for s in range(2):
            sypack[s, z : z + 1, :] = edge_row(wall, s)
    sxpack[...] = walls_out

    def shifted(value, lanes, fill=0.0):
        return jnp.where(lane < lanes, fill, rolled(value, lanes, 1)) if lanes else value

    def first_plane(z, packs):
        f = [pops[m, z] for m in range(19)]
        flag = solid[z]
        post, velocity = collide(f, flag == 1)
        for m in range(19):
            post0[z, m] = post[m]
        for zs, ends_at in ((0, (D - 1, D - 2)), (1, (0, 1))):
            if z in ends_at:
                base = 5 * ends_at.index(z)
                for j, m in enumerate(GROUPS[0][zs]):
                    zpack[zs, base + j] = post[m]
            if z == ends_at[0]:
                sums = level_sums(lambda m: shifted(post[m], 1 + lattice[m][2]), lambda m: None,
                                  row, H - 1, rolled)
                for d in range(3):
                    zpack[zs, 10 + d] = sums[d]
        for s in range(2):
            for i, m in enumerate(GROUPS[1][s]):
                ypack[s, i, z : z + 1, :] = edge_row(post[m], s)
        for zs in range(2):
            for s in range(2):
                for r, (m, source, _) in enumerate(edge_table[zs][s]):
                    if source == z:
                        epack[zs, s, r : r + 1, :] = edge_row(post[m], s)
        if z == 0:
            inflow = equilibrium_at_inlet()
            for j, m in enumerate(GROUPS[0][0]):
                bound[0, j] = jnp.where(ports[0] == 1, inflow[m], post[opposite[m]])
        if z == D - 1:
            outflow = balance(base_density, velocity, GROUPS[0][1])
            for j, m in enumerate(GROUPS[0][1]):
                leaving = jnp.where(ports[1] == 1, outflow[m], post[opposite[m]])
                bound[0, j] = jnp.where(last_mask, leaving, bound[0, j])
        twos, ones = packs
        for i, m in enumerate(GROUPS[2][0]):
            q = i * T + z + lattice[m][0] + 1
            twos = put_pair(twos, post[m], q, 2 * q + 2)
        for i, m in enumerate(FLAT):
            q = i * T + z + lattice[m][0] + 1
            ones = put(ones, post[m], q, q + 1)
        if z in (0, D - 1):
            q = solid_at // 2 + (0 if z == 0 else 1)
            ones = put_pair(ones, flag.astype(f32), q, 2 * q + 2)
        return twos, ones

    def enter():
        count = lambda flag: jnp.where(flag, len(targets), 0)
        pl.semaphore_wait(barrier, len(flat) - len(told) + count(has_up) + count(has_down))

    def send(copies_of):
        for dz, there in ((-1, has_down), (1, has_up)):
            if dz in copies_of:
                @pl.when(there)
                def _():
                    start(copies_of[dz])

    def pack_z(zs, packs):
        twos, ones = packs
        base = 0 if zs == 1 else D
        mine = lane < 0
        for i in range(5):
            mine = mine | ((pair >= i * T + base) & (pair < i * T + base + 2))
        fpack[zs] = jnp.where(mine, twos, rolled(ones, 4, 1))
        epack_far[zs] = jnp.where(lane >= W - 2, epack[zs, 0], rolled(epack[zs, 1], 2, 1))

    packs = (zero, zero)
    planes_in[0].wait()
    for z in (0, 1):
        packs = first_plane(z, packs)
    pack_z(1, packs)

    @pl.when(late)
    def _():
        enter()
        start(flags)
        send(first_z)

    @pl.when(late)
    def _():
        send({-1: along_z[-1]})

    planes_in[1].wait()
    for z in (D - 1, D - 2):
        packs = first_plane(z, packs)
    pack_z(0, packs)

    @pl.when(late)
    def _():
        send({1: along_z[1]})

    planes_in[2].wait()
    for z in range(2, D - 2):
        packs = first_plane(z, packs)
    twos, ones = packs
    for j in range(5):
        ones = put(ones, bound[0, j], bound_at + j, bound_at + j + 1)
    for j in range(2):
        ones = put(ones, ports[j].astype(f32), port_at + j, port_at + j + 1)
    xpack[0], xpack[1] = twos, ones
    for s in range(2):
        acc = zero
        for i in range(5):
            acc = put_pair(acc, ypack[s, i], i, 2 * i + 2)
        cpack[s] = acc

    @pl.when(early)
    def _():
        enter()
        start(flags)
        send(first_z)
        send({1: along_z[1]})

    start(slab)

    x_low, x_high = [], []
    for members, spot in ((GROUPS[2][0], pair), (FLAT, lane)):
        low, high = lane < 0, lane < 0
        for i, m in enumerate(members):
            cz = lattice[m][0]
            if cz >= 0:
                low = low | ((spot >= i * T) & (spot < i * T + 1 + cz))
            if cz <= 0:
                high = high | ((spot >= i * T + D + 1 + cz) & (spot < i * T + T))
        x_low.append(low)
        x_high.append(high)

    diffs = []
    wide = sent_v.shape[-1]
    parts = []
    for c in (1, 0, -1):
        voxel = lax.broadcasted_iota(jnp.int32, (W, wide), 0) + gx * W - 1 + c
        voxel = jnp.where(voxel < 0, voxel + nx * W, voxel)
        cell = lax.broadcasted_iota(jnp.int32, (W, wide), 1) * CELL
        parts.append(((voxel >= cell) & (voxel < cell + CELL)).astype(f32))
    pick = jnp.concatenate(parts, axis=0).astype(jnp.bfloat16)

    arrived(recv_sem.at[FLAGS], 5)
    for s in range(2):
        for n in range(3):
            tile, far = syrecv[s], screcv[s]
            sline[s, n] = shifted(tile, n, rolled(far, n, 1)) if n else tile
    for n in range(9):
        pore[0, n] = zero
        pore[D + 1, n] = zero
    for k in range(1, D + 1):
        walls = solid[k - 1].astype(f32)
        columns = sxrecv[...]
        one = shifted(walls, 1, rolled(columns, 1 - 2 * k, 1))
        two = shifted(walls, 2, rolled(columns, 2 - 2 * k, 1))
        frame[k] = one
        for n, view in enumerate((walls, one, two)):
            cx = 1 - n
            pore[k, TYPES.index((0, cx))] = 1.0 - view
            for cy in (1, -1):
                s = 1 if cy == 1 else 0
                line = sline[s, n, k - 1 : k, :]
                moved = jnp.where(row == (H - 1 if cy == 1 else 0),
                                  jnp.broadcast_to(line, (H, W)), rolled(view, -cy, 0))
                pore[k, TYPES.index((cy, cx))] = 1.0 - moved

    arrived(recv_sem.at[Y], 12)

    def filled(tile, columns, lanes, spot):
        return shifted(tile, lanes, rolled(columns, -(spot + 2 - lanes), 1)) if lanes else tile

    for s in range(2):
        corner = crecv[s]
        for i, m in enumerate(GROUPS[1][s]):
            cz, _, cx = lattice[m]
            yline[s, i, 1 + cz : 1 + cz + D, :] = filled(yrecv[s, i], corner, 1 + cx, 2 * i)

    def column_of(m, k):
        if lattice[m][2] == 1:
            return rolled(xline[0], -2 * (GROUPS[2][0].index(m) * T + k), 1)
        return rolled(xline[1], -(FLAT.index(m) * T + k), 1)

    def line_of(m, k):
        s = 0 if lattice[m][1] == 1 else 1
        return yline[s, GROUPS[1][s].index(m), k : k + 1, :]

    def stream(k, members):
        f = {}
        for m in members:
            cz, cy, cx = lattice[m]
            z = k - 1 - cz
            if 0 <= z < D:
                v = post0[z, m]
            else:
                zs = 0 if cz == 1 else 1
                v = zrecv[zs, GROUPS[0][zs].index(m) + (5 if z in (-2, D + 1) else 0)]
            if cx >= 0:
                v = shifted(v, 1 + cx, column_of(m, k))
            if cy:
                v = jnp.where(row == (0 if cy == 1 else H - 1),
                              jnp.broadcast_to(line_of(m, k), (H, W)), rolled(v, cy, 0))
            f[m] = v
        return f

    def port_view(j):
        return shifted(ports[j].astype(f32), 1, rolled(xline[1], -(port_at + j), 1)) > 0.5

    def bound_view(j):
        return shifted(bound[0, j], 1, rolled(xline[1], -(bound_at + j), 1))

    names = [("n", cy, cx) for cy, cx in TYPES if cy or cx]
    names += [("z", cy, cx) for cy, cx in TYPES if not (cy and cx)]

    def keep(k, post, carry):
        twos, ones, sums = carry
        for m, value in post.items():
            cz, cy, cx = lattice[m]
            post1[k, m] = value
            t = k - 1 + cz
            if not 0 <= t < D:
                continue
            if cy:
                s = 0 if cy == 1 else 1
                ypack1[s, GROUPS[1][s].index(m), t : t + 1, :] = edge_row(value, s)
            if cx == -1:
                q = GROUPS[2][1].index(m) * D + t
                twos = put_pair(twos, value, q, 2 * q)
            elif cx == 0:
                q = FLAT.index(m) * D + t
                ones = put(ones, value, q, q)
            if m:
                part = value * pore[k + cz, TYPES.index((cy, cx))]
                if cy or cx:
                    sums["n", cy, cx] = sums["n", cy, cx] + part
                if cz == 1:
                    sums["z", cy, cx] = sums["z", cy, cx] + part
                if cz == -1:
                    sums["z", cy, cx] = sums["z", cy, cx] - part
        return twos, ones, sums

    def inner_plane(k, carry):
        f = stream(k, range(19))
        if k == 1:
            for j, m in enumerate(GROUPS[0][0]):
                f[m] = jnp.where(first_mask, bound_view(j), f[m])
        if k == D:
            for j, m in enumerate(GROUPS[0][1]):
                f[m] = jnp.where(last_mask, bound_view(j), f[m])
        post, velocity = collide([f[m] for m in range(19)], frame[k] > 0.5)
        carry = keep(k, dict(enumerate(post)), carry)
        if k in (1, D):
            if k == 1:
                members, opened, mask = GROUPS[0][0], port_view(0), first_mask
                values = equilibrium_at_inlet()
            else:
                members, opened, mask = GROUPS[0][1], port_view(1), last_mask
                values = balance(base_density, velocity, members)
            extra = [zero, zero, zero]
            for j, m in enumerate(members):
                value = jnp.where(opened, values[m], post[opposite[m]])
                bound[1, j] = value if k == 1 else jnp.where(last_mask, value, bound[1, j])
                for d in range(3):
                    if lattice[m][d]:
                        extra[d] = extra[d] + value if lattice[m][d] == 1 else extra[d] - value
            for d in range(3):
                add = jnp.where(mask, extra[d] * pore[k, TYPES.index((0, 0))], 0.0)
                speed[d] = add if k == 1 else speed[d] + add
        return carry

    def outer_plane(k, carry):
        zs, mask = (0, first_mask) if k == 0 else (1, last_mask)
        members = GROUPS[0][zs]
        f = stream(k, GROUPS[0][0] + GROUPS[0][1])
        sums = level_sums(
            lambda m: jnp.where(lane < 1 + lattice[m][2], column_of(m, k), 0.0) if lattice[m][2] >= 0 else None,
            lambda m: line_of(m, k), row, H - 1, rolled)
        density, flow_y, flow_x = [zrecv[zs, 10 + d] + sums[d] for d in range(3)]
        flows = [None, flow_y, flow_x]
        for m, value in f.items():
            density = density + value
            for d in range(3):
                if lattice[m][d]:
                    signed = value if lattice[m][d] == 1 else -value
                    flows[d] = signed if flows[d] is None else flows[d] + signed
        inverse = 1.0 / density
        feq = balance(relax_rate * density, [flow * inverse for flow in flows], members)
        wall = frame[k] > 0.5
        post = {}
        for m in members:
            made = jnp.where(wall, f[opposite[m]], (1.0 - relax_rate) * f[m] + feq[m])
            post[m] = jnp.where(mask, 0.0, made)
        return keep(k, post, carry)

    arrived(recv_sem.at[X], 2)
    xline[0], xline[1] = xrecv[0], xrecv[1]
    carry = (zero, zero, {name: zero for name in names})
    for k in range(2, D):
        carry = inner_plane(k, carry)

    for zs, there, group in ((0, has_down, BELOW), (1, has_up, ABOVE)):
        @pl.when(there)
        def _():
            arrived(recv_sem.at[group], z_tiles)

        beside = xside[zs]
        move = -D if zs == 0 else D
        masks = x_low if zs == 0 else x_high
        xline[0] = jnp.where(masks[0], rolled(beside, 2 * move, 1), xline[0])
        xline[1] = jnp.where(masks[1], rolled(beside, move - 4, 1), xline[1])
        for s in range(2):
            tile = erecv[zs, s]
            far = erecv_far[zs, 0 if ny == 2 else s]
            if s == 1:
                far = rolled(far, -2, 1)
            views = [tile] + [shifted(tile, n, rolled(far, n, 1)) for n in (1, 2)]
            for r, (m, _, target) in enumerate(edge_table[zs][s]):
                k = target if zs == 0 else D + 1 - target
                yline[s, GROUPS[1][s].index(m), k : k + 1, :] = views[1 + lattice[m][2]][r : r + 1, :]
        k = 0 if zs == 0 else D + 1
        spot = solid_at + 4 + (3 if zs == 0 else 1)
        frame[k] = shifted(szrecv[zs], 1, rolled(beside, -spot, 1))
        carry = inner_plane(1 if zs == 0 else D, carry)
        carry = outer_plane(k, carry)

    twos, ones, sums = carry
    for j in range(5):
        ones = put(ones, bound[1, j], bound_at1 + j, bound_at1 + j)
    xpack1[0], xpack1[1] = twos, ones
    top, bottom = row == H - 1, row == 0
    blocks = []
    for cx in (1, 0, -1):
        own = [zero, zero, zero]
        up, down = [zero] * 3, [zero] * 3
        if ("n", 0, cx) in sums and cx:
            own[2] = sums["n", 0, cx] if cx == 1 else -sums["n", 0, cx]
        own[0] = sums["z", 0, cx]
        for cy, beyond, edge in ((1, up, top), (-1, down, bottom)):
            n = sums["n", cy, cx]
            values = [sums.get(("z", cy, cx)), n if cy == 1 else -n, {1: n, 0: None, -1: -n}[cx]]
            for d in range(3):
                if values[d] is not None:
                    own[d] = own[d] + jnp.where(edge, 0.0, values[d])
                    beyond[d] = values[d]
        if cx == 0:
            own = [own[d] + speed[d] for d in range(3)]
        totals = [jnp.sum(v, axis=0, keepdims=True) for v in own]
        ups = [v[H - 1 :, :] for v in up]
        downs = [v[:1, :] for v in down]
        if ny == 2:
            lines = totals + [a + b for a, b in zip(ups, downs)]
        else:
            lines = totals + ups + downs
        blocks.append(lines)
    tiles = []
    for base in range(0, sent_v.shape[0], H):
        here = []
        for lines in blocks:
            tile = zero
            for r, line in enumerate(lines[base : base + H]):
                tile = jnp.where(row == r, jnp.broadcast_to(line, (H, W)), tile)
            here.append(tile)
        tiles.append(jnp.concatenate(here, axis=1))

    def exact_pick(x):
        high = x.astype(jnp.bfloat16).astype(f32)
        mid = (x - high).astype(jnp.bfloat16).astype(f32)
        low = x - high - mid
        stacked = jnp.concatenate([high, mid, low], axis=0).astype(jnp.bfloat16)
        made = jnp.dot(stacked, pick, preferred_element_type=f32)
        return made[:H] + made[H : 2 * H] + made[2 * H :]

    for i, tile in enumerate(tiles):
        sent_v[i * H : (i + 1) * H, :] = exact_pick(tile) * (1.0 / (CELL * CELL * CELL * base_density))
    tell = [
        pltpu.make_async_remote_copy(
            src_ref=sent_v, dst_ref=all_v.at[gy, gx], send_sem=send_sem.at[VEL_OUT],
            recv_sem=recv_sem.at[VEL], device_id=at(offset), device_id_type=MESH)
        for offset in flat
    ]
    start(tell)
    start(back)
    all_v[gy, gx] = sent_v[...]
    for s in range(2):
        acc = zero
        for i, m in enumerate(GROUPS[1][s]):
            if lattice[m][2] <= 0:
                acc = put_pair(acc, ypack1[s, i], i, 2 * i)
        cpack1[s] = acc
    start(back_c)

    @pl.when(is_first)
    def _():
        for s in range(2):
            near[0, s * ncy : (s + 1) * ncy, :] = jnp.full((ncy, wide), feed_level[s], f32)

    @pl.when(is_last)
    def _():
        near[1] = cend[...]

    source = lax.broadcasted_iota(jnp.int32, (ncx, ncx), 0)
    target = lax.broadcasted_iota(jnp.int32, (ncx, ncx), 1)
    ahead = jnp.where(target == ncx - 1, 0, target + 1)
    behind = jnp.where(target == 0, ncx - 1, target - 1)
    take_after = (source == ahead).astype(f32)
    take_before = (source == behind).astype(f32)

    def exact_dot(a, b):
        return jnp.dot(a, b, precision=lax.Precision.HIGHEST, preferred_element_type=f32)

    for s in range(2):
        c = conc[s, 0]
        wrapped[s, 1 : ncy + 1, :] = c
        wrapped[s, 0:1, :] = conc[s, 0, ncy - 1 : ncy, :]
        wrapped[s, ncy + 1 : ncy + 2, :] = conc[s, 0, 0:1, :]
        pairs = [
            tuple(near[e, s * ncy : (s + 1) * ncy, 0:ncx] for e in range(2)),
            (wrapped[s, 0:ncy, :], wrapped[s, 2 : ncy + 2, :]),
            (exact_dot(c, take_before), exact_dot(c, take_after)),
        ]
        curvature = sum(b + a - 2.0 * c for b, a in pairs)
        rate = uptake_rate[s] * (affinity[s] * c - load[s, 0])
        new_load[s, 0] = load[s, 0] + rate
        diffs.append((c - phase_ratio * rate + spread_base[s] * curvature, curvature,
                      [(c - b, a - c) for b, a in pairs]))

    arrived(recv_sem.at[BACK], 14)

    def emptied(tile, lanes, columns):
        return jnp.where(lane >= W - lanes, columns, rolled(tile, -lanes, 1)) if lanes else tile

    for s in range(2):
        corner = crecv1[s]
        for i, m in enumerate(GROUPS[1][s]):
            lanes = 1 - lattice[m][2]
            yline1[s, i] = emptied(yrecv1[s, i], lanes, rolled(corner, -lanes - 2 * i, 1))

    for t in range(D):
        for m in range(19):
            cz, cy, cx = lattice[m]
            v = post1[t + 1 - cz, m]
            if cx == -1:
                spot = 2 * (GROUPS[2][1].index(m) * D + t)
                v = emptied(v, 2, rolled(xrecv1[0], -2 - spot, 1))
            elif cx == 0:
                v = emptied(v, 1, rolled(xrecv1[1], -1 - (FLAT.index(m) * D + t), 1))
            if cy:
                s = 0 if cy == 1 else 1
                line = yline1[s, GROUPS[1][s].index(m), t : t + 1, :]
                v = jnp.where(row == (0 if s == 0 else H - 1),
                              jnp.broadcast_to(line, (H, W)), rolled(v, cy, 0))
            if (t == 0 and cz == 1) or (t == D - 1 and cz == -1):
                j = GROUPS[0][0 if cz == 1 else 1].index(m)
                kept = emptied(bound[1, j], 1, rolled(xrecv1[1], -1 - (bound_at1 + j), 1))
                v = jnp.where(first_mask if cz == 1 else last_mask, kept, v)
            out[m, t] = v

    arrived(send_sem.at[SLAB], slab_tiles)
    for sem, there in ((UP, has_up), (DOWN, has_down)):
        @pl.when(there)
        def _():
            arrived(send_sem.at[sem], z_tiles)
    vel_tiles = len(flat) * (sent_v.shape[0] // H)
    arrived(recv_sem.at[VEL], vel_tiles)
    totals = []
    for y in range(ny):
        total = all_v[y, 0]
        for x in range(1, nx):
            total = total + all_v[y, x]
        totals.append(total)
    for y in range(ny):
        for d in range(3):
            own = totals[y][d : d + 1]
            if ny == 2:
                own = own + totals[1 - y][3 + d : 4 + d]
            else:
                own = own + totals[(y - 1) % ny][3 + d : 4 + d] + totals[(y + 1) % ny][6 + d : 7 + d]
            vel[d, y : y + 1, :] = own
    courant = [CELL * vel[d][:, :ncx] for d in range(3)]
    reach = jnp.abs(courant[0]) + jnp.abs(courant[1]) + jnp.abs(courant[2])
    for s in range(2):
        value, curvature, steps = diffs[s]
        for d in range(3):
            low, high = steps[d]
            value = value - jnp.maximum(courant[d], 0.0) * low - jnp.minimum(courant[d], 0.0) * high
        new_conc[s, 0] = value + spread_length * reach * curvature
    arrived(send_sem.at[VEL_OUT], vel_tiles)


def hand_out(*refs):
    copies = [pltpu.make_async_copy(refs[i], refs[3 + i], refs[6].at[i]) for i in range(3)]
    for copy in copies:
        copy.start()
    for copy in copies:
        copy.wait()


def equilibrium_at_inlet():
    result = {}
    for m in GROUPS[0][0]:
        along = inlet_speed
        result[m] = weights[m] * base_density * (
            1.0 + 3.0 * along + 4.5 * along * along - 1.5 * inlet_speed * inlet_speed)
    return result


def solution(mesh):
    sizes = tuple(mesh.shape[a] for a in ("gz", "gy", "gx"))
    nz, ny, nx = sizes

    def body(populations, solid, ports, concentration, loaded):
        D, H, W = solid.shape
        ncy, ncx = concentration.shape[2:]
        assert D == CELL and H == CELL and W % 128 == 0 and 12 * (D + 2) <= W
        wide = -(-ncx // 128) * 128
        assert nz > 1 and ny > 1 and nx > 1 and W == wide
        f32 = jnp.float32
        tile = (H, W)
        rows = H if ny == 2 else 2 * H
        ends = -(-2 * ncy // H) * H
        anywhere = pl.BlockSpec(memory_space=pl.ANY)
        inside = pl.BlockSpec(memory_space=pltpu.VMEM)
        results = (populations, concentration, loaded)
        made = pl.pallas_call(
            functools.partial(kernel, sizes),
            out_shape=tuple(pltpu.VMEM(a.shape, f32) for a in results),
            in_specs=[anywhere] * 5,
            out_specs=(inside,) * 3,
            scratch_shapes=[
                pltpu.VMEM(populations.shape, f32),
                pltpu.VMEM(solid.shape, jnp.int32),
                pltpu.VMEM(ports.shape, jnp.int32),
                pltpu.VMEM(concentration.shape, f32),
                pltpu.VMEM(loaded.shape, f32),
                pltpu.VMEM((D, 19) + tile, f32),
                pltpu.VMEM((D + 2, 19) + tile, f32),
                pltpu.VMEM((2, 5) + tile, f32),
                pltpu.VMEM((3,) + tile, f32),
                pltpu.VMEM((2, 13) + tile, f32),
                pltpu.VMEM((2, 13) + tile, f32),
                pltpu.VMEM((2,) + tile, f32),
                pltpu.VMEM((2,) + tile, f32),
                pltpu.VMEM((2,) + tile, f32),
                pltpu.VMEM((2,) + tile, f32),
                pltpu.VMEM((2, 5, D, W), f32),
                pltpu.VMEM((2, 5, D, W), f32),
                pltpu.VMEM((2, 5, D, W), f32),
                pltpu.VMEM((2, 5, D, W), f32),
                pltpu.VMEM((2, D, W), f32),
                pltpu.VMEM((2, D, W), f32),
                pltpu.VMEM((2, D, W), f32),
                pltpu.VMEM((2, D, W), f32),
                pltpu.VMEM((2, 2) + tile, f32),
                pltpu.VMEM((2, 2) + tile, f32),
                pltpu.VMEM((2, 2) + tile, f32),
                pltpu.VMEM((2,) + tile, f32),
                pltpu.VMEM((2,) + tile, f32),
                pltpu.VMEM((2, 5, 2 * H, W), f32),
                pltpu.VMEM((2, 5, D, W), f32),
                pltpu.VMEM((2, 3, D, W), f32),
                pltpu.VMEM((D + 2,) + tile, f32),
                pltpu.VMEM((D + 2, 9) + tile, f32),
                pltpu.VMEM(tile, f32),
                pltpu.VMEM(tile, f32),
                pltpu.VMEM((2, D, W), f32),
                pltpu.VMEM((2, D, W), f32),
                pltpu.VMEM((2, D, W), f32),
                pltpu.VMEM((2,) + tile, f32),
                pltpu.VMEM((2,) + tile, f32),
                pltpu.VMEM((2,) + tile, f32),
                pltpu.VMEM((2,) + tile, f32),
                pltpu.VMEM((ends, wide), f32),
                pltpu.VMEM((2, ends, wide), f32),
                pltpu.VMEM((2, ncy + 2, ncx), f32),
                pltpu.VMEM((rows, wide), f32),
                pltpu.VMEM((ny, nx, rows, wide), f32),
                pltpu.VMEM((3, ncy, wide), f32),
                pltpu.VMEM((max(40, 2 * ny * nx),) + tile, f32),
                pltpu.SemaphoreType.DMA((7,)),
                pltpu.SemaphoreType.DMA((4,)),
                pltpu.SemaphoreType.DMA((7,)),
            ],
            compiler_params=pltpu.CompilerParams(collective_id=0, has_side_effects=True),
        )(populations, solid, ports, concentration, loaded)
        return pl.pallas_call(
            hand_out,
            out_shape=tuple(jax.ShapeDtypeStruct(a.shape, f32) for a in results),
            in_specs=[inside] * 3,
            out_specs=(anywhere,) * 3,
            scratch_shapes=[pltpu.SemaphoreType.DMA((3,))],
        )(*[pltpu.with_memory_space_constraint(a, pltpu.VMEM) for a in made])

    placed = (
        P(None, "gz", "gy", "gx"),
        P("gz", "gy", "gx"),
        P(None, "gy", "gx"),
        P(None, "gz", None, None),
        P(None, "gz", None, None),
    )
    return jax.shard_map(
        body,
        mesh=mesh,
        in_specs=placed,
        out_specs=(P(None, "gz", "gy", "gx"), P(None, "gz", None, None), P(None, "gz", None, None)),
        check_vma=False,
    )
```

```python
import functools

import jax
import jax.numpy as jnp
from jax import lax
from jax.experimental import pallas as pl
from jax.experimental.pallas import tpu as pltpu
from jax.sharding import PartitionSpec as P

ITERS = 2
CELL = 8
MESH = pl.DeviceIdType.MESH

lattice = [
    (0, 0, 0),
    (1, 0, 0),
    (-1, 0, 0),
    (0, 1, 0),
    (0, -1, 0),
    (0, 0, 1),
    (0, 0, -1),
    (1, 1, 0),
    (-1, -1, 0),
    (1, -1, 0),
    (-1, 1, 0),
    (1, 0, 1),
    (-1, 0, -1),
    (1, 0, -1),
    (-1, 0, 1),
    (0, 1, 1),
    (0, -1, -1),
    (0, 1, -1),
    (0, -1, 1),
]
opposite = [0, 2, 1, 4, 3, 6, 5, 8, 7, 10, 9, 12, 11, 14, 13, 16, 15, 18, 17]
weights = [1.0 / 3.0] + [1.0 / 18.0] * 6 + [1.0 / 36.0] * 12
relax_rate = 1.25
base_density = 36.0
inlet_speed = 0.05
spread_base = (0.03, 0.06)
spread_length = 0.1
uptake_rate = (0.3, 0.6)
affinity = (2.0, 0.5)
phase_ratio = 0.5
feed_level = (1.0, 0.5)

GROUPS = [[[m for m in range(19) if lattice[m][d] == s] for s in (1, -1)] for d in range(3)]
FLAT = [m for m in range(19) if lattice[m][2] == 0]
SOLID = 14
ORDER = GROUPS[0][0] + [m for m in range(19) if lattice[m][0] == 0] + [None] + GROUPS[0][1]
SLOT = {m: i for i, m in enumerate(ORDER) if m is not None}
TYPES = [(cy, cx) for cy in (1, 0, -1) for cx in (1, 0, -1)]


def moments(f):
    density = f[0]
    for member in range(1, 19):
        density = density + f[member]
    return density, momentum(f)


def momentum(f):
    flows = []
    for d in range(3):
        total = None
        for a, b in zip(GROUPS[d][0], [opposite[m] for m in GROUPS[d][0]]):
            part = f[a] - f[b]
            total = part if total is None else total + part
        flows.append(total)
    return flows


def balance(scale, velocity, members):
    square = velocity[0] * velocity[0] + velocity[1] * velocity[1] + velocity[2] * velocity[2]
    base = 1.0 - 1.5 * square
    cache, result = {}, {}
    for w in set(weights[m] for m in members):
        cache[w] = scale * w
    for m in members:
        if m == 0:
            result[m] = cache[weights[0]] * base
            continue
        key = min(m, opposite[m])
        if ("pair", key) not in cache:
            along = None
            for d in range(3):
                step = lattice[key][d]
                if step:
                    term = velocity[d]
                    if along is None:
                        along = term if step == 1 else -term
                    else:
                        along = along + term if step == 1 else along - term
            cache[("pair", key)] = (base + 4.5 * along * along, 3.0 * along)
        even, odd = cache[("pair", key)]
        result[m] = cache[weights[m]] * (even + odd if m == key else even - odd)
    return result


def collide(f, solid):
    density, flows = moments(f)
    inverse = 1.0 / density
    velocity = [flow * inverse for flow in flows]
    feq = balance(relax_rate * density, velocity, range(19))
    post = [
        jnp.where(solid, f[opposite[m]], (1.0 - relax_rate) * f[m] + feq[m]) for m in range(19)
    ]
    return post, velocity


def edge_rows(side, ends):
    far, near = ends
    across = [m for m in GROUPS[0][side[0]] if lattice[m][1] == 1 - 2 * side[1]]
    along = [m for m in GROUPS[1][side[1]] if lattice[m][0] == 0]
    return [(across[0], far, 0), (across[0], near, 1)] + [(m, near, 0) for m in along]


def level_sums(view, line, row, last, rolled):
    parts = {}
    for cy in (0, 1, -1):
        members = [m for m in range(19) if lattice[m][0] == 0 and lattice[m][1] == cy]
        for weigh in (lambda m: 1, lambda m: lattice[m][2]):
            moved, edge = None, None
            for m in members:
                for which, value in ((0, view(m)), (1, line(m) if cy else None)):
                    if value is None or not weigh(m):
                        continue
                    if which == 0:
                        value = value if weigh(m) == 1 else -value
                        moved = value if moved is None else moved + value
                    else:
                        value = value if weigh(m) == 1 else -value
                        edge = value if edge is None else edge + value
            if cy:
                edge = 0.0 if edge is None else jnp.broadcast_to(edge, moved.shape)
                moved = jnp.where(row == (0 if cy == 1 else last), edge, rolled(moved, cy, 0))
            parts.setdefault(cy, []).append(moved)
    return (parts[0][0] + parts[1][0] + parts[-1][0], parts[1][0] - parts[-1][0],
            parts[0][1] + parts[1][1] + parts[-1][1])


def kernel(sizes, *refs):
    nz, ny, nx = sizes
    (pop_hbm, solid_hbm, ports_hbm, conc_hbm, load_hbm, out, new_conc, new_load,
     pops, solid, ports, conc, load, post0, post1, bound, speed, zpack, zrecv, xpack, xrecv, xside, xline,
     ypack, yrecv, ypack1, yrecv1, cpack, crecv, cpack1, crecv1, epack, erecv, erecv_far, xpack1, xrecv1,
     yline, yline1, sline, frame, pore, sxpack, sxrecv, sypack, syrecv, screcv, szpack, szrecv, fpack, epack_far, cend, near, wrapped,
     sent_v, all_v, terms_ref, count_ref, load_sem, send_sem, recv_sem) = refs
    D, H, W = solid.shape
    T = D + 2
    ncy, ncx = conc.shape[2:]
    f32 = jnp.float32
    gz, gy, gx = lax.axis_index("gz"), lax.axis_index("gy"), lax.axis_index("gx")
    is_first, is_last = gz == 0, gz == nz - 1
    has_up, has_down = gz < nz - 1, gz > 0
    early = jnp.where(gz == 0, gx, 1) == 0
    late = jnp.where(gz == 0, gx, 1) > 0
    bound_at = len(FLAT) * T
    port_at = bound_at + 5
    solid_at = port_at + 2 + (port_at % 2)
    bound_at1 = len(FLAT) * D

    spans = [(0, 2), (D - 2, 2), (2, D - 4)]
    planes_in = [
        pltpu.make_async_copy(pop_hbm.at[:, pl.ds(a, n)], pops.at[:, pl.ds(a, n)], load_sem.at[i])
        for i, (a, n) in enumerate(spans)
    ]
    small = [
        pltpu.make_async_copy(a, b, load_sem.at[3 + i])
        for i, (a, b) in enumerate(
            ((solid_hbm, solid), (ports_hbm, ports), (conc_hbm, conc), (load_hbm, load)))
    ]
    def at(offset):
        dz, dy, dx = offset
        return {"gz": gz + dz, "gy": lax.rem(gy + dy + ny, ny), "gx": lax.rem(gx + dx + nx, nx)}

    flat = [(0, dy, dx) for dx in list(range(1, nx)) + [0] for dy in range(ny) if dy or dx]
    told = {(0, dy % ny, nx - 1) for dy in (0, 1, -1)} if nx > 2 else set()
    targets = sorted({(dy % ny, dx) for dy in (0, 1, -1) for dx in (0, 1)})
    barrier = pltpu.get_barrier_semaphore()

    def greet(offsets):
        for offset in offsets:
            pl.semaphore_signal(barrier, inc=1, device_id=at(offset), device_id_type=MESH)

    @pl.when(has_down)
    def _():
        greet([(-1, -dy, -dx) for dy, dx in targets])

    @pl.when(has_up)
    def _():
        greet([(1, -dy, -dx) for dy, dx in targets])

    greet([(0, -dy, -dx) for _, dy, dx in flat if (0, dy, dx) not in told])

    small[0].start()
    planes_in[0].start()
    small[1].start()
    small[2].start()
    small[3].start()
    planes_in[1].start()
    planes_in[2].start()

    lane = lax.broadcasted_iota(jnp.int32, (H, W), 1)
    row = lax.broadcasted_iota(jnp.int32, (H, W), 0)
    pair = lax.div(lane, 2)
    first_mask = jnp.full((H, W), gz, jnp.int32) == 0
    last_mask = jnp.full((H, W), gz, jnp.int32) == nz - 1
    zero = jnp.zeros((H, W), f32)

    def rolled(x, step, axis):
        step = step % x.shape[axis]
        return pltpu.roll(x, step, axis) if step else x

    def put(acc, value, spot, shift):
        return jnp.where(lane == spot, rolled(value, shift, 1), acc)

    def put_pair(acc, value, half, shift):
        return jnp.where(pair == half, rolled(value, shift, 1), acc)

    def edge_row(value, s):
        return value[H - 1 :, :] if s == 0 else value[:1, :]

    FLAGS, Y, X, BELOW, ABOVE, BACK, VEL, ENDS = range(8)
    SLAB, UP, DOWN, VEL_OUT = range(4)
    side_sets = [(pl.ds(0, 2), 1)] if ny == 2 else [(pl.ds(0, 1), 1), (pl.ds(1, 1), -1)]

    def remote(src, dst, offset, group):
        sent = {0: SLAB, 1: UP, -1: DOWN}[offset[0]]
        return pltpu.make_async_remote_copy(
            src_ref=src, dst_ref=dst, send_sem=send_sem.at[sent], recv_sem=recv_sem.at[group],
            device_id=at(offset), device_id_type=MESH)

    def arrived(sem, tiles):
        whole = count_ref.at[pl.ds(0, tiles)]
        pltpu.make_async_copy(whole, whole, sem).wait()

    def start(copies):
        for copy in copies:
            copy.start()

    along_z, first_z, ends = {}, {}, {}
    for dz, zs, group in ((1, 0, BELOW), (-1, 1, ABOVE)):
        first_z[dz] = [remote(szpack.at[zs], szrecv.at[zs], (dz, 0, 0), group)]
        ends[dz] = [remote(cend, near.at[zs], (dz, 0, 0), ENDS + zs)]
        along_z[dz] = [
            remote(zpack.at[zs], zrecv.at[zs], (dz, 0, 0), group),
            remote(fpack.at[zs], xside.at[zs], (dz, 0, 1), group),
        ]
        for i, (where, dy) in enumerate(side_sets):
            along_z[dz].append(remote(epack_far.at[zs], erecv_far.at[zs, i], (dz, dy, 1), group))
            along_z[dz].append(remote(epack.at[zs, where], erecv.at[zs, where], (dz, dy, 0), group))
    end_tiles = cend.shape[0] // H
    z_tiles = 1 + zpack.shape[1] + 1 + len(side_sets) + 2
    flags = [remote(sxpack, sxrecv, (0, 0, 1), FLAGS)]
    for where, dy in side_sets:
        flags.append(remote(sypack.at[where], screcv.at[where], (0, dy, 1), FLAGS))
        flags.append(remote(sypack.at[where], syrecv.at[where], (0, dy, 0), FLAGS))
    slab = [remote(xpack, xrecv, (0, 0, 1), X)]
    back_c = []
    back = [remote(xpack1, xrecv1, (0, 0, -1), BACK)]
    for where, dy in side_sets:
        slab.append(remote(cpack.at[where], crecv.at[where], (0, dy, 1), Y))
        slab.append(remote(ypack.at[where], yrecv.at[where], (0, dy, 0), Y))
        back.append(remote(ypack1.at[where], yrecv1.at[where], (0, dy, 0), BACK))
        back_c.append(remote(cpack1.at[where], crecv1.at[where], (0, dy, -1), BACK))
    slab_tiles = 5 + 2 + 12 + 14

    edge_table = [
        [edge_rows((zs, s), ((D - 2, D - 1), (1, 0))[zs]) for s in range(2)] for zs in range(2)]

    for copy in small:
        copy.wait()
    cend[...] = jnp.zeros(cend.shape, f32)
    for s in range(2):
        cend[s * ncy : (s + 1) * ncy, 0:ncx] = conc[s, 0]
    szpack[0] = solid[D - 1].astype(f32)
    szpack[1] = solid[0].astype(f32)
    walls_out = zero
    for z in range(D):
        wall = solid[z].astype(f32)
        walls_out = put_pair(walls_out, wall, z, 2 * z + 2)
        for s in range(2):
            sypack[s, z : z + 1, :] = edge_row(wall, s)
    sxpack[...] = walls_out

    def shifted(value, lanes, fill=0.0):
        return jnp.where(lane < lanes, fill, rolled(value, lanes, 1)) if lanes else value

    def first_plane(z, packs):
        f = [pops[m, z] for m in range(19)]
        flag = solid[z]
        post, velocity = collide(f, flag == 1)
        for m in range(19):
            post0[z, m] = post[m]
        for zs, ends_at in ((0, (D - 1, D - 2)), (1, (0, 1))):
            if z in ends_at:
                base = 5 * ends_at.index(z)
                for j, m in enumerate(GROUPS[0][zs]):
                    zpack[zs, base + j] = post[m]
            if z == ends_at[0]:
                sums = level_sums(lambda m: shifted(post[m], 1 + lattice[m][2]), lambda m: None,
                                  row, H - 1, rolled)
                for d in range(3):
                    zpack[zs, 10 + d] = sums[d]
        for s in range(2):
            for i, m in enumerate(GROUPS[1][s]):
                ypack[s, i, z : z + 1, :] = edge_row(post[m], s)
        for zs in range(2):
            for s in range(2):
                for r, (m, source, _) in enumerate(edge_table[zs][s]):
                    if source == z:
                        epack[zs, s, r : r + 1, :] = edge_row(post[m], s)
        if z == 0:
            inflow = equilibrium_at_inlet()
            for j, m in enumerate(GROUPS[0][0]):
                bound[0, j] = jnp.where(ports[0] == 1, inflow[m], post[opposite[m]])
        if z == D - 1:
            outflow = balance(base_density, velocity, GROUPS[0][1])
            for j, m in enumerate(GROUPS[0][1]):
                leaving = jnp.where(ports[1] == 1, outflow[m], post[opposite[m]])
                bound[0, j] = jnp.where(last_mask, leaving, bound[0, j])
        twos, ones = packs
        for i, m in enumerate(GROUPS[2][0]):
            q = i * T + z + lattice[m][0] + 1
            twos = put_pair(twos, post[m], q, 2 * q + 2)
        for i, m in enumerate(FLAT):
            q = i * T + z + lattice[m][0] + 1
            ones = put(ones, post[m], q, q + 1)
        if z in (0, D - 1):
            q = solid_at // 2 + (0 if z == 0 else 1)
            ones = put_pair(ones, flag.astype(f32), q, 2 * q + 2)
        return twos, ones

    def enter():
        count = lambda flag: jnp.where(flag, len(targets), 0)
        pl.semaphore_wait(barrier, len(flat) - len(told) + count(has_up) + count(has_down))

    def send(copies_of):
        for dz, there in ((-1, has_down), (1, has_up)):
            if dz in copies_of:
                @pl.when(there)
                def _():
                    start(copies_of[dz])

    def pack_z(zs, packs):
        twos, ones = packs
        base = 0 if zs == 1 else D
        mine = lane < 0
        for i in range(5):
            mine = mine | ((pair >= i * T + base) & (pair < i * T + base + 2))
        fpack[zs] = jnp.where(mine, twos, rolled(ones, 4, 1))
        epack_far[zs] = jnp.where(lane >= W - 2, epack[zs, 0], rolled(epack[zs, 1], 2, 1))

    packs = (zero, zero)
    planes_in[0].wait()
    for z in (0, 1):
        packs = first_plane(z, packs)
    pack_z(1, packs)
    planes_in[1].wait()
    for z in (D - 1, D - 2):
        packs = first_plane(z, packs)
    pack_z(0, packs)

    @pl.when(late)
    def _():
        enter()
        start(flags)
        send({-1: first_z[-1] + along_z[-1]})
        send({1: first_z[1] + along_z[1]})

    planes_in[2].wait()
    for z in range(2, D - 2):
        packs = first_plane(z, packs)
    twos, ones = packs
    for j in range(5):
        ones = put(ones, bound[0, j], bound_at + j, bound_at + j + 1)
    for j in range(2):
        ones = put(ones, ports[j].astype(f32), port_at + j, port_at + j + 1)
    xpack[0], xpack[1] = twos, ones
    for s in range(2):
        acc = zero
        for i in range(5):
            acc = put_pair(acc, ypack[s, i], i, 2 * i + 2)
        cpack[s] = acc

    @pl.when(early)
    def _():
        enter()
        start(flags)
        send(first_z)
        send({1: along_z[1]})

    start(slab)
    send(ends)

    x_low, x_high = [], []
    for members, spot in ((GROUPS[2][0], pair), (FLAT, lane)):
        low, high = lane < 0, lane < 0
        for i, m in enumerate(members):
            cz = lattice[m][0]
            if cz >= 0:
                low = low | ((spot >= i * T) & (spot < i * T + 1 + cz))
            if cz <= 0:
                high = high | ((spot >= i * T + D + 1 + cz) & (spot < i * T + T))
        x_low.append(low)
        x_high.append(high)

    diffs = []
    wide = sent_v.shape[-1]
    parts = []
    for c in (1, 0, -1):
        voxel = lax.broadcasted_iota(jnp.int32, (W, wide), 0) + gx * W - 1 + c
        voxel = jnp.where(voxel < 0, voxel + nx * W, voxel)
        cell = lax.broadcasted_iota(jnp.int32, (W, wide), 1) * CELL
        parts.append(((voxel >= cell) & (voxel < cell + CELL)).astype(f32))
    pick = jnp.concatenate(parts, axis=0).astype(jnp.bfloat16)

    arrived(recv_sem.at[FLAGS], 5)
    for s in range(2):
        for n in range(3):
            tile, far = syrecv[s], screcv[s]
            sline[s, n] = shifted(tile, n, rolled(far, n, 1)) if n else tile
    for n in range(9):
        pore[0, n] = zero
        pore[D + 1, n] = zero
    for k in range(1, D + 1):
        walls = solid[k - 1].astype(f32)
        columns = sxrecv[...]
        one = shifted(walls, 1, rolled(columns, 1 - 2 * k, 1))
        two = shifted(walls, 2, rolled(columns, 2 - 2 * k, 1))
        frame[k] = one
        for n, view in enumerate((walls, one, two)):
            cx = 1 - n
            pore[k, TYPES.index((0, cx))] = 1.0 - view
            for cy in (1, -1):
                s = 1 if cy == 1 else 0
                line = sline[s, n, k - 1 : k, :]
                moved = jnp.where(row == (H - 1 if cy == 1 else 0),
                                  jnp.broadcast_to(line, (H, W)), rolled(view, -cy, 0))
                pore[k, TYPES.index((cy, cx))] = 1.0 - moved

    arrived(recv_sem.at[Y], 12)

    def filled(tile, columns, lanes, spot):
        return shifted(tile, lanes, rolled(columns, -(spot + 2 - lanes), 1)) if lanes else tile

    for s in range(2):
        corner = crecv[s]
        for i, m in enumerate(GROUPS[1][s]):
            cz, _, cx = lattice[m]
            yline[s, i, 1 + cz : 1 + cz + D, :] = filled(yrecv[s, i], corner, 1 + cx, 2 * i)

    def column_of(m, k):
        if lattice[m][2] == 1:
            return rolled(xline[0], -2 * (GROUPS[2][0].index(m) * T + k), 1)
        return rolled(xline[1], -(FLAT.index(m) * T + k), 1)

    def line_of(m, k):
        s = 0 if lattice[m][1] == 1 else 1
        return yline[s, GROUPS[1][s].index(m), k : k + 1, :]

    def stream(k, members):
        f = {}
        for m in members:
            cz, cy, cx = lattice[m]
            z = k - 1 - cz
            if 0 <= z < D:
                v = post0[z, m]
            else:
                zs = 0 if cz == 1 else 1
                v = zrecv[zs, GROUPS[0][zs].index(m) + (5 if z in (-2, D + 1) else 0)]
            if cx >= 0:
                v = shifted(v, 1 + cx, column_of(m, k))
            if cy:
                v = jnp.where(row == (0 if cy == 1 else H - 1),
                              jnp.broadcast_to(line_of(m, k), (H, W)), rolled(v, cy, 0))
            f[m] = v
        return f

    def port_view(j):
        return shifted(ports[j].astype(f32), 1, rolled(xline[1], -(port_at + j), 1)) > 0.5

    def bound_view(j):
        return shifted(bound[0, j], 1, rolled(xline[1], -(bound_at + j), 1))

    names = [("n", cy, cx) for cy, cx in TYPES if cy or cx]
    names += [("z", cy, cx) for cy, cx in TYPES if not (cy and cx)]

    def keep(k, post, carry):
        twos, ones, sums = carry
        for m, value in post.items():
            cz, cy, cx = lattice[m]
            post1[k, m] = value
            t = k - 1 + cz
            if not 0 <= t < D:
                continue
            if cy:
                s = 0 if cy == 1 else 1
                ypack1[s, GROUPS[1][s].index(m), t : t + 1, :] = edge_row(value, s)
            if cx == -1:
                q = GROUPS[2][1].index(m) * D + t
                twos = put_pair(twos, value, q, 2 * q)
            elif cx == 0:
                q = FLAT.index(m) * D + t
                ones = put(ones, value, q, q)
            if m:
                part = value * pore[k + cz, TYPES.index((cy, cx))]
                if cy or cx:
                    sums["n", cy, cx] = sums["n", cy, cx] + part
                if cz == 1:
                    sums["z", cy, cx] = sums["z", cy, cx] + part
                if cz == -1:
                    sums["z", cy, cx] = sums["z", cy, cx] - part
        return twos, ones, sums

    def inner_plane(k, carry):
        f = stream(k, range(19))
        if k == 1:
            for j, m in enumerate(GROUPS[0][0]):
                f[m] = jnp.where(first_mask, bound_view(j), f[m])
        if k == D:
            for j, m in enumerate(GROUPS[0][1]):
                f[m] = jnp.where(last_mask, bound_view(j), f[m])
        post, velocity = collide([f[m] for m in range(19)], frame[k] > 0.5)
        carry = keep(k, dict(enumerate(post)), carry)
        if k in (1, D):
            if k == 1:
                members, opened, mask = GROUPS[0][0], port_view(0), first_mask
                values = equilibrium_at_inlet()
            else:
                members, opened, mask = GROUPS[0][1], port_view(1), last_mask
                values = balance(base_density, velocity, members)
            extra = [zero, zero, zero]
            for j, m in enumerate(members):
                value = jnp.where(opened, values[m], post[opposite[m]])
                bound[1, j] = value if k == 1 else jnp.where(last_mask, value, bound[1, j])
                for d in range(3):
                    if lattice[m][d]:
                        extra[d] = extra[d] + value if lattice[m][d] == 1 else extra[d] - value
            for d in range(3):
                add = jnp.where(mask, extra[d] * pore[k, TYPES.index((0, 0))], 0.0)
                speed[d] = add if k == 1 else speed[d] + add
        return carry

    def outer_plane(k, carry):
        zs, mask = (0, first_mask) if k == 0 else (1, last_mask)
        members = GROUPS[0][zs]
        f = stream(k, GROUPS[0][0] + GROUPS[0][1])
        sums = level_sums(
            lambda m: jnp.where(lane < 1 + lattice[m][2], column_of(m, k), 0.0) if lattice[m][2] >= 0 else None,
            lambda m: line_of(m, k), row, H - 1, rolled)
        density, flow_y, flow_x = [zrecv[zs, 10 + d] + sums[d] for d in range(3)]
        flows = [None, flow_y, flow_x]
        for m, value in f.items():
            density = density + value
            for d in range(3):
                if lattice[m][d]:
                    signed = value if lattice[m][d] == 1 else -value
                    flows[d] = signed if flows[d] is None else flows[d] + signed
        inverse = 1.0 / density
        feq = balance(relax_rate * density, [flow * inverse for flow in flows], members)
        wall = frame[k] > 0.5
        post = {}
        for m in members:
            made = jnp.where(wall, f[opposite[m]], (1.0 - relax_rate) * f[m] + feq[m])
            post[m] = jnp.where(mask, 0.0, made)
        return keep(k, post, carry)

    arrived(recv_sem.at[X], 2)
    xline[0], xline[1] = xrecv[0], xrecv[1]
    carry = (zero, zero, {name: zero for name in names})
    for k in range(2, D):
        carry = inner_plane(k, carry)

    for zs, there, group in ((0, has_down, BELOW), (1, has_up, ABOVE)):
        @pl.when(there)
        def _():
            arrived(recv_sem.at[group], z_tiles)

        beside = xside[zs]
        move = -D if zs == 0 else D
        masks = x_low if zs == 0 else x_high
        xline[0] = jnp.where(masks[0], rolled(beside, 2 * move, 1), xline[0])
        xline[1] = jnp.where(masks[1], rolled(beside, move - 4, 1), xline[1])
        for s in range(2):
            tile = erecv[zs, s]
            far = erecv_far[zs, 0 if ny == 2 else s]
            if s == 1:
                far = rolled(far, -2, 1)
            views = [tile] + [shifted(tile, n, rolled(far, n, 1)) for n in (1, 2)]
            for r, (m, _, target) in enumerate(edge_table[zs][s]):
                k = target if zs == 0 else D + 1 - target
                yline[s, GROUPS[1][s].index(m), k : k + 1, :] = views[1 + lattice[m][2]][r : r + 1, :]
        k = 0 if zs == 0 else D + 1
        spot = solid_at + 4 + (3 if zs == 0 else 1)
        frame[k] = shifted(szrecv[zs], 1, rolled(beside, -spot, 1))
        carry = inner_plane(1 if zs == 0 else D, carry)
        carry = outer_plane(k, carry)

    twos, ones, sums = carry
    for j in range(5):
        ones = put(ones, bound[1, j], bound_at1 + j, bound_at1 + j)
    xpack1[0], xpack1[1] = twos, ones
    top, bottom = row == H - 1, row == 0
    blocks = []
    for cx in (1, 0, -1):
        own = [zero, zero, zero]
        up, down = [zero] * 3, [zero] * 3
        if ("n", 0, cx) in sums and cx:
            own[2] = sums["n", 0, cx] if cx == 1 else -sums["n", 0, cx]
        own[0] = sums["z", 0, cx]
        for cy, beyond, edge in ((1, up, top), (-1, down, bottom)):
            n = sums["n", cy, cx]
            values = [sums.get(("z", cy, cx)), n if cy == 1 else -n, {1: n, 0: None, -1: -n}[cx]]
            for d in range(3):
                if values[d] is not None:
                    own[d] = own[d] + jnp.where(edge, 0.0, values[d])
                    beyond[d] = values[d]
        if cx == 0:
            own = [own[d] + speed[d] for d in range(3)]
        totals = [jnp.sum(v, axis=0, keepdims=True) for v in own]
        ups = [v[H - 1 :, :] for v in up]
        downs = [v[:1, :] for v in down]
        rows_of = [(0, totals)]
        if ny == 2:
            rows_of.append((1, [a + b for a, b in zip(ups, downs)]))
        else:
            rows_of += [(1, ups), (-1, downs)]
        blocks.append(rows_of)
    tiles = []
    for base in range(0, sent_v.shape[0], H):
        here = []
        for rows_of in blocks:
            tile = zero
            for dy, lines in rows_of:
                spot = lax.rem(gy + dy + ny, ny) - base
                for d in range(3):
                    tile = jnp.where(row == spot + d * ny, jnp.broadcast_to(lines[d], (H, W)), tile)
            here.append(tile)
        tiles.append(jnp.concatenate(here, axis=1))

    def exact_pick(x):
        high = x.astype(jnp.bfloat16).astype(f32)
        mid = (x - high).astype(jnp.bfloat16).astype(f32)
        low = x - high - mid
        stacked = jnp.concatenate([high, mid, low], axis=0).astype(jnp.bfloat16)
        made = jnp.dot(stacked, pick, preferred_element_type=f32)
        return made[:H] + made[H : 2 * H] + made[2 * H :]

    for i, tile in enumerate(tiles):
        sent_v[i * H : (i + 1) * H, :] = exact_pick(tile) * (1.0 / (CELL * CELL * CELL * base_density))
    tell = [
        pltpu.make_async_remote_copy(
            src_ref=sent_v, dst_ref=all_v.at[gy, gx], send_sem=send_sem.at[VEL_OUT],
            recv_sem=recv_sem.at[VEL], device_id=at(offset), device_id_type=MESH)
        for offset in flat
    ]
    start(tell)
    start(back)
    all_v[gy, gx] = sent_v[...]
    for s in range(2):
        acc = zero
        for i, m in enumerate(GROUPS[1][s]):
            if lattice[m][2] <= 0:
                acc = put_pair(acc, ypack1[s, i], i, 2 * i)
        cpack1[s] = acc
    start(back_c)

    for zs, there in ((0, has_down), (1, has_up)):
        @pl.when(there)
        def _():
            arrived(recv_sem.at[ENDS + zs], end_tiles)

    @pl.when(is_first)
    def _():
        for s in range(2):
            near[0, s * ncy : (s + 1) * ncy, :] = jnp.full((ncy, wide), feed_level[s], f32)

    @pl.when(is_last)
    def _():
        near[1] = cend[...]

    source = lax.broadcasted_iota(jnp.int32, (ncx, ncx), 0)
    target = lax.broadcasted_iota(jnp.int32, (ncx, ncx), 1)
    ahead = jnp.where(target == ncx - 1, 0, target + 1)
    behind = jnp.where(target == 0, ncx - 1, target - 1)
    take_after = (source == ahead).astype(f32)
    take_before = (source == behind).astype(f32)

    def exact_dot(a, b):
        return jnp.dot(a, b, precision=lax.Precision.HIGHEST, preferred_element_type=f32)

    terms_ref[...] = jnp.zeros(terms_ref.shape, f32)
    for s in range(2):
        c = conc[s, 0]
        wrapped[s, 1 : ncy + 1, :] = c
        wrapped[s, 0:1, :] = conc[s, 0, ncy - 1 : ncy, :]
        wrapped[s, ncy + 1 : ncy + 2, :] = conc[s, 0, 0:1, :]
        pairs = [
            tuple(near[e, s * ncy : (s + 1) * ncy, 0:ncx] for e in range(2)),
            (wrapped[s, 0:ncy, :], wrapped[s, 2 : ncy + 2, :]),
            (exact_dot(c, take_before), exact_dot(c, take_after)),
        ]
        curvature = sum(b + a - 2.0 * c for b, a in pairs)
        rate = uptake_rate[s] * (affinity[s] * c - load[s, 0])
        new_load[s, 0] = load[s, 0] + rate
        diffs.append(c - phase_ratio * rate + spread_base[s] * curvature)
        for d, (before, after) in enumerate(pairs):
            for n, value in enumerate((c - before, after - c, curvature)):
                terms_ref[s, n, d * ncy : (d + 1) * ncy, 0:ncx] = value

    arrived(recv_sem.at[BACK], 14)

    def emptied(tile, lanes, columns):
        return jnp.where(lane >= W - lanes, columns, rolled(tile, -lanes, 1)) if lanes else tile

    for s in range(2):
        corner = crecv1[s]
        for i, m in enumerate(GROUPS[1][s]):
            lanes = 1 - lattice[m][2]
            yline1[s, i] = emptied(yrecv1[s, i], lanes, rolled(corner, -lanes - 2 * i, 1))

    for t in range(D):
        for m in range(19):
            cz, cy, cx = lattice[m]
            v = post1[t + 1 - cz, m]
            if cx == -1:
                spot = 2 * (GROUPS[2][1].index(m) * D + t)
                v = emptied(v, 2, rolled(xrecv1[0], -2 - spot, 1))
            elif cx == 0:
                v = emptied(v, 1, rolled(xrecv1[1], -1 - (FLAT.index(m) * D + t), 1))
            if cy:
                s = 0 if cy == 1 else 1
                line = yline1[s, GROUPS[1][s].index(m), t : t + 1, :]
                v = jnp.where(row == (0 if s == 0 else H - 1),
                              jnp.broadcast_to(line, (H, W)), rolled(v, cy, 0))
            if (t == 0 and cz == 1) or (t == D - 1 and cz == -1):
                j = GROUPS[0][0 if cz == 1 else 1].index(m)
                kept = emptied(bound[1, j], 1, rolled(xrecv1[1], -1 - (bound_at1 + j), 1))
                v = jnp.where(first_mask if cz == 1 else last_mask, kept, v)
            out[m, t] = v

    arrived(send_sem.at[SLAB], slab_tiles)
    for sem, there in ((UP, has_up), (DOWN, has_down)):
        @pl.when(there)
        def _():
            arrived(send_sem.at[sem], z_tiles + end_tiles)
    vel_tiles = len(flat) * (sent_v.shape[0] // H)
    arrived(recv_sem.at[VEL], vel_tiles)
    parts = [all_v[y, x] for y in range(ny) for x in range(nx)]
    while len(parts) > 1:
        parts = [sum(parts[i : i + 2][1:], parts[i]) for i in range(0, len(parts), 2)]
    courant = CELL * parts[0]
    forward, backward, reach = jnp.maximum(courant, 0.0), jnp.minimum(courant, 0.0), jnp.abs(courant)
    for s in range(2):
        terms = spread_length * reach * terms_ref[s, 2] - forward * terms_ref[s, 0] - backward * terms_ref[s, 1]
        moved = terms[0:ncy] + terms[ncy : 2 * ncy] + terms[2 * ncy : 3 * ncy]
        new_conc[s, 0] = diffs[s] + moved[:, 0:ncx]
    arrived(send_sem.at[VEL_OUT], vel_tiles)


def hand_out(*refs):
    copies = [pltpu.make_async_copy(refs[i], refs[3 + i], refs[6].at[i]) for i in range(3)]
    for copy in copies:
        copy.start()
    for copy in copies:
        copy.wait()


def equilibrium_at_inlet():
    result = {}
    for m in GROUPS[0][0]:
        along = inlet_speed
        result[m] = weights[m] * base_density * (
            1.0 + 3.0 * along + 4.5 * along * along - 1.5 * inlet_speed * inlet_speed)
    return result


def solution(mesh):
    sizes = tuple(mesh.shape[a] for a in ("gz", "gy", "gx"))
    nz, ny, nx = sizes

    def body(populations, solid, ports, concentration, loaded):
        D, H, W = solid.shape
        ncy, ncx = concentration.shape[2:]
        assert D == CELL and H == CELL and W % 128 == 0 and 12 * (D + 2) <= W
        wide = -(-ncx // 128) * 128
        assert nz > 1 and ny > 1 and nx > 1 and W == wide
        f32 = jnp.float32
        tile = (H, W)
        rows = -(-3 * ny // H) * H
        assert ncy == ny
        ends = -(-2 * ncy // H) * H
        anywhere = pl.BlockSpec(memory_space=pl.ANY)
        inside = pl.BlockSpec(memory_space=pltpu.VMEM)
        results = (populations, concentration, loaded)
        made = pl.pallas_call(
            functools.partial(kernel, sizes),
            out_shape=tuple(pltpu.VMEM(a.shape, f32) for a in results),
            in_specs=[anywhere] * 5,
            out_specs=(inside,) * 3,
            scratch_shapes=[
                pltpu.VMEM(populations.shape, f32),
                pltpu.VMEM(solid.shape, jnp.int32),
                pltpu.VMEM(ports.shape, jnp.int32),
                pltpu.VMEM(concentration.shape, f32),
                pltpu.VMEM(loaded.shape, f32),
                pltpu.VMEM((D, 19) + tile, f32),
                pltpu.VMEM((D + 2, 19) + tile, f32),
                pltpu.VMEM((2, 5) + tile, f32),
                pltpu.VMEM((3,) + tile, f32),
                pltpu.VMEM((2, 13) + tile, f32),
                pltpu.VMEM((2, 13) + tile, f32),
                pltpu.VMEM((2,) + tile, f32),
                pltpu.VMEM((2,) + tile, f32),
                pltpu.VMEM((2,) + tile, f32),
                pltpu.VMEM((2,) + tile, f32),
                pltpu.VMEM((2, 5, D, W), f32),
                pltpu.VMEM((2, 5, D, W), f32),
                pltpu.VMEM((2, 5, D, W), f32),
                pltpu.VMEM((2, 5, D, W), f32),
                pltpu.VMEM((2, D, W), f32),
                pltpu.VMEM((2, D, W), f32),
                pltpu.VMEM((2, D, W), f32),
                pltpu.VMEM((2, D, W), f32),
                pltpu.VMEM((2, 2) + tile, f32),
                pltpu.VMEM((2, 2) + tile, f32),
                pltpu.VMEM((2, 2) + tile, f32),
                pltpu.VMEM((2,) + tile, f32),
                pltpu.VMEM((2,) + tile, f32),
                pltpu.VMEM((2, 5, 2 * H, W), f32),
                pltpu.VMEM((2, 5, D, W), f32),
                pltpu.VMEM((2, 3, D, W), f32),
                pltpu.VMEM((D + 2,) + tile, f32),
                pltpu.VMEM((D + 2, 9) + tile, f32),
                pltpu.VMEM(tile, f32),
                pltpu.VMEM(tile, f32),
                pltpu.VMEM((2, D, W), f32),
                pltpu.VMEM((2, D, W), f32),
                pltpu.VMEM((2, D, W), f32),
                pltpu.VMEM((2,) + tile, f32),
                pltpu.VMEM((2,) + tile, f32),
                pltpu.VMEM((2,) + tile, f32),
                pltpu.VMEM((2,) + tile, f32),
                pltpu.VMEM((ends, wide), f32),
                pltpu.VMEM((2, ends, wide), f32),
                pltpu.VMEM((2, ncy + 2, ncx), f32),
                pltpu.VMEM((rows, wide), f32),
                pltpu.VMEM((ny, nx, rows, wide), f32),
                pltpu.VMEM((2, 3, rows, wide), f32),
                pltpu.VMEM((max(40, ny * nx * (rows // H)),) + tile, f32),
                pltpu.SemaphoreType.DMA((7,)),
                pltpu.SemaphoreType.DMA((4,)),
                pltpu.SemaphoreType.DMA((9,)),
            ],
            compiler_params=pltpu.CompilerParams(collective_id=0, has_side_effects=True),
        )(populations, solid, ports, concentration, loaded)
        return pl.pallas_call(
            hand_out,
            out_shape=tuple(jax.ShapeDtypeStruct(a.shape, f32) for a in results),
            in_specs=[inside] * 3,
            out_specs=(anywhere,) * 3,
            scratch_shapes=[pltpu.SemaphoreType.DMA((3,))],
        )(*[pltpu.with_memory_space_constraint(a, pltpu.VMEM) for a in made])

    placed = (
        P(None, "gz", "gy", "gx"),
        P("gz", "gy", "gx"),
        P(None, "gy", "gx"),
        P(None, "gz", None, None),
        P(None, "gz", None, None),
    )
    return jax.shard_map(
        body,
        mesh=mesh,
        in_specs=placed,
        out_specs=(P(None, "gz", "gy", "gx"), P(None, "gz", None, None), P(None, "gz", None, None)),
        check_vma=False,
    )
```

```python
import functools

import jax
import jax.numpy as jnp
from jax import lax
from jax.experimental import pallas as pl
from jax.experimental.pallas import tpu as pltpu
from jax.sharding import PartitionSpec as P

ITERS = 2
CELL = 8
MESH = pl.DeviceIdType.MESH

lattice = [
    (0, 0, 0),
    (1, 0, 0),
    (-1, 0, 0),
    (0, 1, 0),
    (0, -1, 0),
    (0, 0, 1),
    (0, 0, -1),
    (1, 1, 0),
    (-1, -1, 0),
    (1, -1, 0),
    (-1, 1, 0),
    (1, 0, 1),
    (-1, 0, -1),
    (1, 0, -1),
    (-1, 0, 1),
    (0, 1, 1),
    (0, -1, -1),
    (0, 1, -1),
    (0, -1, 1),
]
opposite = [0, 2, 1, 4, 3, 6, 5, 8, 7, 10, 9, 12, 11, 14, 13, 16, 15, 18, 17]
weights = [1.0 / 3.0] + [1.0 / 18.0] * 6 + [1.0 / 36.0] * 12
relax_rate = 1.25
base_density = 36.0
inlet_speed = 0.05
spread_base = (0.03, 0.06)
spread_length = 0.1
uptake_rate = (0.3, 0.6)
affinity = (2.0, 0.5)
phase_ratio = 0.5
feed_level = (1.0, 0.5)

GROUPS = [[[m for m in range(19) if lattice[m][d] == s] for s in (1, -1)] for d in range(3)]
FLAT = [m for m in range(19) if lattice[m][2] == 0]
SOLID = 14
ORDER = GROUPS[0][0] + [m for m in range(19) if lattice[m][0] == 0] + [None] + GROUPS[0][1]
SLOT = {m: i for i, m in enumerate(ORDER) if m is not None}
TYPES = [(cy, cx) for cy in (1, 0, -1) for cx in (1, 0, -1)]


def moments(f):
    density = f[0]
    for member in range(1, 19):
        density = density + f[member]
    return density, momentum(f)


def momentum(f):
    flows = []
    for d in range(3):
        total = None
        for a, b in zip(GROUPS[d][0], [opposite[m] for m in GROUPS[d][0]]):
            part = f[a] - f[b]
            total = part if total is None else total + part
        flows.append(total)
    return flows


def balance(scale, velocity, members):
    square = velocity[0] * velocity[0] + velocity[1] * velocity[1] + velocity[2] * velocity[2]
    base = 1.0 - 1.5 * square
    cache, result = {}, {}
    for w in set(weights[m] for m in members):
        cache[w] = scale * w
    for m in members:
        if m == 0:
            result[m] = cache[weights[0]] * base
            continue
        key = min(m, opposite[m])
        if ("pair", key) not in cache:
            along = None
            for d in range(3):
                step = lattice[key][d]
                if step:
                    term = velocity[d]
                    if along is None:
                        along = term if step == 1 else -term
                    else:
                        along = along + term if step == 1 else along - term
            cache[("pair", key)] = (base + 4.5 * along * along, 3.0 * along)
        even, odd = cache[("pair", key)]
        result[m] = cache[weights[m]] * (even + odd if m == key else even - odd)
    return result


def collide(f, solid):
    density, flows = moments(f)
    inverse = 1.0 / density
    velocity = [flow * inverse for flow in flows]
    feq = balance(relax_rate * density, velocity, range(19))
    post = [
        jnp.where(solid, f[opposite[m]], (1.0 - relax_rate) * f[m] + feq[m]) for m in range(19)
    ]
    return post, velocity


def edge_rows(side, ends):
    far, near = ends
    across = [m for m in GROUPS[0][side[0]] if lattice[m][1] == 1 - 2 * side[1]]
    along = [m for m in GROUPS[1][side[1]] if lattice[m][0] == 0]
    return [(across[0], far, 0), (across[0], near, 1)] + [(m, near, 0) for m in along]


def level_sums(view, line, row, last, rolled):
    parts = {}
    for cy in (0, 1, -1):
        members = [m for m in range(19) if lattice[m][0] == 0 and lattice[m][1] == cy]
        for weigh in (lambda m: 1, lambda m: lattice[m][2]):
            moved, edge = None, None
            for m in members:
                for which, value in ((0, view(m)), (1, line(m) if cy else None)):
                    if value is None or not weigh(m):
                        continue
                    if which == 0:
                        value = value if weigh(m) == 1 else -value
                        moved = value if moved is None else moved + value
                    else:
                        value = value if weigh(m) == 1 else -value
                        edge = value if edge is None else edge + value
            if cy:
                edge = 0.0 if edge is None else jnp.broadcast_to(edge, moved.shape)
                moved = jnp.where(row == (0 if cy == 1 else last), edge, rolled(moved, cy, 0))
            parts.setdefault(cy, []).append(moved)
    return (parts[0][0] + parts[1][0] + parts[-1][0], parts[1][0] - parts[-1][0],
            parts[0][1] + parts[1][1] + parts[-1][1])


def kernel(sizes, *refs):
    nz, ny, nx = sizes
    (pop_hbm, solid_hbm, ports_hbm, conc_hbm, load_hbm, out, new_conc, new_load,
     pops, solid, ports, conc, load, post0, post1, bound, speed, zpack, zrecv, xpack, xrecv, xside, xline,
     ypack, yrecv, ypack1, yrecv1, cpack, crecv, cpack1, crecv1, epack, erecv, erecv_far, xpack1, xrecv1,
     yline, yline1, sline, frame, pore, sxpack, sxrecv, sypack, syrecv, screcv, fpack, epack_far, cend, near, wrapped,
     sent_v, all_v, terms_ref, count_ref, load_sem, send_sem, recv_sem) = refs
    D, H, W = solid.shape
    T = D + 2
    ncy, ncx = conc.shape[2:]
    f32 = jnp.float32
    gz, gy, gx = lax.axis_index("gz"), lax.axis_index("gy"), lax.axis_index("gx")
    is_first, is_last = gz == 0, gz == nz - 1
    has_up, has_down = gz < nz - 1, gz > 0
    early = jnp.where(gz == 0, gx, 1) == 0
    late = jnp.where(gz == 0, gx, 1) > 0
    bound_at = len(FLAT) * T
    port_at = bound_at + 5
    solid_at = port_at + 2 + (port_at % 2)
    bound_at1 = len(FLAT) * D

    spans = [(0, 2), (D - 2, 2), (2, D - 4)]
    planes_in = [
        pltpu.make_async_copy(pop_hbm.at[:, pl.ds(a, n)], pops.at[:, pl.ds(a, n)], load_sem.at[i])
        for i, (a, n) in enumerate(spans)
    ]
    small = [
        pltpu.make_async_copy(a, b, load_sem.at[3 + i])
        for i, (a, b) in enumerate(
            ((solid_hbm, solid), (ports_hbm, ports), (conc_hbm, conc), (load_hbm, load)))
    ]
    def at(offset):
        dz, dy, dx = offset
        return {"gz": gz + dz, "gy": lax.rem(gy + dy + ny, ny), "gx": lax.rem(gx + dx + nx, nx)}

    flat = [(0, dy, dx) for dx in list(range(1, nx)) + [0] for dy in range(ny) if dy or dx]
    told = {(0, dy % ny, nx - 1) for dy in (0, 1, -1)} if nx > 2 else set()
    targets = sorted({(dy % ny, dx) for dy in (0, 1, -1) for dx in (0, 1)})
    barrier = pltpu.get_barrier_semaphore()

    def greet(offsets):
        for offset in offsets:
            pl.semaphore_signal(barrier, inc=1, device_id=at(offset), device_id_type=MESH)

    @pl.when(has_down)
    def _():
        greet([(-1, -dy, -dx) for dy, dx in targets])

    @pl.when(has_up)
    def _():
        greet([(1, -dy, -dx) for dy, dx in targets])

    greet([(0, -dy, -dx) for _, dy, dx in flat if (0, dy, dx) not in told])

    small[0].start()
    planes_in[0].start()
    small[1].start()
    small[2].start()
    small[3].start()
    planes_in[1].start()
    planes_in[2].start()

    lane = lax.broadcasted_iota(jnp.int32, (H, W), 1)
    row = lax.broadcasted_iota(jnp.int32, (H, W), 0)
    pair = lax.div(lane, 2)
    first_mask = jnp.full((H, W), gz, jnp.int32) == 0
    last_mask = jnp.full((H, W), gz, jnp.int32) == nz - 1
    zero = jnp.zeros((H, W), f32)

    def rolled(x, step, axis):
        step = step % x.shape[axis]
        return pltpu.roll(x, step, axis) if step else x

    def put(acc, value, spot, shift):
        return jnp.where(lane == spot, rolled(value, shift, 1), acc)

    def put_pair(acc, value, half, shift):
        return jnp.where(pair == half, rolled(value, shift, 1), acc)

    def edge_row(value, s):
        return value[H - 1 :, :] if s == 0 else value[:1, :]

    FLAGS, Y, X, BELOW, ABOVE, BACK, VEL, ENDS = range(8)
    SLAB, UP, DOWN, VEL_OUT = range(4)
    side_sets = [(pl.ds(0, 2), 1)] if ny == 2 else [(pl.ds(0, 1), 1), (pl.ds(1, 1), -1)]

    def remote(src, dst, offset, group):
        sent = {0: SLAB, 1: UP, -1: DOWN}[offset[0]]
        return pltpu.make_async_remote_copy(
            src_ref=src, dst_ref=dst, send_sem=send_sem.at[sent], recv_sem=recv_sem.at[group],
            device_id=at(offset), device_id_type=MESH)

    def arrived(sem, tiles):
        whole = count_ref.at[pl.ds(0, tiles)]
        pltpu.make_async_copy(whole, whole, sem).wait()

    def start(copies):
        for copy in copies:
            copy.start()

    along_z, ends = {}, {}
    for dz, zs, group in ((1, 0, BELOW), (-1, 1, ABOVE)):
        ends[dz] = [remote(cend, near.at[zs], (dz, 0, 0), ENDS + zs)]
        along_z[dz] = [
            remote(zpack.at[zs], zrecv.at[zs], (dz, 0, 0), group),
            remote(fpack.at[zs], xside.at[zs], (dz, 0, 1), group),
        ]
        for i, (where, dy) in enumerate(side_sets):
            along_z[dz].append(remote(epack_far.at[zs], erecv_far.at[zs, i], (dz, dy, 1), group))
            along_z[dz].append(remote(epack.at[zs, where], erecv.at[zs, where], (dz, dy, 0), group))
    end_tiles = cend.shape[0] // H
    z_tiles = zpack.shape[1] + 1 + len(side_sets) + 2
    flags = [remote(sxpack, sxrecv, (0, 0, 1), FLAGS)]
    for where, dy in side_sets:
        flags.append(remote(sypack.at[where], screcv.at[where], (0, dy, 1), FLAGS))
        flags.append(remote(sypack.at[where], syrecv.at[where], (0, dy, 0), FLAGS))
    slab = [remote(xpack, xrecv, (0, 0, 1), X)]
    back_c = []
    back = [remote(xpack1, xrecv1, (0, 0, -1), BACK)]
    for where, dy in side_sets:
        slab.append(remote(cpack.at[where], crecv.at[where], (0, dy, 1), Y))
        slab.append(remote(ypack.at[where], yrecv.at[where], (0, dy, 0), Y))
        back.append(remote(ypack1.at[where], yrecv1.at[where], (0, dy, 0), BACK))
        back_c.append(remote(cpack1.at[where], crecv1.at[where], (0, dy, -1), BACK))
    slab_tiles = 5 + 2 + 12 + 14

    edge_table = [
        [edge_rows((zs, s), ((D - 2, D - 1), (1, 0))[zs]) for s in range(2)] for zs in range(2)]

    for copy in small:
        copy.wait()
    cend[...] = jnp.zeros(cend.shape, f32)
    for s in range(2):
        cend[s * ncy : (s + 1) * ncy, 0:ncx] = conc[s, 0]
    zpack[0, 13] = solid[D - 1].astype(f32)
    zpack[1, 13] = solid[0].astype(f32)
    walls_out = zero
    for z in range(D):
        wall = solid[z].astype(f32)
        walls_out = put_pair(walls_out, wall, z, 2 * z + 2)
        for s in range(2):
            sypack[s, z : z + 1, :] = edge_row(wall, s)
    sxpack[...] = walls_out

    def shifted(value, lanes, fill=0.0):
        return jnp.where(lane < lanes, fill, rolled(value, lanes, 1)) if lanes else value

    def first_plane(z, packs):
        f = [pops[m, z] for m in range(19)]
        flag = solid[z]
        post, velocity = collide(f, flag == 1)
        for m in range(19):
            post0[z, m] = post[m]
        for zs, ends_at in ((0, (D - 1, D - 2)), (1, (0, 1))):
            if z in ends_at:
                base = 5 * ends_at.index(z)
                for j, m in enumerate(GROUPS[0][zs]):
                    zpack[zs, base + j] = post[m]
            if z == ends_at[0]:
                sums = level_sums(lambda m: shifted(post[m], 1 + lattice[m][2]), lambda m: None,
                                  row, H - 1, rolled)
                for d in range(3):
                    zpack[zs, 10 + d] = sums[d]
        for s in range(2):
            for i, m in enumerate(GROUPS[1][s]):
                ypack[s, i, z : z + 1, :] = edge_row(post[m], s)
        for zs in range(2):
            for s in range(2):
                for r, (m, source, _) in enumerate(edge_table[zs][s]):
                    if source == z:
                        epack[zs, s, r : r + 1, :] = edge_row(post[m], s)
        if z == 0:
            inflow = equilibrium_at_inlet()
            for j, m in enumerate(GROUPS[0][0]):
                bound[0, j] = jnp.where(ports[0] == 1, inflow[m], post[opposite[m]])
        if z == D - 1:
            outflow = balance(base_density, velocity, GROUPS[0][1])
            for j, m in enumerate(GROUPS[0][1]):
                leaving = jnp.where(ports[1] == 1, outflow[m], post[opposite[m]])
                bound[0, j] = jnp.where(last_mask, leaving, bound[0, j])
        twos, ones = packs
        for i, m in enumerate(GROUPS[2][0]):
            q = i * T + z + lattice[m][0] + 1
            twos = put_pair(twos, post[m], q, 2 * q + 2)
        for i, m in enumerate(FLAT):
            q = i * T + z + lattice[m][0] + 1
            ones = put(ones, post[m], q, q + 1)
        if z in (0, D - 1):
            q = solid_at // 2 + (0 if z == 0 else 1)
            ones = put_pair(ones, flag.astype(f32), q, 2 * q + 2)
        return twos, ones

    def enter():
        count = lambda flag: jnp.where(flag, len(targets), 0)
        pl.semaphore_wait(barrier, len(flat) - len(told) + count(has_up) + count(has_down))

    def send(copies_of):
        for dz, there in ((-1, has_down), (1, has_up)):
            if dz in copies_of:
                @pl.when(there)
                def _():
                    start(copies_of[dz])

    def pack_z(zs, packs):
        twos, ones = packs
        base = 0 if zs == 1 else D
        mine = lane < 0
        for i in range(5):
            mine = mine | ((pair >= i * T + base) & (pair < i * T + base + 2))
        fpack[zs] = jnp.where(mine, twos, rolled(ones, 4, 1))
        epack_far[zs] = jnp.where(lane >= W - 2, epack[zs, 0], rolled(epack[zs, 1], 2, 1))

    packs = (zero, zero)
    planes_in[0].wait()
    for z in (0, 1):
        packs = first_plane(z, packs)
    pack_z(1, packs)
    planes_in[1].wait()
    for z in (D - 1, D - 2):
        packs = first_plane(z, packs)
    pack_z(0, packs)

    @pl.when(late)
    def _():
        enter()
        start(flags)
        send({-1: along_z[-1]})
        send({1: along_z[1]})

    planes_in[2].wait()
    for z in range(2, D - 2):
        packs = first_plane(z, packs)
    twos, ones = packs
    for j in range(5):
        ones = put(ones, bound[0, j], bound_at + j, bound_at + j + 1)
    for j in range(2):
        ones = put(ones, ports[j].astype(f32), port_at + j, port_at + j + 1)
    xpack[0], xpack[1] = twos, ones
    for s in range(2):
        acc = zero
        for i in range(5):
            acc = put_pair(acc, ypack[s, i], i, 2 * i + 2)
        cpack[s] = acc

    @pl.when(early)
    def _():
        enter()
        start(flags)
        send({1: along_z[1]})

    start(slab)
    send(ends)

    x_low, x_high = [], []
    for members, spot in ((GROUPS[2][0], pair), (FLAT, lane)):
        low, high = lane < 0, lane < 0
        for i, m in enumerate(members):
            cz = lattice[m][0]
            if cz >= 0:
                low = low | ((spot >= i * T) & (spot < i * T + 1 + cz))
            if cz <= 0:
                high = high | ((spot >= i * T + D + 1 + cz) & (spot < i * T + T))
        x_low.append(low)
        x_high.append(high)

    diffs = []
    wide = sent_v.shape[-1]
    parts = []
    for c in (1, 0, -1):
        voxel = lax.broadcasted_iota(jnp.int32, (W, wide), 0) + gx * W - 1 + c
        voxel = jnp.where(voxel < 0, voxel + nx * W, voxel)
        cell = lax.broadcasted_iota(jnp.int32, (W, wide), 1) * CELL
        parts.append(((voxel >= cell) & (voxel < cell + CELL)).astype(f32))
    pick = jnp.concatenate(parts, axis=0).astype(jnp.bfloat16)

    arrived(recv_sem.at[FLAGS], 5)
    for s in range(2):
        for n in range(3):
            tile, far = syrecv[s], screcv[s]
            sline[s, n] = shifted(tile, n, rolled(far, n, 1)) if n else tile
    for n in range(9):
        pore[0, n] = zero
        pore[D + 1, n] = zero
    for k in range(1, D + 1):
        walls = solid[k - 1].astype(f32)
        columns = sxrecv[...]
        one = shifted(walls, 1, rolled(columns, 1 - 2 * k, 1))
        two = shifted(walls, 2, rolled(columns, 2 - 2 * k, 1))
        frame[k] = one
        for n, view in enumerate((walls, one, two)):
            cx = 1 - n
            pore[k, TYPES.index((0, cx))] = 1.0 - view
            for cy in (1, -1):
                s = 1 if cy == 1 else 0
                line = sline[s, n, k - 1 : k, :]
                moved = jnp.where(row == (H - 1 if cy == 1 else 0),
                                  jnp.broadcast_to(line, (H, W)), rolled(view, -cy, 0))
                pore[k, TYPES.index((cy, cx))] = 1.0 - moved

    arrived(recv_sem.at[Y], 12)

    def filled(tile, columns, lanes, spot):
        return shifted(tile, lanes, rolled(columns, -(spot + 2 - lanes), 1)) if lanes else tile

    for s in range(2):
        corner = crecv[s]
        for i, m in enumerate(GROUPS[1][s]):
            cz, _, cx = lattice[m]
            yline[s, i, 1 + cz : 1 + cz + D, :] = filled(yrecv[s, i], corner, 1 + cx, 2 * i)

    def column_of(m, k):
        if lattice[m][2] == 1:
            return rolled(xline[0], -2 * (GROUPS[2][0].index(m) * T + k), 1)
        return rolled(xline[1], -(FLAT.index(m) * T + k), 1)

    def line_of(m, k):
        s = 0 if lattice[m][1] == 1 else 1
        return yline[s, GROUPS[1][s].index(m), k : k + 1, :]

    def stream(k, members):
        f = {}
        for m in members:
            cz, cy, cx = lattice[m]
            z = k - 1 - cz
            if 0 <= z < D:
                v = post0[z, m]
            else:
                zs = 0 if cz == 1 else 1
                v = zrecv[zs, GROUPS[0][zs].index(m) + (5 if z in (-2, D + 1) else 0)]
            if cx >= 0:
                v = shifted(v, 1 + cx, column_of(m, k))
            if cy:
                v = jnp.where(row == (0 if cy == 1 else H - 1),
                              jnp.broadcast_to(line_of(m, k), (H, W)), rolled(v, cy, 0))
            f[m] = v
        return f

    def port_view(j):
        return shifted(ports[j].astype(f32), 1, rolled(xline[1], -(port_at + j), 1)) > 0.5

    def bound_view(j):
        return shifted(bound[0, j], 1, rolled(xline[1], -(bound_at + j), 1))

    names = [("n", cy, cx) for cy, cx in TYPES if cy or cx]
    names += [("z", cy, cx) for cy, cx in TYPES if not (cy and cx)]

    def keep(k, post, carry):
        twos, ones, sums = carry
        for m, value in post.items():
            cz, cy, cx = lattice[m]
            post1[k, m] = value
            t = k - 1 + cz
            if not 0 <= t < D:
                continue
            if cy:
                s = 0 if cy == 1 else 1
                ypack1[s, GROUPS[1][s].index(m), t : t + 1, :] = edge_row(value, s)
            if cx == -1:
                q = GROUPS[2][1].index(m) * D + t
                twos = put_pair(twos, value, q, 2 * q)
            elif cx == 0:
                q = FLAT.index(m) * D + t
                ones = put(ones, value, q, q)
            if m:
                part = value * pore[k + cz, TYPES.index((cy, cx))]
                if cy or cx:
                    sums["n", cy, cx] = sums["n", cy, cx] + part
                if cz == 1:
                    sums["z", cy, cx] = sums["z", cy, cx] + part
                if cz == -1:
                    sums["z", cy, cx] = sums["z", cy, cx] - part
        return twos, ones, sums

    def inner_plane(k, carry):
        f = stream(k, range(19))
        if k == 1:
            for j, m in enumerate(GROUPS[0][0]):
                f[m] = jnp.where(first_mask, bound_view(j), f[m])
        if k == D:
            for j, m in enumerate(GROUPS[0][1]):
                f[m] = jnp.where(last_mask, bound_view(j), f[m])
        post, velocity = collide([f[m] for m in range(19)], frame[k] > 0.5)
        carry = keep(k, dict(enumerate(post)), carry)
        if k in (1, D):
            if k == 1:
                members, opened, mask = GROUPS[0][0], port_view(0), first_mask
                values = equilibrium_at_inlet()
            else:
                members, opened, mask = GROUPS[0][1], port_view(1), last_mask
                values = balance(base_density, velocity, members)
            extra = [zero, zero, zero]
            for j, m in enumerate(members):
                value = jnp.where(opened, values[m], post[opposite[m]])
                bound[1, j] = value if k == 1 else jnp.where(last_mask, value, bound[1, j])
                for d in range(3):
                    if lattice[m][d]:
                        extra[d] = extra[d] + value if lattice[m][d] == 1 else extra[d] - value
            for d in range(3):
                add = jnp.where(mask, extra[d] * pore[k, TYPES.index((0, 0))], 0.0)
                speed[d] = add if k == 1 else speed[d] + add
        return carry

    def outer_plane(k, carry):
        zs, mask = (0, first_mask) if k == 0 else (1, last_mask)
        members = GROUPS[0][zs]
        f = stream(k, GROUPS[0][0] + GROUPS[0][1])
        sums = level_sums(
            lambda m: jnp.where(lane < 1 + lattice[m][2], column_of(m, k), 0.0) if lattice[m][2] >= 0 else None,
            lambda m: line_of(m, k), row, H - 1, rolled)
        density, flow_y, flow_x = [zrecv[zs, 10 + d] + sums[d] for d in range(3)]
        flows = [None, flow_y, flow_x]
        for m, value in f.items():
            density = density + value
            for d in range(3):
                if lattice[m][d]:
                    signed = value if lattice[m][d] == 1 else -value
                    flows[d] = signed if flows[d] is None else flows[d] + signed
        inverse = 1.0 / density
        feq = balance(relax_rate * density, [flow * inverse for flow in flows], members)
        wall = frame[k] > 0.5
        post = {}
        for m in members:
            made = jnp.where(wall, f[opposite[m]], (1.0 - relax_rate) * f[m] + feq[m])
            post[m] = jnp.where(mask, 0.0, made)
        return keep(k, post, carry)

    arrived(recv_sem.at[X], 2)
    xline[0], xline[1] = xrecv[0], xrecv[1]
    carry = (zero, zero, {name: zero for name in names})
    for k in range(2, D):
        carry = inner_plane(k, carry)

    for zs, there, group in ((0, has_down, BELOW), (1, has_up, ABOVE)):
        @pl.when(there)
        def _():
            arrived(recv_sem.at[group], z_tiles)

        beside = xside[zs]
        move = -D if zs == 0 else D
        masks = x_low if zs == 0 else x_high
        xline[0] = jnp.where(masks[0], rolled(beside, 2 * move, 1), xline[0])
        xline[1] = jnp.where(masks[1], rolled(beside, move - 4, 1), xline[1])
        for s in range(2):
            tile = erecv[zs, s]
            far = erecv_far[zs, 0 if ny == 2 else s]
            if s == 1:
                far = rolled(far, -2, 1)
            views = [tile] + [shifted(tile, n, rolled(far, n, 1)) for n in (1, 2)]
            for r, (m, _, target) in enumerate(edge_table[zs][s]):
                k = target if zs == 0 else D + 1 - target
                yline[s, GROUPS[1][s].index(m), k : k + 1, :] = views[1 + lattice[m][2]][r : r + 1, :]
        k = 0 if zs == 0 else D + 1
        spot = solid_at + 4 + (3 if zs == 0 else 1)
        frame[k] = shifted(zrecv[zs, 13], 1, rolled(beside, -spot, 1))
        carry = inner_plane(1 if zs == 0 else D, carry)
        carry = outer_plane(k, carry)

    twos, ones, sums = carry
    for j in range(5):
        ones = put(ones, bound[1, j], bound_at1 + j, bound_at1 + j)
    xpack1[0], xpack1[1] = twos, ones
    top, bottom = row == H - 1, row == 0
    blocks = []
    for cx in (1, 0, -1):
        own = [zero, zero, zero]
        up, down = [zero] * 3, [zero] * 3
        if ("n", 0, cx) in sums and cx:
            own[2] = sums["n", 0, cx] if cx == 1 else -sums["n", 0, cx]
        own[0] = sums["z", 0, cx]
        for cy, beyond, edge in ((1, up, top), (-1, down, bottom)):
            n = sums["n", cy, cx]
            values = [sums.get(("z", cy, cx)), n if cy == 1 else -n, {1: n, 0: None, -1: -n}[cx]]
            for d in range(3):
                if values[d] is not None:
                    own[d] = own[d] + jnp.where(edge, 0.0, values[d])
                    beyond[d] = values[d]
        if cx == 0:
            own = [own[d] + speed[d] for d in range(3)]
        totals = [jnp.sum(v, axis=0, keepdims=True) for v in own]
        ups = [v[H - 1 :, :] for v in up]
        downs = [v[:1, :] for v in down]
        rows_of = [(0, totals)]
        if ny == 2:
            rows_of.append((1, [a + b for a, b in zip(ups, downs)]))
        else:
            rows_of += [(1, ups), (-1, downs)]
        blocks.append(rows_of)
    tiles = []
    for base in range(0, sent_v.shape[0], H):
        here = []
        for rows_of in blocks:
            tile = zero
            for dy, lines in rows_of:
                spot = lax.rem(gy + dy + ny, ny) - base
                for d in range(3):
                    tile = jnp.where(row == spot + d * ny, jnp.broadcast_to(lines[d], (H, W)), tile)
            here.append(tile)
        tiles.append(jnp.concatenate(here, axis=1))

    def exact_pick(x):
        high = x.astype(jnp.bfloat16).astype(f32)
        mid = (x - high).astype(jnp.bfloat16).astype(f32)
        low = x - high - mid
        stacked = jnp.concatenate([high, mid, low], axis=0).astype(jnp.bfloat16)
        made = jnp.dot(stacked, pick, preferred_element_type=f32)
        return made[:H] + made[H : 2 * H] + made[2 * H :]

    for i, tile in enumerate(tiles):
        sent_v[i * H : (i + 1) * H, :] = exact_pick(tile) * (1.0 / (CELL * CELL * CELL * base_density))
    tell = [
        pltpu.make_async_remote_copy(
            src_ref=sent_v, dst_ref=all_v.at[gy, gx], send_sem=send_sem.at[VEL_OUT],
            recv_sem=recv_sem.at[VEL], device_id=at(offset), device_id_type=MESH)
        for offset in flat
    ]
    start(tell)
    start(back)
    all_v[gy, gx] = sent_v[...]
    for s in range(2):
        acc = zero
        for i, m in enumerate(GROUPS[1][s]):
            if lattice[m][2] <= 0:
                acc = put_pair(acc, ypack1[s, i], i, 2 * i)
        cpack1[s] = acc
    start(back_c)

    for zs, there in ((0, has_down), (1, has_up)):
        @pl.when(there)
        def _():
            arrived(recv_sem.at[ENDS + zs], end_tiles)

    @pl.when(is_first)
    def _():
        for s in range(2):
            near[0, s * ncy : (s + 1) * ncy, :] = jnp.full((ncy, wide), feed_level[s], f32)

    @pl.when(is_last)
    def _():
        near[1] = cend[...]

    source = lax.broadcasted_iota(jnp.int32, (ncx, ncx), 0)
    target = lax.broadcasted_iota(jnp.int32, (ncx, ncx), 1)
    ahead = jnp.where(target == ncx - 1, 0, target + 1)
    behind = jnp.where(target == 0, ncx - 1, target - 1)
    take_after = (source == ahead).astype(f32)
    take_before = (source == behind).astype(f32)

    def exact_dot(a, b):
        return jnp.dot(a, b, precision=lax.Precision.HIGHEST, preferred_element_type=f32)

    terms_ref[...] = jnp.zeros(terms_ref.shape, f32)
    for s in range(2):
        c = conc[s, 0]
        wrapped[s, 1 : ncy + 1, :] = c
        wrapped[s, 0:1, :] = conc[s, 0, ncy - 1 : ncy, :]
        wrapped[s, ncy + 1 : ncy + 2, :] = conc[s, 0, 0:1, :]
        pairs = [
            tuple(near[e, s * ncy : (s + 1) * ncy, 0:ncx] for e in range(2)),
            (wrapped[s, 0:ncy, :], wrapped[s, 2 : ncy + 2, :]),
            (exact_dot(c, take_before), exact_dot(c, take_after)),
        ]
        curvature = sum(b + a - 2.0 * c for b, a in pairs)
        rate = uptake_rate[s] * (affinity[s] * c - load[s, 0])
        new_load[s, 0] = load[s, 0] + rate
        diffs.append(c - phase_ratio * rate + spread_base[s] * curvature)
        for d, (before, after) in enumerate(pairs):
            for n, value in enumerate((c - before, after - c, curvature)):
                terms_ref[s, n, d * ncy : (d + 1) * ncy, 0:ncx] = value

    arrived(recv_sem.at[BACK], 14)

    def emptied(tile, lanes, columns):
        return jnp.where(lane >= W - lanes, columns, rolled(tile, -lanes, 1)) if lanes else tile

    for s in range(2):
        corner = crecv1[s]
        for i, m in enumerate(GROUPS[1][s]):
            lanes = 1 - lattice[m][2]
            yline1[s, i] = emptied(yrecv1[s, i], lanes, rolled(corner, -lanes - 2 * i, 1))

    for t in range(D):
        for m in range(19):
            cz, cy, cx = lattice[m]
            v = post1[t + 1 - cz, m]
            if cx == -1:
                spot = 2 * (GROUPS[2][1].index(m) * D + t)
                v = emptied(v, 2, rolled(xrecv1[0], -2 - spot, 1))
            elif cx == 0:
                v = emptied(v, 1, rolled(xrecv1[1], -1 - (FLAT.index(m) * D + t), 1))
            if cy:
                s = 0 if cy == 1 else 1
                line = yline1[s, GROUPS[1][s].index(m), t : t + 1, :]
                v = jnp.where(row == (0 if s == 0 else H - 1),
                              jnp.broadcast_to(line, (H, W)), rolled(v, cy, 0))
            if (t == 0 and cz == 1) or (t == D - 1 and cz == -1):
                j = GROUPS[0][0 if cz == 1 else 1].index(m)
                kept = emptied(bound[1, j], 1, rolled(xrecv1[1], -1 - (bound_at1 + j), 1))
                v = jnp.where(first_mask if cz == 1 else last_mask, kept, v)
            out[m, t] = v

    arrived(send_sem.at[SLAB], slab_tiles)
    for sem, there in ((UP, has_up), (DOWN, has_down)):
        @pl.when(there)
        def _():
            arrived(send_sem.at[sem], z_tiles + end_tiles)
    vel_tiles = len(flat) * (sent_v.shape[0] // H)
    arrived(recv_sem.at[VEL], vel_tiles)
    parts = [all_v[y, x] for y in range(ny) for x in range(nx)]
    while len(parts) > 1:
        parts = [sum(parts[i : i + 2][1:], parts[i]) for i in range(0, len(parts), 2)]
    courant = CELL * parts[0]
    forward, backward, reach = jnp.maximum(courant, 0.0), jnp.minimum(courant, 0.0), jnp.abs(courant)
    for s in range(2):
        terms = spread_length * reach * terms_ref[s, 2] - forward * terms_ref[s, 0] - backward * terms_ref[s, 1]
        moved = terms[0:ncy] + terms[ncy : 2 * ncy] + terms[2 * ncy : 3 * ncy]
        new_conc[s, 0] = diffs[s] + moved[:, 0:ncx]
    arrived(send_sem.at[VEL_OUT], vel_tiles)


def hand_out(*refs):
    copies = [pltpu.make_async_copy(refs[i], refs[3 + i], refs[6].at[i]) for i in range(3)]
    for copy in copies:
        copy.start()
    for copy in copies:
        copy.wait()


def equilibrium_at_inlet():
    result = {}
    for m in GROUPS[0][0]:
        along = inlet_speed
        result[m] = weights[m] * base_density * (
            1.0 + 3.0 * along + 4.5 * along * along - 1.5 * inlet_speed * inlet_speed)
    return result


def solution(mesh):
    sizes = tuple(mesh.shape[a] for a in ("gz", "gy", "gx"))
    nz, ny, nx = sizes

    def body(populations, solid, ports, concentration, loaded):
        D, H, W = solid.shape
        ncy, ncx = concentration.shape[2:]
        assert D == CELL and H == CELL and W % 128 == 0 and 12 * (D + 2) <= W
        wide = -(-ncx // 128) * 128
        assert nz > 1 and ny > 1 and nx > 1 and W == wide
        f32 = jnp.float32
        tile = (H, W)
        rows = -(-3 * ny // H) * H
        assert ncy == ny
        ends = -(-2 * ncy // H) * H
        anywhere = pl.BlockSpec(memory_space=pl.ANY)
        inside = pl.BlockSpec(memory_space=pltpu.VMEM)
        results = (populations, concentration, loaded)
        made = pl.pallas_call(
            functools.partial(kernel, sizes),
            out_shape=tuple(pltpu.VMEM(a.shape, f32) for a in results),
            in_specs=[anywhere] * 5,
            out_specs=(inside,) * 3,
            scratch_shapes=[
                pltpu.VMEM(populations.shape, f32),
                pltpu.VMEM(solid.shape, jnp.int32),
                pltpu.VMEM(ports.shape, jnp.int32),
                pltpu.VMEM(concentration.shape, f32),
                pltpu.VMEM(loaded.shape, f32),
                pltpu.VMEM((D, 19) + tile, f32),
                pltpu.VMEM((D + 2, 19) + tile, f32),
                pltpu.VMEM((2, 5) + tile, f32),
                pltpu.VMEM((3,) + tile, f32),
                pltpu.VMEM((2, 14) + tile, f32),
                pltpu.VMEM((2, 14) + tile, f32),
                pltpu.VMEM((2,) + tile, f32),
                pltpu.VMEM((2,) + tile, f32),
                pltpu.VMEM((2,) + tile, f32),
                pltpu.VMEM((2,) + tile, f32),
                pltpu.VMEM((2, 5, D, W), f32),
                pltpu.VMEM((2, 5, D, W), f32),
                pltpu.VMEM((2, 5, D, W), f32),
                pltpu.VMEM((2, 5, D, W), f32),
                pltpu.VMEM((2, D, W), f32),
                pltpu.VMEM((2, D, W), f32),
                pltpu.VMEM((2, D, W), f32),
                pltpu.VMEM((2, D, W), f32),
                pltpu.VMEM((2, 2) + tile, f32),
                pltpu.VMEM((2, 2) + tile, f32),
                pltpu.VMEM((2, 2) + tile, f32),
                pltpu.VMEM((2,) + tile, f32),
                pltpu.VMEM((2,) + tile, f32),
                pltpu.VMEM((2, 5, 2 * H, W), f32),
                pltpu.VMEM((2, 5, D, W), f32),
                pltpu.VMEM((2, 3, D, W), f32),
                pltpu.VMEM((D + 2,) + tile, f32),
                pltpu.VMEM((D + 2, 9) + tile, f32),
                pltpu.VMEM(tile, f32),
                pltpu.VMEM(tile, f32),
                pltpu.VMEM((2, D, W), f32),
                pltpu.VMEM((2, D, W), f32),
                pltpu.VMEM((2, D, W), f32),
                pltpu.VMEM((2,) + tile, f32),
                pltpu.VMEM((2,) + tile, f32),
                pltpu.VMEM((ends, wide), f32),
                pltpu.VMEM((2, ends, wide), f32),
                pltpu.VMEM((2, ncy + 2, ncx), f32),
                pltpu.VMEM((rows, wide), f32),
                pltpu.VMEM((ny, nx, rows, wide), f32),
                pltpu.VMEM((2, 3, rows, wide), f32),
                pltpu.VMEM((max(40, ny * nx * (rows // H)),) + tile, f32),
                pltpu.SemaphoreType.DMA((7,)),
                pltpu.SemaphoreType.DMA((4,)),
                pltpu.SemaphoreType.DMA((9,)),
            ],
            compiler_params=pltpu.CompilerParams(collective_id=0, has_side_effects=True),
        )(populations, solid, ports, concentration, loaded)
        return pl.pallas_call(
            hand_out,
            out_shape=tuple(jax.ShapeDtypeStruct(a.shape, f32) for a in results),
            in_specs=[inside] * 3,
            out_specs=(anywhere,) * 3,
            scratch_shapes=[pltpu.SemaphoreType.DMA((3,))],
        )(*[pltpu.with_memory_space_constraint(a, pltpu.VMEM) for a in made])

    placed = (
        P(None, "gz", "gy", "gx"),
        P("gz", "gy", "gx"),
        P(None, "gy", "gx"),
        P(None, "gz", None, None),
        P(None, "gz", None, None),
    )
    return jax.shard_map(
        body,
        mesh=mesh,
        in_specs=placed,
        out_specs=(P(None, "gz", "gy", "gx"), P(None, "gz", None, None), P(None, "gz", None, None)),
        check_vma=False,
    )
```

```python
import functools

import jax
import jax.numpy as jnp
from jax import lax
from jax.experimental import pallas as pl
from jax.experimental.pallas import tpu as pltpu
from jax.sharding import PartitionSpec as P

ITERS = 2
CELL = 8
MESH = pl.DeviceIdType.MESH

lattice = [
    (0, 0, 0),
    (1, 0, 0),
    (-1, 0, 0),
    (0, 1, 0),
    (0, -1, 0),
    (0, 0, 1),
    (0, 0, -1),
    (1, 1, 0),
    (-1, -1, 0),
    (1, -1, 0),
    (-1, 1, 0),
    (1, 0, 1),
    (-1, 0, -1),
    (1, 0, -1),
    (-1, 0, 1),
    (0, 1, 1),
    (0, -1, -1),
    (0, 1, -1),
    (0, -1, 1),
]
opposite = [0, 2, 1, 4, 3, 6, 5, 8, 7, 10, 9, 12, 11, 14, 13, 16, 15, 18, 17]
weights = [1.0 / 3.0] + [1.0 / 18.0] * 6 + [1.0 / 36.0] * 12
relax_rate = 1.25
base_density = 36.0
inlet_speed = 0.05
spread_base = (0.03, 0.06)
spread_length = 0.1
uptake_rate = (0.3, 0.6)
affinity = (2.0, 0.5)
phase_ratio = 0.5
feed_level = (1.0, 0.5)

GROUPS = [[[m for m in range(19) if lattice[m][d] == s] for s in (1, -1)] for d in range(3)]
FLAT = [m for m in range(19) if lattice[m][2] == 0]
SOLID = 14
ORDER = GROUPS[0][0] + [m for m in range(19) if lattice[m][0] == 0] + [None] + GROUPS[0][1]
SLOT = {m: i for i, m in enumerate(ORDER) if m is not None}
TYPES = [(cy, cx) for cy in (1, 0, -1) for cx in (1, 0, -1)]


def moments(f):
    density = f[0]
    for member in range(1, 19):
        density = density + f[member]
    return density, momentum(f)


def momentum(f):
    flows = []
    for d in range(3):
        total = None
        for a, b in zip(GROUPS[d][0], [opposite[m] for m in GROUPS[d][0]]):
            part = f[a] - f[b]
            total = part if total is None else total + part
        flows.append(total)
    return flows


def balance(scale, velocity, members):
    square = velocity[0] * velocity[0] + velocity[1] * velocity[1] + velocity[2] * velocity[2]
    base = 1.0 - 1.5 * square
    cache, result = {}, {}
    for w in set(weights[m] for m in members):
        cache[w] = scale * w
    for m in members:
        if m == 0:
            result[m] = cache[weights[0]] * base
            continue
        key = min(m, opposite[m])
        if ("pair", key) not in cache:
            along = None
            for d in range(3):
                step = lattice[key][d]
                if step:
                    term = velocity[d]
                    if along is None:
                        along = term if step == 1 else -term
                    else:
                        along = along + term if step == 1 else along - term
            cache[("pair", key)] = (base + 4.5 * along * along, 3.0 * along)
        even, odd = cache[("pair", key)]
        result[m] = cache[weights[m]] * (even + odd if m == key else even - odd)
    return result


def collide(f, solid):
    density, flows = moments(f)
    inverse = 1.0 / density
    velocity = [flow * inverse for flow in flows]
    feq = balance(relax_rate * density, velocity, range(19))
    post = [
        jnp.where(solid, f[opposite[m]], (1.0 - relax_rate) * f[m] + feq[m]) for m in range(19)
    ]
    return post, velocity


def edge_rows(side, ends):
    far, near = ends
    across = [m for m in GROUPS[0][side[0]] if lattice[m][1] == 1 - 2 * side[1]]
    along = [m for m in GROUPS[1][side[1]] if lattice[m][0] == 0]
    return [(across[0], far, 0), (across[0], near, 1)] + [(m, near, 0) for m in along]


def level_sums(view, line, row, last, rolled):
    parts = {}
    for cy in (0, 1, -1):
        members = [m for m in range(19) if lattice[m][0] == 0 and lattice[m][1] == cy]
        for weigh in (lambda m: 1, lambda m: lattice[m][2]):
            moved, edge = None, None
            for m in members:
                for which, value in ((0, view(m)), (1, line(m) if cy else None)):
                    if value is None or not weigh(m):
                        continue
                    if which == 0:
                        value = value if weigh(m) == 1 else -value
                        moved = value if moved is None else moved + value
                    else:
                        value = value if weigh(m) == 1 else -value
                        edge = value if edge is None else edge + value
            if cy:
                edge = 0.0 if edge is None else jnp.broadcast_to(edge, moved.shape)
                moved = jnp.where(row == (0 if cy == 1 else last), edge, rolled(moved, cy, 0))
            parts.setdefault(cy, []).append(moved)
    return (parts[0][0] + parts[1][0] + parts[-1][0], parts[1][0] - parts[-1][0],
            parts[0][1] + parts[1][1] + parts[-1][1])


def kernel(sizes, *refs):
    nz, ny, nx = sizes
    (pop_hbm, solid_hbm, ports_hbm, conc_hbm, load_hbm, out, new_conc, new_load,
     pops, solid, ports, conc, load, post0, post1, bound, speed, zpack, zrecv, xpack, xrecv, xside, xline,
     ypack, yrecv, ypack1, yrecv1, cpack, crecv, cpack1, crecv1, epack, erecv, erecv_far, xpack1, xrecv1,
     yline, yline1, sline, frame, pore, sxpack, sxrecv, sypack, syrecv, screcv, fpack, epack_far, cend, near, wrapped,
     sent_v, all_v, terms_ref, count_ref, load_sem, send_sem, recv_sem) = refs
    D, H, W = solid.shape
    T = D + 2
    ncy, ncx = conc.shape[2:]
    f32 = jnp.float32
    gz, gy, gx = lax.axis_index("gz"), lax.axis_index("gy"), lax.axis_index("gx")
    is_first, is_last = gz == 0, gz == nz - 1
    has_up, has_down = gz < nz - 1, gz > 0
    early = jnp.where(gz == 0, gx, 1) == 0
    late = jnp.where(gz == 0, gx, 1) > 0
    bound_at = len(FLAT) * T
    port_at = bound_at + 5
    solid_at = port_at + 2 + (port_at % 2)
    bound_at1 = len(FLAT) * D

    spans = [(0, 2), (D - 2, 2), (2, D - 4)]
    planes_in = [
        pltpu.make_async_copy(pop_hbm.at[:, pl.ds(a, n)], pops.at[:, pl.ds(a, n)], load_sem.at[i])
        for i, (a, n) in enumerate(spans)
    ]
    small = [
        pltpu.make_async_copy(a, b, load_sem.at[3 + i])
        for i, (a, b) in enumerate(
            ((solid_hbm, solid), (ports_hbm, ports), (conc_hbm, conc), (load_hbm, load)))
    ]
    def at(offset):
        dz, dy, dx = offset
        return {"gz": gz + dz, "gy": lax.rem(gy + dy + ny, ny), "gx": lax.rem(gx + dx + nx, nx)}

    flat = [(0, dy, dx) for dx in list(range(1, nx)) + [0] for dy in range(ny) if dy or dx]
    told = {(0, dy % ny, nx - 1) for dy in (0, 1, -1)} if nx > 2 else set()
    targets = sorted({(dy % ny, dx) for dy in (0, 1, -1) for dx in (0, 1)})
    barrier = pltpu.get_barrier_semaphore()

    def greet(offsets):
        for offset in offsets:
            pl.semaphore_signal(barrier, inc=1, device_id=at(offset), device_id_type=MESH)

    @pl.when(has_down)
    def _():
        greet([(-1, -dy, -dx) for dy, dx in targets])

    @pl.when(has_up)
    def _():
        greet([(1, -dy, -dx) for dy, dx in targets])

    greet([(0, -dy, -dx) for _, dy, dx in flat if (0, dy, dx) not in told])

    small[0].start()
    planes_in[0].start()
    small[1].start()
    small[2].start()
    small[3].start()
    planes_in[1].start()
    planes_in[2].start()

    lane = lax.broadcasted_iota(jnp.int32, (H, W), 1)
    row = lax.broadcasted_iota(jnp.int32, (H, W), 0)
    pair = lax.div(lane, 2)
    first_mask = jnp.full((H, W), gz, jnp.int32) == 0
    last_mask = jnp.full((H, W), gz, jnp.int32) == nz - 1
    zero = jnp.zeros((H, W), f32)

    def rolled(x, step, axis):
        step = step % x.shape[axis]
        return pltpu.roll(x, step, axis) if step else x

    def put(acc, value, spot, shift):
        return jnp.where(lane == spot, rolled(value, shift, 1), acc)

    def put_pair(acc, value, half, shift):
        return jnp.where(pair == half, rolled(value, shift, 1), acc)

    def edge_row(value, s):
        return value[H - 1 :, :] if s == 0 else value[:1, :]

    FLAGS, Y, X, BELOW, ABOVE, BACK, VEL, ENDS = range(8)
    SLAB, UP, DOWN, VEL_OUT = range(4)
    side_sets = [(pl.ds(0, 2), 1)] if ny == 2 else [(pl.ds(0, 1), 1), (pl.ds(1, 1), -1)]

    def remote(src, dst, offset, group):
        sent = {0: SLAB, 1: UP, -1: DOWN}[offset[0]]
        return pltpu.make_async_remote_copy(
            src_ref=src, dst_ref=dst, send_sem=send_sem.at[sent], recv_sem=recv_sem.at[group],
            device_id=at(offset), device_id_type=MESH)

    def arrived(sem, tiles):
        whole = count_ref.at[pl.ds(0, tiles)]
        pltpu.make_async_copy(whole, whole, sem).wait()

    def start(copies):
        for copy in copies:
            copy.start()

    along_z, ends = {}, {}
    for dz, zs, group in ((1, 0, BELOW), (-1, 1, ABOVE)):
        ends[dz] = [remote(cend, near.at[zs], (dz, 0, 0), ENDS + zs)]
        along_z[dz] = [
            remote(zpack.at[zs], zrecv.at[zs], (dz, 0, 0), group),
            remote(fpack.at[zs], xside.at[zs], (dz, 0, 1), group),
        ]
        for i, (where, dy) in enumerate(side_sets):
            along_z[dz].append(remote(epack_far.at[zs], erecv_far.at[zs, i], (dz, dy, 1), group))
            along_z[dz].append(remote(epack.at[zs, where], erecv.at[zs, where], (dz, dy, 0), group))
    end_tiles = cend.shape[0] // H
    z_tiles = zpack.shape[1] + 1 + len(side_sets) + 2
    flags = [remote(sxpack, sxrecv, (0, 0, 1), FLAGS)]
    for where, dy in side_sets:
        flags.append(remote(sypack.at[where], screcv.at[where], (0, dy, 1), FLAGS))
        flags.append(remote(sypack.at[where], syrecv.at[where], (0, dy, 0), FLAGS))
    slab = [remote(xpack, xrecv, (0, 0, 1), X)]
    back_c = []
    back = [remote(xpack1, xrecv1, (0, 0, -1), BACK)]
    for where, dy in side_sets:
        slab.append(remote(cpack.at[where], crecv.at[where], (0, dy, 1), Y))
        slab.append(remote(ypack.at[where], yrecv.at[where], (0, dy, 0), Y))
        back.append(remote(ypack1.at[where], yrecv1.at[where], (0, dy, 0), BACK))
        back_c.append(remote(cpack1.at[where], crecv1.at[where], (0, dy, -1), BACK))
    slab_tiles = 5 + 2 + 12 + 14

    edge_table = [
        [edge_rows((zs, s), ((D - 2, D - 1), (1, 0))[zs]) for s in range(2)] for zs in range(2)]

    for copy in small:
        copy.wait()
    cend[...] = jnp.zeros(cend.shape, f32)
    for s in range(2):
        cend[s * ncy : (s + 1) * ncy, 0:ncx] = conc[s, 0]
    zpack[0, 13] = solid[D - 1].astype(f32)
    zpack[1, 13] = solid[0].astype(f32)
    walls_out = zero
    for z in range(D):
        wall = solid[z].astype(f32)
        walls_out = put_pair(walls_out, wall, z, 2 * z + 2)
        for s in range(2):
            sypack[s, z : z + 1, :] = edge_row(wall, s)
    sxpack[...] = walls_out

    def shifted(value, lanes, fill=0.0):
        return jnp.where(lane < lanes, fill, rolled(value, lanes, 1)) if lanes else value

    def first_plane(z, packs):
        f = [pops[m, z] for m in range(19)]
        flag = solid[z]
        post, velocity = collide(f, flag == 1)
        for m in range(19):
            post0[z, m] = post[m]
        for zs, ends_at in ((0, (D - 1, D - 2)), (1, (0, 1))):
            if z in ends_at:
                base = 5 * ends_at.index(z)
                for j, m in enumerate(GROUPS[0][zs]):
                    zpack[zs, base + j] = post[m]
            if z == ends_at[0]:
                sums = level_sums(lambda m: shifted(post[m], 1 + lattice[m][2]), lambda m: None,
                                  row, H - 1, rolled)
                for d in range(3):
                    zpack[zs, 10 + d] = sums[d]
        for s in range(2):
            for i, m in enumerate(GROUPS[1][s]):
                ypack[s, i, z : z + 1, :] = edge_row(post[m], s)
        for zs in range(2):
            for s in range(2):
                for r, (m, source, _) in enumerate(edge_table[zs][s]):
                    if source == z:
                        epack[zs, s, r : r + 1, :] = edge_row(post[m], s)
        if z == 0:
            inflow = equilibrium_at_inlet()
            for j, m in enumerate(GROUPS[0][0]):
                bound[0, j] = jnp.where(ports[0] == 1, inflow[m], post[opposite[m]])
        if z == D - 1:
            outflow = balance(base_density, velocity, GROUPS[0][1])
            for j, m in enumerate(GROUPS[0][1]):
                leaving = jnp.where(ports[1] == 1, outflow[m], post[opposite[m]])
                bound[0, j] = jnp.where(last_mask, leaving, bound[0, j])
        twos, ones = packs
        for i, m in enumerate(GROUPS[2][0]):
            q = i * T + z + lattice[m][0] + 1
            twos = put_pair(twos, post[m], q, 2 * q + 2)
        for i, m in enumerate(FLAT):
            q = i * T + z + lattice[m][0] + 1
            ones = put(ones, post[m], q, q + 1)
        if z in (0, D - 1):
            q = solid_at // 2 + (0 if z == 0 else 1)
            ones = put_pair(ones, flag.astype(f32), q, 2 * q + 2)
        return twos, ones

    def enter():
        count = lambda flag: jnp.where(flag, len(targets), 0)
        pl.semaphore_wait(barrier, len(flat) - len(told) + count(has_up) + count(has_down))

    def send(copies_of):
        for dz, there in ((-1, has_down), (1, has_up)):
            if dz in copies_of:
                @pl.when(there)
                def _():
                    start(copies_of[dz])

    def pack_z(zs, packs):
        twos, ones = packs
        base = 0 if zs == 1 else D
        mine = lane < 0
        for i in range(5):
            mine = mine | ((pair >= i * T + base) & (pair < i * T + base + 2))
        fpack[zs] = jnp.where(mine, twos, rolled(ones, 4, 1))
        epack_far[zs] = jnp.where(lane >= W - 2, epack[zs, 0], rolled(epack[zs, 1], 2, 1))

    packs = (zero, zero)
    planes_in[0].wait()
    for z in (0, 1):
        packs = first_plane(z, packs)
    pack_z(1, packs)
    planes_in[1].wait()
    for z in (D - 1, D - 2):
        packs = first_plane(z, packs)
    pack_z(0, packs)

    @pl.when(late)
    def _():
        enter()
        start(flags)
        send({-1: along_z[-1][:1] + along_z[-1][3::2] + along_z[-1][1:2] + along_z[-1][2::2]})
        send({1: along_z[1][:1] + along_z[1][3::2] + along_z[1][1:2] + along_z[1][2::2]})

    planes_in[2].wait()
    for z in range(2, D - 2):
        packs = first_plane(z, packs)
    twos, ones = packs
    for j in range(5):
        ones = put(ones, bound[0, j], bound_at + j, bound_at + j + 1)
    for j in range(2):
        ones = put(ones, ports[j].astype(f32), port_at + j, port_at + j + 1)
    xpack[0], xpack[1] = twos, ones
    for s in range(2):
        acc = zero
        for i in range(5):
            acc = put_pair(acc, ypack[s, i], i, 2 * i + 2)
        cpack[s] = acc

    @pl.when(early)
    def _():
        enter()
        start(flags)
        send({1: along_z[1]})

    start(slab)
    send(ends)

    x_low, x_high = [], []
    for members, spot in ((GROUPS[2][0], pair), (FLAT, lane)):
        low, high = lane < 0, lane < 0
        for i, m in enumerate(members):
            cz = lattice[m][0]
            if cz >= 0:
                low = low | ((spot >= i * T) & (spot < i * T + 1 + cz))
            if cz <= 0:
                high = high | ((spot >= i * T + D + 1 + cz) & (spot < i * T + T))
        x_low.append(low)
        x_high.append(high)

    diffs = []
    wide = sent_v.shape[-1]
    parts = []
    for c in (1, 0, -1):
        voxel = lax.broadcasted_iota(jnp.int32, (W, wide), 0) + gx * W - 1 + c
        voxel = jnp.where(voxel < 0, voxel + nx * W, voxel)
        cell = lax.broadcasted_iota(jnp.int32, (W, wide), 1) * CELL
        parts.append(((voxel >= cell) & (voxel < cell + CELL)).astype(f32))
    pick = jnp.concatenate(parts, axis=0).astype(jnp.bfloat16)

    arrived(recv_sem.at[FLAGS], 5)
    for s in range(2):
        for n in range(3):
            tile, far = syrecv[s], screcv[s]
            sline[s, n] = shifted(tile, n, rolled(far, n, 1)) if n else tile
    for n in range(9):
        pore[0, n] = zero
        pore[D + 1, n] = zero
    for k in range(1, D + 1):
        walls = solid[k - 1].astype(f32)
        columns = sxrecv[...]
        one = shifted(walls, 1, rolled(columns, 1 - 2 * k, 1))
        two = shifted(walls, 2, rolled(columns, 2 - 2 * k, 1))
        frame[k] = one
        for n, view in enumerate((walls, one, two)):
            cx = 1 - n
            pore[k, TYPES.index((0, cx))] = 1.0 - view
            for cy in (1, -1):
                s = 1 if cy == 1 else 0
                line = sline[s, n, k - 1 : k, :]
                moved = jnp.where(row == (H - 1 if cy == 1 else 0),
                                  jnp.broadcast_to(line, (H, W)), rolled(view, -cy, 0))
                pore[k, TYPES.index((cy, cx))] = 1.0 - moved

    arrived(recv_sem.at[Y], 12)

    def filled(tile, columns, lanes, spot):
        return shifted(tile, lanes, rolled(columns, -(spot + 2 - lanes), 1)) if lanes else tile

    for s in range(2):
        corner = crecv[s]
        for i, m in enumerate(GROUPS[1][s]):
            cz, _, cx = lattice[m]
            yline[s, i, 1 + cz : 1 + cz + D, :] = filled(yrecv[s, i], corner, 1 + cx, 2 * i)

    def column_of(m, k):
        if lattice[m][2] == 1:
            return rolled(xline[0], -2 * (GROUPS[2][0].index(m) * T + k), 1)
        return rolled(xline[1], -(FLAT.index(m) * T + k), 1)

    def line_of(m, k):
        s = 0 if lattice[m][1] == 1 else 1
        return yline[s, GROUPS[1][s].index(m), k : k + 1, :]

    def stream(k, members):
        f = {}
        for m in members:
            cz, cy, cx = lattice[m]
            z = k - 1 - cz
            if 0 <= z < D:
                v = post0[z, m]
            else:
                zs = 0 if cz == 1 else 1
                v = zrecv[zs, GROUPS[0][zs].index(m) + (5 if z in (-2, D + 1) else 0)]
            if cx >= 0:
                v = shifted(v, 1 + cx, column_of(m, k))
            if cy:
                v = jnp.where(row == (0 if cy == 1 else H - 1),
                              jnp.broadcast_to(line_of(m, k), (H, W)), rolled(v, cy, 0))
            f[m] = v
        return f

    def port_view(j):
        return shifted(ports[j].astype(f32), 1, rolled(xline[1], -(port_at + j), 1)) > 0.5

    def bound_view(j):
        return shifted(bound[0, j], 1, rolled(xline[1], -(bound_at + j), 1))

    names = [("n", cy, cx) for cy, cx in TYPES if cy or cx]
    names += [("z", cy, cx) for cy, cx in TYPES if not (cy and cx)]

    def keep(k, post, carry):
        twos, ones, sums = carry
        for m, value in post.items():
            cz, cy, cx = lattice[m]
            post1[k, m] = value
            t = k - 1 + cz
            if not 0 <= t < D:
                continue
            if cy:
                s = 0 if cy == 1 else 1
                ypack1[s, GROUPS[1][s].index(m), t : t + 1, :] = edge_row(value, s)
            if cx == -1:
                q = GROUPS[2][1].index(m) * D + t
                twos = put_pair(twos, value, q, 2 * q)
            elif cx == 0:
                q = FLAT.index(m) * D + t
                ones = put(ones, value, q, q)
            if m:
                part = value * pore[k + cz, TYPES.index((cy, cx))]
                if cy or cx:
                    sums["n", cy, cx] = sums["n", cy, cx] + part
                if cz == 1:
                    sums["z", cy, cx] = sums["z", cy, cx] + part
                if cz == -1:
                    sums["z", cy, cx] = sums["z", cy, cx] - part
        return twos, ones, sums

    def inner_plane(k, carry):
        f = stream(k, range(19))
        if k == 1:
            for j, m in enumerate(GROUPS[0][0]):
                f[m] = jnp.where(first_mask, bound_view(j), f[m])
        if k == D:
            for j, m in enumerate(GROUPS[0][1]):
                f[m] = jnp.where(last_mask, bound_view(j), f[m])
        post, velocity = collide([f[m] for m in range(19)], frame[k] > 0.5)
        carry = keep(k, dict(enumerate(post)), carry)
        if k in (1, D):
            if k == 1:
                members, opened, mask = GROUPS[0][0], port_view(0), first_mask
                values = equilibrium_at_inlet()
            else:
                members, opened, mask = GROUPS[0][1], port_view(1), last_mask
                values = balance(base_density, velocity, members)
            extra = [zero, zero, zero]
            for j, m in enumerate(members):
                value = jnp.where(opened, values[m], post[opposite[m]])
                bound[1, j] = value if k == 1 else jnp.where(last_mask, value, bound[1, j])
                for d in range(3):
                    if lattice[m][d]:
                        extra[d] = extra[d] + value if lattice[m][d] == 1 else extra[d] - value
            for d in range(3):
                add = jnp.where(mask, extra[d] * pore[k, TYPES.index((0, 0))], 0.0)
                speed[d] = add if k == 1 else speed[d] + add
        return carry

    def outer_plane(k, carry):
        zs, mask = (0, first_mask) if k == 0 else (1, last_mask)
        members = GROUPS[0][zs]
        f = stream(k, GROUPS[0][0] + GROUPS[0][1])
        sums = level_sums(
            lambda m: jnp.where(lane < 1 + lattice[m][2], column_of(m, k), 0.0) if lattice[m][2] >= 0 else None,
            lambda m: line_of(m, k), row, H - 1, rolled)
        density, flow_y, flow_x = [zrecv[zs, 10 + d] + sums[d] for d in range(3)]
        flows = [None, flow_y, flow_x]
        for m, value in f.items():
            density = density + value
            for d in range(3):
                if lattice[m][d]:
                    signed = value if lattice[m][d] == 1 else -value
                    flows[d] = signed if flows[d] is None else flows[d] + signed
        inverse = 1.0 / density
        feq = balance(relax_rate * density, [flow * inverse for flow in flows], members)
        wall = frame[k] > 0.5
        post = {}
        for m in members:
            made = jnp.where(wall, f[opposite[m]], (1.0 - relax_rate) * f[m] + feq[m])
            post[m] = jnp.where(mask, 0.0, made)
        return keep(k, post, carry)

    arrived(recv_sem.at[X], 2)
    xline[0], xline[1] = xrecv[0], xrecv[1]
    carry = (zero, zero, {name: zero for name in names})
    for k in range(2, D):
        carry = inner_plane(k, carry)

    for zs, there, group in ((0, has_down, BELOW), (1, has_up, ABOVE)):
        @pl.when(there)
        def _():
            arrived(recv_sem.at[group], z_tiles)

        beside = xside[zs]
        move = -D if zs == 0 else D
        masks = x_low if zs == 0 else x_high
        xline[0] = jnp.where(masks[0], rolled(beside, 2 * move, 1), xline[0])
        xline[1] = jnp.where(masks[1], rolled(beside, move - 4, 1), xline[1])
        for s in range(2):
            tile = erecv[zs, s]
            far = erecv_far[zs, 0 if ny == 2 else s]
            if s == 1:
                far = rolled(far, -2, 1)
            views = [tile] + [shifted(tile, n, rolled(far, n, 1)) for n in (1, 2)]
            for r, (m, _, target) in enumerate(edge_table[zs][s]):
                k = target if zs == 0 else D + 1 - target
                yline[s, GROUPS[1][s].index(m), k : k + 1, :] = views[1 + lattice[m][2]][r : r + 1, :]
        k = 0 if zs == 0 else D + 1
        spot = solid_at + 4 + (3 if zs == 0 else 1)
        frame[k] = shifted(zrecv[zs, 13], 1, rolled(beside, -spot, 1))
        carry = inner_plane(1 if zs == 0 else D, carry)
        carry = outer_plane(k, carry)

    twos, ones, sums = carry
    for j in range(5):
        ones = put(ones, bound[1, j], bound_at1 + j, bound_at1 + j)
    xpack1[0], xpack1[1] = twos, ones
    top, bottom = row == H - 1, row == 0
    blocks = []
    for cx in (1, 0, -1):
        own = [zero, zero, zero]
        up, down = [zero] * 3, [zero] * 3
        if ("n", 0, cx) in sums and cx:
            own[2] = sums["n", 0, cx] if cx == 1 else -sums["n", 0, cx]
        own[0] = sums["z", 0, cx]
        for cy, beyond, edge in ((1, up, top), (-1, down, bottom)):
            n = sums["n", cy, cx]
            values = [sums.get(("z", cy, cx)), n if cy == 1 else -n, {1: n, 0: None, -1: -n}[cx]]
            for d in range(3):
                if values[d] is not None:
                    own[d] = own[d] + jnp.where(edge, 0.0, values[d])
                    beyond[d] = values[d]
        if cx == 0:
            own = [own[d] + speed[d] for d in range(3)]
        totals = [jnp.sum(v, axis=0, keepdims=True) for v in own]
        ups = [v[H - 1 :, :] for v in up]
        downs = [v[:1, :] for v in down]
        rows_of = [(0, totals)]
        if ny == 2:
            rows_of.append((1, [a + b for a, b in zip(ups, downs)]))
        else:
            rows_of += [(1, ups), (-1, downs)]
        blocks.append(rows_of)
    tiles = []
    for base in range(0, sent_v.shape[0], H):
        here = []
        for rows_of in blocks:
            tile = zero
            for dy, lines in rows_of:
                spot = lax.rem(gy + dy + ny, ny) - base
                for d in range(3):
                    tile = jnp.where(row == spot + d * ny, jnp.broadcast_to(lines[d], (H, W)), tile)
            here.append(tile)
        tiles.append(jnp.concatenate(here, axis=1))

    def exact_pick(x):
        high = x.astype(jnp.bfloat16).astype(f32)
        mid = (x - high).astype(jnp.bfloat16).astype(f32)
        low = x - high - mid
        stacked = jnp.concatenate([high, mid, low], axis=0).astype(jnp.bfloat16)
        made = jnp.dot(stacked, pick, preferred_element_type=f32)
        return made[:H] + made[H : 2 * H] + made[2 * H :]

    for i, tile in enumerate(tiles):
        sent_v[i * H : (i + 1) * H, :] = exact_pick(tile) * (1.0 / (CELL * CELL * CELL * base_density))
    tell = [
        pltpu.make_async_remote_copy(
            src_ref=sent_v, dst_ref=all_v.at[gy, gx], send_sem=send_sem.at[VEL_OUT],
            recv_sem=recv_sem.at[VEL], device_id=at(offset), device_id_type=MESH)
        for offset in flat
    ]
    start(tell)
    start(back)
    all_v[gy, gx] = sent_v[...]
    for s in range(2):
        acc = zero
        for i, m in enumerate(GROUPS[1][s]):
            if lattice[m][2] <= 0:
                acc = put_pair(acc, ypack1[s, i], i, 2 * i)
        cpack1[s] = acc
    start(back_c)

    for zs, there in ((0, has_down), (1, has_up)):
        @pl.when(there)
        def _():
            arrived(recv_sem.at[ENDS + zs], end_tiles)

    @pl.when(is_first)
    def _():
        for s in range(2):
            near[0, s * ncy : (s + 1) * ncy, :] = jnp.full((ncy, wide), feed_level[s], f32)

    @pl.when(is_last)
    def _():
        near[1] = cend[...]

    source = lax.broadcasted_iota(jnp.int32, (ncx, ncx), 0)
    target = lax.broadcasted_iota(jnp.int32, (ncx, ncx), 1)
    ahead = jnp.where(target == ncx - 1, 0, target + 1)
    behind = jnp.where(target == 0, ncx - 1, target - 1)
    take_after = (source == ahead).astype(f32)
    take_before = (source == behind).astype(f32)

    def exact_dot(a, b):
        return jnp.dot(a, b, precision=lax.Precision.HIGHEST, preferred_element_type=f32)

    terms_ref[...] = jnp.zeros(terms_ref.shape, f32)
    for s in range(2):
        c = conc[s, 0]
        wrapped[s, 1 : ncy + 1, :] = c
        wrapped[s, 0:1, :] = conc[s, 0, ncy - 1 : ncy, :]
        wrapped[s, ncy + 1 : ncy + 2, :] = conc[s, 0, 0:1, :]
        pairs = [
            tuple(near[e, s * ncy : (s + 1) * ncy, 0:ncx] for e in range(2)),
            (wrapped[s, 0:ncy, :], wrapped[s, 2 : ncy + 2, :]),
            (exact_dot(c, take_before), exact_dot(c, take_after)),
        ]
        curvature = sum(b + a - 2.0 * c for b, a in pairs)
        rate = uptake_rate[s] * (affinity[s] * c - load[s, 0])
        new_load[s, 0] = load[s, 0] + rate
        diffs.append(c - phase_ratio * rate + spread_base[s] * curvature)
        for d, (before, after) in enumerate(pairs):
            for n, value in enumerate((c - before, after - c, curvature)):
                terms_ref[s, n, d * ncy : (d + 1) * ncy, 0:ncx] = value

    arrived(recv_sem.at[BACK], 14)

    def emptied(tile, lanes, columns):
        return jnp.where(lane >= W - lanes, columns, rolled(tile, -lanes, 1)) if lanes else tile

    for s in range(2):
        corner = crecv1[s]
        for i, m in enumerate(GROUPS[1][s]):
            lanes = 1 - lattice[m][2]
            yline1[s, i] = emptied(yrecv1[s, i], lanes, rolled(corner, -lanes - 2 * i, 1))

    for t in range(D):
        for m in range(19):
            cz, cy, cx = lattice[m]
            v = post1[t + 1 - cz, m]
            if cx == -1:
                spot = 2 * (GROUPS[2][1].index(m) * D + t)
                v = emptied(v, 2, rolled(xrecv1[0], -2 - spot, 1))
            elif cx == 0:
                v = emptied(v, 1, rolled(xrecv1[1], -1 - (FLAT.index(m) * D + t), 1))
            if cy:
                s = 0 if cy == 1 else 1
                line = yline1[s, GROUPS[1][s].index(m), t : t + 1, :]
                v = jnp.where(row == (0 if s == 0 else H - 1),
                              jnp.broadcast_to(line, (H, W)), rolled(v, cy, 0))
            if (t == 0 and cz == 1) or (t == D - 1 and cz == -1):
                j = GROUPS[0][0 if cz == 1 else 1].index(m)
                kept = emptied(bound[1, j], 1, rolled(xrecv1[1], -1 - (bound_at1 + j), 1))
                v = jnp.where(first_mask if cz == 1 else last_mask, kept, v)
            out[m, t] = v

    arrived(send_sem.at[SLAB], slab_tiles)
    for sem, there in ((UP, has_up), (DOWN, has_down)):
        @pl.when(there)
        def _():
            arrived(send_sem.at[sem], z_tiles + end_tiles)
    vel_tiles = len(flat) * (sent_v.shape[0] // H)
    arrived(recv_sem.at[VEL], vel_tiles)
    parts = [all_v[y, x] for y in range(ny) for x in range(nx)]
    while len(parts) > 1:
        parts = [sum(parts[i : i + 2][1:], parts[i]) for i in range(0, len(parts), 2)]
    courant = CELL * parts[0]
    forward, backward, reach = jnp.maximum(courant, 0.0), jnp.minimum(courant, 0.0), jnp.abs(courant)
    for s in range(2):
        terms = spread_length * reach * terms_ref[s, 2] - forward * terms_ref[s, 0] - backward * terms_ref[s, 1]
        moved = terms[0:ncy] + terms[ncy : 2 * ncy] + terms[2 * ncy : 3 * ncy]
        new_conc[s, 0] = diffs[s] + moved[:, 0:ncx]
    arrived(send_sem.at[VEL_OUT], vel_tiles)


def hand_out(*refs):
    copies = [pltpu.make_async_copy(refs[i], refs[3 + i], refs[6].at[i]) for i in range(3)]
    for copy in copies:
        copy.start()
    for copy in copies:
        copy.wait()


def equilibrium_at_inlet():
    result = {}
    for m in GROUPS[0][0]:
        along = inlet_speed
        result[m] = weights[m] * base_density * (
            1.0 + 3.0 * along + 4.5 * along * along - 1.5 * inlet_speed * inlet_speed)
    return result


def solution(mesh):
    sizes = tuple(mesh.shape[a] for a in ("gz", "gy", "gx"))
    nz, ny, nx = sizes

    def body(populations, solid, ports, concentration, loaded):
        D, H, W = solid.shape
        ncy, ncx = concentration.shape[2:]
        assert D == CELL and H == CELL and W % 128 == 0 and 12 * (D + 2) <= W
        wide = -(-ncx // 128) * 128
        assert nz > 1 and ny > 1 and nx > 1 and W == wide
        f32 = jnp.float32
        tile = (H, W)
        rows = -(-3 * ny // H) * H
        assert ncy == ny
        ends = -(-2 * ncy // H) * H
        anywhere = pl.BlockSpec(memory_space=pl.ANY)
        inside = pl.BlockSpec(memory_space=pltpu.VMEM)
        results = (populations, concentration, loaded)
        made = pl.pallas_call(
            functools.partial(kernel, sizes),
            out_shape=tuple(pltpu.VMEM(a.shape, f32) for a in results),
            in_specs=[anywhere] * 5,
            out_specs=(inside,) * 3,
            scratch_shapes=[
                pltpu.VMEM(populations.shape, f32),
                pltpu.VMEM(solid.shape, jnp.int32),
                pltpu.VMEM(ports.shape, jnp.int32),
                pltpu.VMEM(concentration.shape, f32),
                pltpu.VMEM(loaded.shape, f32),
                pltpu.VMEM((D, 19) + tile, f32),
                pltpu.VMEM((D + 2, 19) + tile, f32),
                pltpu.VMEM((2, 5) + tile, f32),
                pltpu.VMEM((3,) + tile, f32),
                pltpu.VMEM((2, 14) + tile, f32),
                pltpu.VMEM((2, 14) + tile, f32),
                pltpu.VMEM((2,) + tile, f32),
                pltpu.VMEM((2,) + tile, f32),
                pltpu.VMEM((2,) + tile, f32),
                pltpu.VMEM((2,) + tile, f32),
                pltpu.VMEM((2, 5, D, W), f32),
                pltpu.VMEM((2, 5, D, W), f32),
                pltpu.VMEM((2, 5, D, W), f32),
                pltpu.VMEM((2, 5, D, W), f32),
                pltpu.VMEM((2, D, W), f32),
                pltpu.VMEM((2, D, W), f32),
                pltpu.VMEM((2, D, W), f32),
                pltpu.VMEM((2, D, W), f32),
                pltpu.VMEM((2, 2) + tile, f32),
                pltpu.VMEM((2, 2) + tile, f32),
                pltpu.VMEM((2, 2) + tile, f32),
                pltpu.VMEM((2,) + tile, f32),
                pltpu.VMEM((2,) + tile, f32),
                pltpu.VMEM((2, 5, 2 * H, W), f32),
                pltpu.VMEM((2, 5, D, W), f32),
                pltpu.VMEM((2, 3, D, W), f32),
                pltpu.VMEM((D + 2,) + tile, f32),
                pltpu.VMEM((D + 2, 9) + tile, f32),
                pltpu.VMEM(tile, f32),
                pltpu.VMEM(tile, f32),
                pltpu.VMEM((2, D, W), f32),
                pltpu.VMEM((2, D, W), f32),
                pltpu.VMEM((2, D, W), f32),
                pltpu.VMEM((2,) + tile, f32),
                pltpu.VMEM((2,) + tile, f32),
                pltpu.VMEM((ends, wide), f32),
                pltpu.VMEM((2, ends, wide), f32),
                pltpu.VMEM((2, ncy + 2, ncx), f32),
                pltpu.VMEM((rows, wide), f32),
                pltpu.VMEM((ny, nx, rows, wide), f32),
                pltpu.VMEM((2, 3, rows, wide), f32),
                pltpu.VMEM((max(40, ny * nx * (rows // H)),) + tile, f32),
                pltpu.SemaphoreType.DMA((7,)),
                pltpu.SemaphoreType.DMA((4,)),
                pltpu.SemaphoreType.DMA((9,)),
            ],
            compiler_params=pltpu.CompilerParams(collective_id=0, has_side_effects=True),
        )(populations, solid, ports, concentration, loaded)
        return pl.pallas_call(
            hand_out,
            out_shape=tuple(jax.ShapeDtypeStruct(a.shape, f32) for a in results),
            in_specs=[inside] * 3,
            out_specs=(anywhere,) * 3,
            scratch_shapes=[pltpu.SemaphoreType.DMA((3,))],
        )(*[pltpu.with_memory_space_constraint(a, pltpu.VMEM) for a in made])

    placed = (
        P(None, "gz", "gy", "gx"),
        P("gz", "gy", "gx"),
        P(None, "gy", "gx"),
        P(None, "gz", None, None),
        P(None, "gz", None, None),
    )
    return jax.shard_map(
        body,
        mesh=mesh,
        in_specs=placed,
        out_specs=(P(None, "gz", "gy", "gx"), P(None, "gz", None, None), P(None, "gz", None, None)),
        check_vma=False,
    )
```
